256 devices in a mesh: row: 8 (over y, z_lo), col: 32 (over x, z_hi, core).
Axes of the slice: x: 4, y: 4, z: 8 (z_hi: 4, z_lo: 2; z = z_hi * 2 + z_lo), core: 2. Of those that a mesh axis runs over, the one named last changes fastest.
Arguments:
- image_student: bfloat16 [16384, 1024], P(('row', 'col')), may hold values from -2.5 to 2.5
- text_student: bfloat16 [16384, 1024], P(('col', 'row')), may hold values from -2.5 to 2.5
- image_teacher: bfloat16 [16384, 1024], P(('row', 'col')), may hold values from -2.5 to 2.5
- text_teacher: bfloat16 [16384, 1024], P(('col', 'row')), may hold values from -2.5 to 2.5
Outputs:
- loss: float32 [], replicated
- image_grad: float32 [16384, 1024], P(('row', 'col'))
- text_grad: float32 [16384, 1024], P(('col', 'row'))
The draws below stay inside these ranges and needn't reach their ends.
All inputs are finite; a program needn't handle non-finite values.
Results may differ from the reference program's by a relative error of at most 0.002.
Values may be sent and summed in bfloat16 or wider, within the bound.
No kernel may reach another device: no remote copies, remote signals or barrier semaphores. Data moves between devices by JAX's collectives and lax.ppermute only.
A program may use at most 128 MiB of HBM per device.

```python
import math
import jax
import jax.numpy as jnp
from jax import lax

D = 1024
B = 16384


def embedding(key, which):
    base = jnp.clip(jax.random.normal(jax.random.fold_in(key, which), (B, D), jnp.float32), -5.0, 5.0) / math.sqrt(D)
    return base


def draw_image_student(key, part):
    return embedding(key, 11).astype(jnp.bfloat16)


def draw_text_student(key, part):
    return embedding(key, 12).astype(jnp.bfloat16)


def draw_image_teacher(key, part):
    return embedding(key, 13).astype(jnp.bfloat16)


def draw_text_teacher(key, part):
    return embedding(key, 14).astype(jnp.bfloat16)


def setup_inputs(seed: int = 0) -> dict:
    key_of = jax.random.split(jax.random.key(seed), 5)
    image_student = draw_image_student(jax.random.fold_in(key_of[4], 71), 0)
    text_student = draw_text_student(jax.random.fold_in(key_of[4], 71), 0)
    image_teacher = draw_image_teacher(jax.random.fold_in(key_of[4], 71), 0)
    text_teacher = draw_text_teacher(jax.random.fold_in(key_of[4], 71), 0)
    return dict(image_student=image_student, text_student=text_student, image_teacher=image_teacher, text_teacher=text_teacher)


logit_scale = 100.0

def tile_logits(left, right):
    return logit_scale * lax.dot_general(left.astype(jnp.float32), right.astype(jnp.float32), (((1,), (1,)), ((), ())), preferred_element_type=jnp.float32)

def partial_stats(student, teacher, along):
    student_high = jnp.max(student, along, keepdims=True)
    student_total = jnp.sum(jnp.exp(student - student_high), along)
    teacher_high = jnp.max(teacher, along, keepdims=True)
    weights = jnp.exp(teacher - teacher_high)
    teacher_total = jnp.sum(weights, along)
    divergence = jnp.sum(weights * (teacher - student), along)
    return (jnp.squeeze(student_high, along), student_total, jnp.squeeze(teacher_high, along), teacher_total, divergence)

def merge_stats(first, second):
    student_high = jnp.maximum(first[0], second[0])
    teacher_high = jnp.maximum(first[2], second[2])
    early = jnp.exp(first[2] - teacher_high)
    later = jnp.exp(second[2] - teacher_high)
    student_total = first[1] * jnp.exp(first[0] - student_high) + second[1] * jnp.exp(second[0] - student_high)
    return (student_high, student_total, teacher_high, first[3] * early + second[3] * later, first[4] * early + second[4] * later)

def finish(stats):
    student_lse = stats[0] + jnp.log(stats[1])
    teacher_lse = stats[2] + jnp.log(stats[3])
    divergence = stats[4] / stats[3] - teacher_lse + student_lse
    return (student_lse, teacher_lse, 0.5 * (student_lse + divergence))

def reference(image_student, text_student, image_teacher, text_teacher):
    total = image_student.shape[0]
    width = image_student.shape[1]
    block = math.gcd(total, 512)
    count = total // block
    columns = jnp.arange(total, dtype=jnp.int32)
    starts = jnp.arange(count, dtype=jnp.int32) * block
    image_blocks = image_student.reshape(count, block, width)
    frozen_blocks = image_teacher.reshape(count, block, width)

    def first_pass(carry, inputs):
        image_rows, frozen_rows, start = inputs
        student = tile_logits(image_rows, text_student)
        teacher = tile_logits(frozen_rows, text_teacher)
        row_part = partial_stats(student, teacher, 1)
        merged = merge_stats(carry, partial_stats(student, teacher, 0))
        row_index = start + jnp.arange(block, dtype=jnp.int32)
        identity = (row_index[:, None] == columns[None, :]).astype(jnp.float32)
        return (merged, (row_part, jnp.sum(student * identity)))
    lowest = jnp.full((total,), -1e+30, jnp.float32)
    nothing = jnp.zeros((total,), jnp.float32)
    column_stats, (row_blocks, diagonals) = lax.scan(first_pass, (lowest, nothing, lowest, nothing, nothing), (image_blocks, frozen_blocks, starts))
    row_stats = tuple((member.reshape(total) for member in row_blocks))
    student_rows, teacher_rows, row_terms = finish(row_stats)
    student_columns, teacher_columns, column_terms = finish(column_stats)
    loss = (jnp.sum(row_terms) + jnp.sum(column_terms) - jnp.sum(diagonals)) / total

    def second_pass(text_grad, inputs):
        image_rows, frozen_rows, start, student_lse, teacher_lse = inputs
        student = tile_logits(image_rows, text_student)
        teacher = tile_logits(frozen_rows, text_teacher)
        row_index = start + jnp.arange(block, dtype=jnp.int32)
        identity = (row_index[:, None] == columns[None, :]).astype(jnp.float32)
        gradient = (jnp.exp(student - student_lse[:, None]) + jnp.exp(student - student_columns[None, :]) - 0.5 * (jnp.exp(teacher - teacher_lse[:, None]) + jnp.exp(teacher - teacher_columns[None, :])) - identity).astype(jnp.bfloat16)
        image_part = logit_scale * jnp.dot(gradient.astype(jnp.float32), text_student.astype(jnp.float32), preferred_element_type=jnp.float32)
        text_grad = text_grad + logit_scale * lax.dot_general(gradient.astype(jnp.float32), image_rows.astype(jnp.float32), (((0,), (0,)), ((), ())), preferred_element_type=jnp.float32)
        return (text_grad, image_part)
    text_grad, image_parts = lax.scan(second_pass, jnp.zeros((total, width), jnp.float32), (image_blocks, frozen_blocks, starts, student_rows.reshape(count, block), teacher_rows.reshape(count, block)))
    return (loss, image_parts.reshape(total, width), text_grad)
```

```python
import itertools
import math

import jax
import jax.numpy as jnp
from jax import lax
from jax.experimental import pallas as pl
from jax.experimental.pallas import tpu as pltpu
from jax.sharding import Mesh
from jax.sharding import PartitionSpec as P

NAMES = ("y", "zl", "x", "zh", "c")
SIZES = (4, 2, 4, 4, 2)
ROW_COL = ("y", "zl", "x", "zh", "c")
COL_ROW = ("x", "zh", "c", "y", "zl")
TEXT_GROUP = ("y", "x")
IMAGE_GROUP = ("zl", "zh", "c")

LOG2E = math.log2(math.e)
LN2 = math.log(2.0)
SCALE = 100.0
BLOCK = 64
WIDTH = 1024
SIDE = 1024
STRIP = 128
VMEM_LIMIT = 52 * 1024 * 1024


def places():
    return list(itertools.product(*(range(n) for n in SIZES)))


def index_of(place):
    at = 0
    for value, size in zip(place, SIZES):
        at = at * size + value % size
    return at


def shifted(place, axis, by):
    y, zl, x, zh, c = place
    if axis == "z":
        z = (zh * 2 + zl + by) % 8
        return (y, z % 2, x, z // 2, c)
    if axis == "x":
        return (y, zl, (x + by) % 4, zh, c)
    if axis == "y":
        return ((y + by) % 4, zl, x, zh, c)
    return (y, zl, x, zh, (c + by) % 2)


def moved(value, to):
    pairs = [(index_of(p), index_of(to(p))) for p in places()]
    return lax.ppermute(value, NAMES, pairs)


def along_u(by):
    return lambda p: shifted(p, "x" if p[4] == 0 else "y", by)


def along_v(by):
    return lambda p: shifted(p, "y" if p[4] == 0 else "x", by)


def along_z(by):
    return lambda p: shifted(p, "z", by if p[4] == 0 else -by)


def other_core(p):
    return shifted(p, "c", 1)


def gathered_text(own):
    back = moved(own, along_u(1))
    ahead = moved(own, along_u(-1))
    far = moved(back, along_u(1))
    first = jnp.concatenate([own, back], axis=0)
    second = jnp.concatenate([ahead, far], axis=0)
    first_back = moved(first, along_v(1))
    first_ahead = moved(first, along_v(-1))
    second_back = moved(second, along_v(1))
    second_ahead = moved(second, along_v(-1))
    first_far = moved(first_back, along_v(1))
    second_far = moved(second_ahead, along_v(-1))
    pieces = [
        (first, ((0, 0), (-1, 0))),
        (second, ((1, 0), (2, 0))),
        (first_back, ((0, -1), (-1, -1))),
        (first_ahead, ((0, 1), (-1, 1))),
        (second_back, ((1, -1), (2, -1))),
        (second_ahead, ((1, 1), (2, 1))),
        (first_far, ((0, 2), (-1, 2))),
        (second_far, ((1, 2), (2, 2))),
    ]
    return pieces


def gathered_images(own):
    backs, aheads = [own], [own]
    for _ in range(3):
        backs.append(moved(backs[-1], along_z(1)))
        aheads.append(moved(aheads[-1], along_z(-1)))
    far = moved(backs[3], along_z(1))
    near = jnp.concatenate([own, backs[1], aheads[1], backs[2]], axis=0)
    rest = jnp.concatenate([aheads[2], backs[3], aheads[3], far], axis=0)
    near_other = moved(near, other_core)
    rest_other = moved(rest, other_core)
    steps_near, steps_rest = (0, -1, 1, -2), (2, -3, 3, 4)
    return [
        (near, [(0, k) for k in steps_near]),
        (rest, [(0, k) for k in steps_rest]),
        (near_other, [(1, k) for k in steps_near]),
        (rest_other, [(1, k) for k in steps_rest]),
    ]


def fill(value, shape):
    return jnp.full(shape, value, jnp.float32)


def logits_kernel(counts, *refs):
    n_text, n_image = counts
    place_ref = refs[0]
    row_id_ref, col_id_ref = refs[1:3]
    text_refs = refs[3 : 3 + n_text]
    image_refs = refs[3 + n_text : 3 + n_text + n_image]
    (s_ref, t_ref, text_out, image_out, row_ref, col_ref) = refs[
        3 + n_text + n_image : 9 + n_text + n_image
    ]
    (text_frozen, image_frozen, s_high, t_high, sems) = refs[9 + n_text + n_image :]
    copies = []
    k = 0
    for group, out, frozen in (
        (text_refs, text_out, text_frozen),
        (image_refs, image_out, image_frozen),
    ):
        for ref in group:
            for b in range(ref.shape[0] // BLOCK):
                at = pl.multiple_of(place_ref[k] * BLOCK, BLOCK)
                for half, target in ((0, out), (1, frozen)):
                    copies.append(
                        pltpu.make_async_copy(
                            ref.at[pl.ds(b * BLOCK, BLOCK), pl.ds(half * WIDTH, WIDTH)],
                            target.at[pl.ds(at, BLOCK), :],
                            sems.at[2 * k + half],
                        )
                    )
                k += 1
    for copy in copies:
        copy.start()
    for copy in copies:
        copy.wait()

    lowest = -3.0e38
    s_high[...] = fill(lowest, (8, SIDE))
    t_high[...] = fill(lowest, (8, SIDE))

    @pl.loop(0, SIDE // STRIP)
    def _(i):
        rows = pl.ds(pl.multiple_of(i * STRIP, STRIP), STRIP)
        for left, right, out, high in (
            (image_out, text_out, s_ref, s_high),
            (image_frozen, text_frozen, t_ref, t_high),
        ):
            tile = (SCALE * LOG2E) * lax.dot_general(
                left[rows, :],
                right[...],
                (((1,), (1,)), ((), ())),
                preferred_element_type=jnp.float32,
            )
            out[rows, :] = tile
            high[...] = jnp.maximum(high[...], jnp.max(tile.reshape(STRIP // 8, 8, SIDE), axis=0))

    s_top = jnp.max(s_high[...], axis=0, keepdims=True)
    t_top = jnp.max(t_high[...], axis=0, keepdims=True)
    size = 16

    def strip(i, carry):
        s_sum, t_sum, d_sum, diagonal = carry
        base = pl.multiple_of(i * STRIP, STRIP)
        made = []
        for g in range(STRIP // size):
            rows = pl.ds(pl.multiple_of(base + g * size, size), size)
            s = s_ref[rows, :]
            t = t_ref[rows, :]
            gap = t - s
            s_row = jnp.max(s, axis=1, keepdims=True)
            t_row = jnp.max(t, axis=1, keepdims=True)
            s_total = jnp.sum(jnp.exp2(s - s_row), axis=1, keepdims=True)
            weights = jnp.exp2(t - t_row)
            t_total = jnp.sum(weights, axis=1, keepdims=True)
            divergence = jnp.sum(weights * gap, axis=1, keepdims=True)
            made.append(
                (
                    s_row + jnp.log2(s_total),
                    t_row + jnp.log2(t_total),
                    divergence / t_total,
                )
            )
            s_sum = s_sum + jnp.sum(jnp.exp2(s - s_top).reshape(size // 8, 8, SIDE), axis=0)
            weights = jnp.exp2(t - t_top)
            t_sum = t_sum + jnp.sum(weights.reshape(size // 8, 8, SIDE), axis=0)
            d_sum = d_sum + jnp.sum((weights * gap).reshape(size // 8, 8, SIDE), axis=0)
            same = row_id_ref[rows, :] == col_id_ref[...]
            diagonal = diagonal + jnp.sum(
                jnp.where(same, s, 0.0).reshape(size // 8, 8, SIDE), axis=0
            )
        lanes = pl.ds(base, STRIP)
        for which in range(3):
            column = jnp.concatenate([m[which] for m in made], axis=0)
            row_ref[pl.ds(which, 1), lanes] = jnp.transpose(
                jnp.broadcast_to(column, (STRIP, STRIP))
            )[0:1, :]
        return s_sum, t_sum, d_sum, diagonal

    zero = fill(0.0, (8, SIDE))
    s_sum, t_sum, d_sum, diagonal = lax.fori_loop(0, SIDE // STRIP, strip, (zero, zero, zero, zero))
    s_sum = jnp.sum(s_sum, axis=0, keepdims=True)
    t_sum = jnp.sum(t_sum, axis=0, keepdims=True)
    d_sum = jnp.sum(d_sum, axis=0, keepdims=True)
    col_ref[0:1, :] = s_top + jnp.log2(s_sum)
    col_ref[1:2, :] = t_top + jnp.log2(t_sum)
    col_ref[2:3, :] = d_sum / t_sum
    row_ref[3:4, :] = jnp.max(jnp.abs(text_out[...]).astype(jnp.float32), axis=0, keepdims=True)
    col_ref[3:4, :] = jnp.max(jnp.abs(image_out[...]).astype(jnp.float32), axis=0, keepdims=True)
    col_ref[4:5, :] = jnp.sum(diagonal, axis=0, keepdims=True)
    col_ref[5:8, :] = fill(0.0, (3, SIDE))
    row_ref[4:8, :] = fill(0.0, (4, SIDE))


def logits_and_statistics(places_in, row_id, col_id, text, images):
    f32 = jnp.float32
    anywhere = pl.BlockSpec(memory_space=pl.ANY)
    vmem = pl.BlockSpec(memory_space=pltpu.VMEM)
    smem = pl.BlockSpec(memory_space=pltpu.SMEM)

    def kernel(*refs):
        logits_kernel((len(text), len(images)), *refs)

    square = jax.ShapeDtypeStruct((SIDE, SIDE), f32)
    half = jax.ShapeDtypeStruct((SIDE, WIDTH), jnp.bfloat16)
    small = jax.ShapeDtypeStruct((8, SIDE), f32)
    return pl.pallas_call(
        kernel,
        out_shape=(square, square, half, half, small, small),
        in_specs=[smem, vmem, vmem] + [anywhere] * (len(text) + len(images)),
        out_specs=(vmem,) * 6,
        scratch_shapes=[
            pltpu.VMEM((SIDE, WIDTH), jnp.bfloat16),
            pltpu.VMEM((SIDE, WIDTH), jnp.bfloat16),
            pltpu.VMEM((8, SIDE), f32),
            pltpu.VMEM((8, SIDE), f32),
            pltpu.SemaphoreType.DMA((64,)),
        ],
        compiler_params=pltpu.CompilerParams(vmem_limit_bytes=VMEM_LIMIT),
        cost_estimate=pl.CostEstimate(
            flops=4 * SIDE * SIDE * WIDTH, bytes_accessed=20 << 20, transcendentals=4 * SIDE * SIDE
        ),
    )(places_in, row_id, col_id, *text, *images)


def gradient_kernel(s_ref, t_ref, row_ref, col_ref, row_id_ref, col_id_ref, out_ref):
    s_col = col_ref[0:1, :]
    t_col = col_ref[1:2, :] + 1.0
    size = 16

    @pl.loop(0, SIDE // STRIP)
    def _(i):
        base = pl.multiple_of(i * STRIP, STRIP)
        turned = jnp.transpose(row_ref[:, pl.ds(base, STRIP)])
        for g in range(STRIP // size):
            rows = pl.ds(pl.multiple_of(base + g * size, size), size)
            s = s_ref[rows, :]
            t = t_ref[rows, :]
            s_row = turned[g * size : (g + 1) * size, 0:1]
            t_row = turned[g * size : (g + 1) * size, 1:2] + 1.0
            value = (jnp.exp2(s - s_row) + jnp.exp2(s - s_col)) - (
                jnp.exp2(t - t_row) + jnp.exp2(t - t_col)
            )
            same = row_id_ref[rows, :] == col_id_ref[...]
            out_ref[rows, :] = jnp.where(same, value - 1.0, value).astype(jnp.bfloat16)


def gradient_of_logits(s, t, row, col, row_id, col_id):
    vmem = pl.BlockSpec(memory_space=pltpu.VMEM)
    return pl.pallas_call(
        gradient_kernel,
        out_shape=jax.ShapeDtypeStruct((SIDE, SIDE), jnp.bfloat16),
        in_specs=[vmem] * 6,
        out_specs=vmem,
        compiler_params=pltpu.CompilerParams(vmem_limit_bytes=VMEM_LIMIT),
        cost_estimate=pl.CostEstimate(
            flops=16 * SIDE * SIDE, bytes_accessed=10 << 20, transcendentals=4 * SIDE * SIDE
        ),
    )(s, t, row, col, row_id, col_id)


def sent_to_all(x, axis):
    copies = jnp.broadcast_to(x, (lax.axis_size(axis), *x.shape))
    return lax.all_to_all(copies, axis, split_axis=0, concat_axis=0, tiled=True)


def merged(pieces):
    s, t, d = pieces[:, 0], pieces[:, 1], pieces[:, 2]
    s_high, t_high = jnp.max(s, axis=0), jnp.max(t, axis=0)
    s_lse = s_high + jnp.log2(jnp.sum(jnp.exp2(s - s_high), axis=0))
    weights = jnp.exp2(t - t_high)
    total = jnp.sum(weights, axis=0)
    t_lse = t_high + jnp.log2(total)
    divergence = jnp.sum(weights * d, axis=0) / total - t_lse + s_lse
    largest = jnp.maximum(jnp.max(pieces[:, 3]), 1e-30)
    return s_lse, t_lse, jnp.sum(0.5 * LN2 * (s_lse + divergence)), largest


def summed_over(value, steps):
    for to in steps:
        value = value + moved(value, to)
    return value


def body(image_student, text_student, image_teacher, text_teacher):
    y, zl, x, zh, c = (lax.axis_index(n) for n in NAMES)
    z = zh * 2 + zl
    text_pieces = gathered_text(jnp.concatenate([text_student, text_teacher], axis=1))
    image_pieces = gathered_images(jnp.concatenate([image_student, image_teacher], axis=1))

    sign = 1 - 2 * c
    at = []
    for _, offsets in text_pieces:
        for du, dv in offsets:
            dx = jnp.where(c == 0, du, dv)
            dy = jnp.where(c == 0, dv, du)
            at.append(((y + dy) % 4) * 4 + (x + dx) % 4)
    for _, offsets in image_pieces:
        for swapped, step in offsets:
            core = c ^ swapped
            toward = sign if swapped == 0 else -sign
            at.append(core * 8 + (z + toward * step) % 8)
    where = jnp.stack(at).astype(jnp.int32)

    numbers = jnp.arange(SIDE, dtype=jnp.int32)
    slot, inner = numbers // BLOCK, numbers % BLOCK
    text_y, text_x = slot // 4, slot % 4
    col_id = (((text_x * 8 + zh * 2 + c) * 8) + text_y * 2 + zl) * BLOCK + inner
    image_c, image_z = slot // 8, slot % 8
    row_id = ((y * 2 + image_z % 2) * 32 + x * 8 + (image_z // 2) * 2 + image_c) * BLOCK + inner
    row_id, col_id = row_id[:, None], col_id[None, :]

    s, t, text_slab, image_slab, row_part, col_part = logits_and_statistics(
        where, row_id, col_id, [p for p, _ in text_pieces], [p for p, _ in image_pieces]
    )

    col_all = sent_to_all(col_part, TEXT_GROUP)
    s_col, t_col, col_terms, image_top = merged(col_all)
    diagonal = jnp.sum(col_all[:, 4]) * LN2
    row_all = sent_to_all(row_part, IMAGE_GROUP)
    s_row, t_row, row_terms, text_top = merged(row_all)

    col_value = col_terms - diagonal
    row_value = summed_over(
        jnp.full((8, 128), row_terms),
        [lambda p, k=k, a=a: flipped(p, a, k) for a in ("x", "y") for k in (1, 2)],
    )
    col_value = summed_over(
        jnp.full((8, 128), col_value),
        [other_core] + [lambda p, k=k: flipped(p, "z", k) for k in (1, 2, 4)],
    )
    loss = (row_value[0, 0] + col_value[0, 0]) / (256 * BLOCK)

    pad = jnp.zeros((6, SIDE), jnp.float32)
    gradient = gradient_of_logits(
        s,
        t,
        jnp.concatenate([s_row[None], t_row[None], pad]),
        jnp.concatenate([s_col[None], t_col[None], pad]),
        row_id,
        col_id,
    )

    text_scale = 2.0 / text_top
    image_scale = 2.0 / image_top
    half = SIDE // 2
    theirs = lax.dynamic_slice_in_dim(gradient, (1 - c) * half, half)
    mine = lax.dynamic_slice_in_dim(gradient, c * half, half)
    image_theirs = jnp.dot(theirs, text_slab, preferred_element_type=jnp.float32)
    arrived = moved((image_theirs * text_scale).astype(jnp.float16), other_core)
    text_part = (
        lax.dot_general(
            gradient, image_slab, (((0,), (0,)), ((), ())), preferred_element_type=jnp.float32
        )
        * image_scale
    ).astype(jnp.float16)
    text_blocks = lax.all_to_all(text_part.reshape(16, BLOCK, WIDTH), TEXT_GROUP, 0, 0, tiled=True)
    image_mine = (
        jnp.dot(mine, text_slab, preferred_element_type=jnp.float32) * text_scale
    ) + arrived.astype(jnp.float32)
    blocks = image_mine.astype(jnp.float16).reshape(8, BLOCK, WIDTH)

    def block(step):
        return lax.dynamic_index_in_dim(blocks, (z + sign * step) % 8, 0, keepdims=False).astype(
            jnp.float32
        )

    def narrow(v):
        return v.astype(jnp.float16)

    down = moved(narrow(block(4)), along_z(-1)).astype(jnp.float32)
    up = None
    for k in (3, 2, 1):
        first = narrow(block(-k) + down)
        second = block(k) if up is None else block(k) + up
        down = moved(first, along_z(-1)).astype(jnp.float32)
        up = moved(narrow(second), along_z(1)).astype(jnp.float32)
    image_grad = (block(0) + down + up) * (SCALE / text_scale)
    text_grad = jnp.sum(text_blocks.astype(jnp.float32), axis=0) * (SCALE / image_scale)
    return (loss, image_grad, text_grad)


def flipped(p, axis, bit):
    y, zl, x, zh, c = p
    if axis == "x":
        return (y, zl, x ^ bit, zh, c)
    if axis == "y":
        return (y ^ bit, zl, x, zh, c)
    z = (zh * 2 + zl) ^ bit
    return (y, z % 2, x, z // 2, c)


def solution(mesh):
    finer = Mesh(mesh.devices.reshape(SIZES), NAMES)
    placed = (P(ROW_COL, None), P(COL_ROW, None), P(ROW_COL, None), P(COL_ROW, None))
    return jax.shard_map(
        body,
        mesh=finer,
        in_specs=placed,
        out_specs=(P(), P(ROW_COL, None), P(COL_ROW, None)),
        check_vma=False,
    )
```

```python
import functools
import itertools
import math

import jax
import jax.numpy as jnp
from jax import lax
from jax.experimental import pallas as pl
from jax.experimental.pallas import tpu as pltpu
from jax.sharding import Mesh
from jax.sharding import PartitionSpec as P

NAMES = ("y", "zl", "x", "zh", "c")
SIZES = (4, 2, 4, 4, 2)
ROW_COL = ("y", "zl", "x", "zh", "c")
COL_ROW = ("x", "zh", "c", "y", "zl")
TEXT_GROUP = ("y", "x")
IMAGE_GROUP = ("zl", "zh", "c")

LOG2E = math.log2(math.e)
LN2 = math.log(2.0)
SCALE = 100.0
BLOCK = 64
WIDTH = 1024
SIDE = 1024
STRIP = 128
CHUNK = 256
GROUP = 16
LOGITS_VMEM = 30 * 1024 * 1024
GRADIENT_VMEM = 20 * 1024 * 1024


def places():
    return list(itertools.product(*(range(n) for n in SIZES)))


def index_of(place):
    at = 0
    for value, size in zip(place, SIZES):
        at = at * size + value % size
    return at


def shifted(place, axis, by):
    y, zl, x, zh, c = place
    if axis == "z":
        z = (zh * 2 + zl + by) % 8
        return (y, z % 2, x, z // 2, c)
    if axis == "x":
        return (y, zl, (x + by) % 4, zh, c)
    if axis == "y":
        return ((y + by) % 4, zl, x, zh, c)
    return (y, zl, x, zh, (c + by) % 2)


def moved(value, to):
    pairs = [(index_of(p), index_of(to(p))) for p in places()]
    return lax.ppermute(value, NAMES, pairs)


def along_u(by):
    return lambda p: shifted(p, "x" if p[4] == 0 else "y", by)


def along_v(by):
    return lambda p: shifted(p, "y" if p[4] == 0 else "x", by)


def along_z(by):
    return lambda p: shifted(p, "z", by if p[4] == 0 else -by)


def other_core(p):
    return shifted(p, "c", 1)


def gathered_text(own):
    back = moved(own, along_u(1))
    ahead = moved(own, along_u(-1))
    far = moved(back, along_u(1))
    first = jnp.concatenate([own, back], axis=0)
    second = jnp.concatenate([ahead, far], axis=0)
    first_back = moved(first, along_v(1))
    first_ahead = moved(first, along_v(-1))
    second_back = moved(second, along_v(1))
    second_ahead = moved(second, along_v(-1))
    first_far = moved(first_back, along_v(1))
    second_far = moved(second_ahead, along_v(-1))
    pieces = [
        (first, ((0, 0), (-1, 0))),
        (second, ((1, 0), (2, 0))),
        (first_back, ((0, -1), (-1, -1))),
        (first_ahead, ((0, 1), (-1, 1))),
        (second_back, ((1, -1), (2, -1))),
        (second_ahead, ((1, 1), (2, 1))),
        (first_far, ((0, 2), (-1, 2))),
        (second_far, ((1, 2), (2, 2))),
    ]
    return pieces


def gathered_images(own):
    backs, aheads = [own], [own]
    for _ in range(3):
        backs.append(moved(backs[-1], along_z(1)))
        aheads.append(moved(aheads[-1], along_z(-1)))
    far = moved(backs[3], along_z(1))
    near = jnp.concatenate([own, backs[1], aheads[1], backs[2]], axis=0)
    rest = jnp.concatenate([aheads[2], backs[3], aheads[3], far], axis=0)
    near_other = moved(near, other_core)
    rest_other = moved(rest, other_core)
    steps_near, steps_rest = (0, -1, 1, -2), (2, -3, 3, 4)
    return [
        (near, [(0, k) for k in steps_near]),
        (rest, [(0, k) for k in steps_rest]),
        (near_other, [(1, k) for k in steps_near]),
        (rest_other, [(1, k) for k in steps_rest]),
    ]


def logits_kernel(counts, *refs):
    n_text, n_image = counts
    place_ref = refs[0]
    text_refs = refs[1 : 1 + n_text]
    image_refs = refs[1 + n_text : 1 + n_text + n_image]
    (s_ref, t_ref, text_out, image_out, row_ref, col_ref) = refs[
        1 + n_text + n_image : 7 + n_text + n_image
    ]
    (text_frozen, image_frozen, s_high, s_sum, t_high, t_sum, sems) = refs[7 + n_text + n_image :]
    copies = []
    k = 0
    for group, out, frozen in (
        (text_refs, text_out, text_frozen),
        (image_refs, image_out, image_frozen),
    ):
        for ref in group:
            for b in range(ref.shape[0] // BLOCK):
                at = pl.multiple_of(place_ref[k] * BLOCK, BLOCK)
                for half, target in ((0, out), (1, frozen)):
                    copies.append(
                        pltpu.make_async_copy(
                            ref.at[pl.ds(b * BLOCK, BLOCK), pl.ds(half * WIDTH, WIDTH)],
                            target.at[pl.ds(at, BLOCK), :],
                            sems.at[2 * k + half],
                        )
                    )
                k += 1
    for copy in copies:
        copy.start()
    for copy in copies:
        copy.wait()

    @pl.loop(0, SIDE // CHUNK)
    def _(j):
        cols = pl.ds(pl.multiple_of(j * CHUNK, CHUNK), CHUNK)
        for which, left, right, out in (
            (0, image_out, text_out, s_ref),
            (1, image_frozen, text_frozen, t_ref),
        ):
            tile = (SCALE * LOG2E) * lax.dot_general(
                left[...],
                right[cols, :],
                (((1,), (1,)), ((), ())),
                preferred_element_type=jnp.float32,
            )
            out[:, cols] = tile
            tile = tile.reshape(SIDE // 8, 8, CHUNK)
            high = jnp.max(tile, axis=0)
            total = jnp.sum(jnp.exp2(tile - high), axis=0)
            top = jnp.max(high, axis=0, keepdims=True)
            total = jnp.sum(total * jnp.exp2(high - top), axis=0, keepdims=True)
            lse = top + jnp.log2(total)
            for n in range(GROUP):
                col_ref[n, which : which + 1, cols] = lse

    @pl.loop(0, SIDE // 64)
    def _(i):
        for g in range(8):
            rows = pl.ds(pl.multiple_of(i * 64 + g * 8, 8), 8)
            for ref, high_ref, sum_ref in ((s_ref, s_high, s_sum), (t_ref, t_high, t_sum)):
                tiles = [ref[rows, pl.ds(k * 128, 128)] for k in range(SIDE // 128)]
                high = functools.reduce(jnp.maximum, tiles)
                high_ref[rows, :] = high
                sum_ref[rows, :] = functools.reduce(jnp.add, [jnp.exp2(v - high) for v in tiles])

    @pl.loop(0, SIDE // 128)
    def _(i):
        rows = pl.ds(pl.multiple_of(i * 128, 128), 128)
        for which, high_ref, sum_ref in ((0, s_high, s_sum), (1, t_high, t_sum)):
            high = jnp.transpose(high_ref[rows, :])
            total = jnp.transpose(sum_ref[rows, :])
            top = jnp.max(high, axis=0, keepdims=True)
            total = jnp.sum(total * jnp.exp2(high - top), axis=0, keepdims=True)
            lse = top + jnp.log2(total)
            for n in range(GROUP):
                row_ref[n, which : which + 1, rows] = lse

    for slab, ref in ((text_out, row_ref), (image_out, col_ref)):
        largest = jnp.max(jnp.abs(slab[...]), axis=0, keepdims=True).astype(jnp.float32)
        largest = jnp.full((2, 128), jnp.max(largest), jnp.float32)
        for n in range(GROUP):
            ref[n, :, SIDE : SIDE + 128] = largest


def logits_and_statistics(places_in, text, images):
    f32 = jnp.float32
    anywhere = pl.BlockSpec(memory_space=pl.ANY)
    vmem = pl.BlockSpec(memory_space=pltpu.VMEM)
    smem = pl.BlockSpec(memory_space=pltpu.SMEM)

    def kernel(*refs):
        logits_kernel((len(text), len(images)), *refs)

    square = jax.ShapeDtypeStruct((SIDE, SIDE), f32)
    half = jax.ShapeDtypeStruct((SIDE, WIDTH), jnp.bfloat16)
    small = jax.ShapeDtypeStruct((GROUP, 2, SIDE + 128), f32)
    return pl.pallas_call(
        kernel,
        out_shape=(square, square, half, half, small, small),
        in_specs=[smem] + [anywhere] * (len(text) + len(images)),
        out_specs=(vmem,) * 6,
        scratch_shapes=[
            pltpu.VMEM((SIDE, WIDTH), jnp.bfloat16),
            pltpu.VMEM((SIDE, WIDTH), jnp.bfloat16),
            pltpu.VMEM((SIDE, 128), f32),
            pltpu.VMEM((SIDE, 128), f32),
            pltpu.VMEM((SIDE, 128), f32),
            pltpu.VMEM((SIDE, 128), f32),
            pltpu.SemaphoreType.DMA((64,)),
        ],
        compiler_params=pltpu.CompilerParams(vmem_limit_bytes=LOGITS_VMEM),
        cost_estimate=pl.CostEstimate(
            flops=4 * SIDE * SIDE * WIDTH, bytes_accessed=20 << 20, transcendentals=4 * SIDE * SIDE
        ),
    )(places_in, *text, *images)


def gradient_kernel(
    s_ref, t_ref, row_ref, col_ref, row_id_ref, col_id_ref, out_ref, factor_ref, part_ref, lse_ref
):
    def joined(ref, which):
        values = ref[:, which, :SIDE]
        top = jnp.max(values, axis=0, keepdims=True)
        return top + jnp.log2(jnp.sum(jnp.exp2(values - top), axis=0, keepdims=True))

    s_row_all, t_row_all = joined(row_ref, 0), joined(row_ref, 1)
    s_col_all, t_col_all = joined(col_ref, 0), joined(col_ref, 1)
    shared = (s_row_all - 0.5 * t_row_all) + (s_col_all - 0.5 * t_col_all)
    lse_ref[0:1, :] = s_row_all
    lse_ref[1:2, :] = t_row_all + 1.0
    lse_ref[2:3, :] = s_col_all
    lse_ref[3:4, :] = t_col_all + 1.0
    for k, ref in ((0, row_ref), (1, col_ref)):
        scale = 2.0 / jnp.maximum(jnp.max(ref[:, 0, SIDE : SIDE + 128]), 1e-30)
        factor_ref[k : k + 1, :] = jnp.full((1, SIDE), scale, jnp.float32)
        factor_ref[k + 2 : k + 3, :] = jnp.full((1, SIDE), SCALE, jnp.float32) / jnp.full(
            (1, SIDE), scale, jnp.float32
        )
    factor_ref[4:8, :] = jnp.zeros((4, SIDE), jnp.float32)
    size = 16

    def strip(i, total):
        base = pl.multiple_of(i * STRIP, STRIP)
        turned = jnp.transpose(lse_ref[:, pl.ds(base, STRIP)])
        for g in range(STRIP // size):
            rows = pl.ds(pl.multiple_of(base + g * size, size), size)
            s_row = jnp.broadcast_to(turned[g * size : (g + 1) * size, 0:1], (size, 128))
            t_row = jnp.broadcast_to(turned[g * size : (g + 1) * size, 1:2], (size, 128))
            row_id = jnp.broadcast_to(row_id_ref[rows, :], (size, 128))
            for k in range(SIDE // 128):
                lanes = pl.ds(k * 128, 128)
                s = s_ref[rows, lanes]
                t = t_ref[rows, lanes]
                weights = jnp.exp2(t - t_row) + jnp.exp2(t - lse_ref[3:4, lanes])
                value = (jnp.exp2(s - s_row) + jnp.exp2(s - lse_ref[2:3, lanes])) - weights
                same = row_id == col_id_ref[:, lanes]
                out_ref[rows, lanes] = jnp.where(same, value - 1.0, value).astype(jnp.bfloat16)
                total = total + (weights * (t - s) - jnp.where(same, s, 0.0))
        return total

    total = lax.fori_loop(0, SIDE // STRIP, strip, jnp.zeros((size, 128), jnp.float32))
    part = LN2 * (jnp.sum(total) + jnp.sum(shared) * (1.0 / GROUP))
    part_ref[...] = jnp.full(part_ref.shape, part, jnp.float32)


def gradient_of_logits(s, t, row, col, row_id, col_id):
    vmem = pl.BlockSpec(memory_space=pltpu.VMEM)
    f32 = jnp.float32
    return pl.pallas_call(
        gradient_kernel,
        out_shape=(
            jax.ShapeDtypeStruct((SIDE, SIDE), jnp.bfloat16),
            jax.ShapeDtypeStruct((8, SIDE), f32),
            jax.ShapeDtypeStruct((GROUP, 8, 128), f32),
        ),
        in_specs=[vmem] * 6,
        out_specs=(vmem,) * 3,
        scratch_shapes=[pltpu.VMEM((8, SIDE), f32)],
        compiler_params=pltpu.CompilerParams(vmem_limit_bytes=GRADIENT_VMEM),
        cost_estimate=pl.CostEstimate(
            flops=16 * SIDE * SIDE, bytes_accessed=10 << 20, transcendentals=4 * SIDE * SIDE
        ),
    )(s, t, row, col, row_id, col_id)


def exchanged(copies, axis):
    return lax.all_to_all(copies, axis, split_axis=0, concat_axis=0, tiled=True)


def summed_over(value, steps):
    for to in steps:
        value = value + moved(value, to)
    return value


def body(image_student, text_student, image_teacher, text_teacher):
    y, zl, x, zh, c = (lax.axis_index(n) for n in NAMES)
    z = zh * 2 + zl
    text_pieces = gathered_text(jnp.concatenate([text_student, text_teacher], axis=1))
    image_pieces = gathered_images(jnp.concatenate([image_student, image_teacher], axis=1))

    sign = 1 - 2 * c
    at = []
    for _, offsets in text_pieces:
        for du, dv in offsets:
            dx = jnp.where(c == 0, du, dv)
            dy = jnp.where(c == 0, dv, du)
            at.append(((y + dy) % 4) * 4 + (x + dx) % 4)
    for _, offsets in image_pieces:
        for swapped, step in offsets:
            core = c ^ swapped
            toward = sign if swapped == 0 else -sign
            at.append(core * 8 + (z + toward * step) % 8)
    where = jnp.stack(at).astype(jnp.int32)

    numbers = jnp.arange(SIDE, dtype=jnp.int32)
    slot, inner = numbers // BLOCK, numbers % BLOCK
    text_y, text_x = slot // 4, slot % 4
    col_id = (((text_x * 8 + zh * 2 + c) * 8) + text_y * 2 + zl) * BLOCK + inner
    image_c, image_z = slot // 8, slot % 8
    row_id = ((y * 2 + image_z % 2) * 32 + x * 8 + (image_z // 2) * 2 + image_c) * BLOCK + inner
    row_id, col_id = row_id[:, None], col_id[None, :]

    s, t, text_slab, image_slab, row_part, col_part = logits_and_statistics(
        where, [p for p, _ in text_pieces], [p for p, _ in image_pieces]
    )
    col_all = exchanged(col_part, TEXT_GROUP)
    row_all = exchanged(row_part, IMAGE_GROUP)
    gradient, factors, part = gradient_of_logits(s, t, row_all, col_all, row_id, col_id)
    text_scale, image_scale = factors[0:1], factors[1:2]
    image_factor, text_factor = factors[2:3], factors[3:4]

    value = jnp.sum(exchanged(part, TEXT_GROUP), axis=0)
    value = summed_over(
        value, [other_core] + [lambda p, k=k: flipped(p, "z", k) for k in (1, 2, 4)]
    )
    loss = value[0, 0] / (256 * BLOCK)

    half = SIDE // 2
    theirs = lax.dynamic_slice_in_dim(gradient, (1 - c) * half, half)
    mine = lax.dynamic_slice_in_dim(gradient, c * half, half)
    image_theirs = jnp.dot(theirs, text_slab, preferred_element_type=jnp.float32)
    arrived = moved((image_theirs * text_scale).astype(jnp.float16), other_core)
    text_part = (
        lax.dot_general(
            gradient, image_slab, (((0,), (0,)), ((), ())), preferred_element_type=jnp.float32
        )
        * image_scale
    ).astype(jnp.float16)
    text_blocks = lax.all_to_all(text_part.reshape(16, BLOCK, WIDTH), TEXT_GROUP, 0, 0, tiled=True)
    image_mine = (
        jnp.dot(mine, text_slab, preferred_element_type=jnp.float32) * text_scale
    ) + arrived.astype(jnp.float32)
    blocks = image_mine.astype(jnp.float16).reshape(8, BLOCK, WIDTH)

    def block(step):
        return lax.dynamic_index_in_dim(blocks, (z + sign * step) % 8, 0, keepdims=False).astype(
            jnp.float32
        )

    def narrow(v):
        return v.astype(jnp.float16)

    down = moved(narrow(block(4)), along_z(-1)).astype(jnp.float32)
    up = None
    for k in (3, 2, 1):
        first = narrow(block(-k) + down)
        second = block(k) if up is None else block(k) + up
        down = moved(first, along_z(-1)).astype(jnp.float32)
        up = moved(narrow(second), along_z(1)).astype(jnp.float32)
    image_grad = (block(0) + down + up) * image_factor
    text_grad = jnp.sum(text_blocks.astype(jnp.float32), axis=0) * text_factor
    return (loss, image_grad, text_grad)


def flipped(p, axis, bit):
    y, zl, x, zh, c = p
    if axis == "x":
        return (y, zl, x ^ bit, zh, c)
    if axis == "y":
        return (y ^ bit, zl, x, zh, c)
    z = (zh * 2 + zl) ^ bit
    return (y, z % 2, x, z // 2, c)


def solution(mesh):
    finer = Mesh(mesh.devices.reshape(SIZES), NAMES)
    placed = (P(ROW_COL, None), P(COL_ROW, None), P(ROW_COL, None), P(COL_ROW, None))
    return jax.shard_map(
        body,
        mesh=finer,
        in_specs=placed,
        out_specs=(P(), P(ROW_COL, None), P(COL_ROW, None)),
        check_vma=False,
    )
```

```python
import functools
import itertools
import math

import jax
import jax.numpy as jnp
from jax import lax
from jax.experimental import pallas as pl
from jax.experimental.pallas import tpu as pltpu
from jax.sharding import Mesh
from jax.sharding import PartitionSpec as P

NAMES = ("y", "zl", "x", "zh", "c")
SIZES = (4, 2, 4, 4, 2)
ROW_COL = ("y", "zl", "x", "zh", "c")
COL_ROW = ("x", "zh", "c", "y", "zl")
TEXT_GROUP = ("y", "x")
IMAGE_GROUP = ("zl", "zh", "c")

LOG2E = math.log2(math.e)
LN2 = math.log(2.0)
SCALE = 100.0
BLOCK = 64
WIDTH = 1024
SIDE = 1024
STRIP = 128
CHUNK = 256
GROUP = 16
LOGITS_VMEM = 58 * 1024 * 1024
GRADIENT_VMEM = 56 * 1024 * 1024
ROWS = 256


def places():
    return list(itertools.product(*(range(n) for n in SIZES)))


def index_of(place):
    at = 0
    for value, size in zip(place, SIZES):
        at = at * size + value % size
    return at


def shifted(place, axis, by):
    y, zl, x, zh, c = place
    if axis == "z":
        z = (zh * 2 + zl + by) % 8
        return (y, z % 2, x, z // 2, c)
    if axis == "x":
        return (y, zl, (x + by) % 4, zh, c)
    if axis == "y":
        return ((y + by) % 4, zl, x, zh, c)
    return (y, zl, x, zh, (c + by) % 2)


def moved(value, to):
    pairs = [(index_of(p), index_of(to(p))) for p in places()]
    return lax.ppermute(value, NAMES, pairs)


def along_u(by):
    return lambda p: shifted(p, "x" if p[4] == 0 else "y", by)


def along_v(by):
    return lambda p: shifted(p, "y" if p[4] == 0 else "x", by)


def along_z(by):
    return lambda p: shifted(p, "z", by if p[4] == 0 else -by)


def other_core(p):
    return shifted(p, "c", 1)


def gathered(text, image):
    tie = lax.optimization_barrier
    back, ahead = moved(text, along_u(1)), moved(text, along_u(-1))
    backs, aheads = [image, moved(image, along_z(1))], [image, moved(image, along_z(-1))]
    back, ahead, backs[1], aheads[1] = tie((back, ahead, backs[1], aheads[1]))

    first = jnp.concatenate([text, back], axis=0)
    far = moved(back, along_u(1))
    first_back, first_ahead = moved(first, along_v(1)), moved(first, along_v(-1))
    backs.append(moved(backs[1], along_z(1)))
    aheads.append(moved(aheads[1], along_z(-1)))
    far, first_back, first_ahead, backs[2], aheads[2] = tie(
        (far, first_back, first_ahead, backs[2], aheads[2])
    )

    second = jnp.concatenate([ahead, far], axis=0)
    second_back, second_ahead = moved(second, along_v(1)), moved(second, along_v(-1))
    backs.append(moved(backs[2], along_z(1)))
    aheads.append(moved(aheads[2], along_z(-1)))
    near = jnp.concatenate([image, backs[1], aheads[1], backs[2]], axis=0)
    near_other = moved(near, other_core)
    second_back, second_ahead, backs[3], aheads[3], near_other = tie(
        (second_back, second_ahead, backs[3], aheads[3], near_other)
    )

    first_far = moved(first_back, along_v(1))
    second_far = moved(second_ahead, along_v(-1))
    distant = moved(backs[3], along_z(1))
    rest = jnp.concatenate([aheads[2], backs[3], aheads[3], distant], axis=0)
    rest_other = moved(rest, other_core)
    steps_near, steps_rest = (0, -1, 1, -2), (2, -3, 3, 4)
    return [
        (first, ((0, 0), (-1, 0))),
        (second, ((1, 0), (2, 0))),
        (first_back, ((0, -1), (-1, -1))),
        (first_ahead, ((0, 1), (-1, 1))),
        (second_back, ((1, -1), (2, -1))),
        (second_ahead, ((1, 1), (2, 1))),
        (first_far, ((0, 2), (-1, 2))),
        (second_far, ((1, 2), (2, 2))),
    ], [
        (near, [(0, k) for k in steps_near]),
        (rest, [(0, k) for k in steps_rest]),
        (near_other, [(1, k) for k in steps_near]),
        (rest_other, [(1, k) for k in steps_rest]),
    ]


def logits_kernel(counts, *refs):
    n_text, n_image = counts
    place_ref = refs[0]
    text_refs = refs[1 : 1 + n_text]
    image_refs = refs[1 + n_text : 1 + n_text + n_image]
    (s_hbm, t_hbm, text_hbm, image_hbm, row_ref, col_ref) = refs[
        1 + n_text + n_image : 7 + n_text + n_image
    ]
    (
        s_ref,
        t_ref,
        text_out,
        image_out,
        text_frozen,
        image_frozen,
        s_high,
        s_sum,
        t_high,
        t_sum,
        sems,
        out_sems,
    ) = refs[7 + n_text + n_image :]
    copies = []
    k = 0
    for group, out, frozen in (
        (text_refs, text_out, text_frozen),
        (image_refs, image_out, image_frozen),
    ):
        for ref in group:
            for b in range(ref.shape[0] // BLOCK):
                at = pl.multiple_of(place_ref[k] * BLOCK, BLOCK)
                for half, target in ((0, out), (1, frozen)):
                    copies.append(
                        pltpu.make_async_copy(
                            ref.at[pl.ds(b * BLOCK, BLOCK), pl.ds(half * WIDTH, WIDTH)],
                            target.at[pl.ds(at, BLOCK), :],
                            sems.at[2 * k + half],
                        )
                    )
                k += 1
    for copy in copies:
        copy.start()
    for copy in copies:
        copy.wait()
    slabs = [
        pltpu.make_async_copy(text_out, text_hbm, out_sems.at[2]),
        pltpu.make_async_copy(image_out, image_hbm, out_sems.at[3]),
    ]
    for copy in slabs:
        copy.start()

    @pl.loop(0, SIDE // CHUNK)
    def _(j):
        cols = pl.ds(pl.multiple_of(j * CHUNK, CHUNK), CHUNK)
        for which, left, right, out in (
            (0, image_out, text_out, s_ref),
            (1, image_frozen, text_frozen, t_ref),
        ):
            tile = (SCALE * LOG2E) * lax.dot_general(
                left[...],
                right[cols, :],
                (((1,), (1,)), ((), ())),
                preferred_element_type=jnp.float32,
            )
            out[:, cols] = tile
            tile = tile.reshape(SIDE // 8, 8, CHUNK)
            high = jnp.max(tile, axis=0)
            total = jnp.sum(jnp.exp2(tile - high), axis=0)
            top = jnp.max(high, axis=0, keepdims=True)
            total = jnp.sum(total * jnp.exp2(high - top), axis=0, keepdims=True)
            lse = top + jnp.log2(total)
            for n in range(GROUP):
                col_ref[n, which : which + 1, cols] = lse

    logits = [
        pltpu.make_async_copy(s_ref, s_hbm, out_sems.at[0]),
        pltpu.make_async_copy(t_ref, t_hbm, out_sems.at[1]),
    ]
    for copy in logits:
        copy.start()

    @pl.loop(0, SIDE // 64)
    def _(i):
        for g in range(8):
            rows = pl.ds(pl.multiple_of(i * 64 + g * 8, 8), 8)
            for ref, high_ref, sum_ref in ((s_ref, s_high, s_sum), (t_ref, t_high, t_sum)):
                tiles = [ref[rows, pl.ds(k * 128, 128)] for k in range(SIDE // 128)]
                high = functools.reduce(jnp.maximum, tiles)
                high_ref[rows, :] = high
                sum_ref[rows, :] = functools.reduce(jnp.add, [jnp.exp2(v - high) for v in tiles])

    @pl.loop(0, SIDE // 128)
    def _(i):
        rows = pl.ds(pl.multiple_of(i * 128, 128), 128)
        for which, high_ref, sum_ref in ((0, s_high, s_sum), (1, t_high, t_sum)):
            high = jnp.transpose(high_ref[rows, :])
            total = jnp.transpose(sum_ref[rows, :])
            top = jnp.max(high, axis=0, keepdims=True)
            total = jnp.sum(total * jnp.exp2(high - top), axis=0, keepdims=True)
            lse = top + jnp.log2(total)
            for n in range(GROUP):
                row_ref[n, which : which + 1, rows] = lse

    for slab, ref in ((text_out, row_ref), (image_out, col_ref)):
        largest = jnp.max(jnp.abs(slab[...]), axis=0, keepdims=True).astype(jnp.float32)
        largest = jnp.full((2, 128), jnp.max(largest), jnp.float32)
        for n in range(GROUP):
            ref[n, :, SIDE : SIDE + 128] = largest
    for copy in slabs + logits:
        copy.wait()


def logits_and_statistics(places_in, text, images):
    f32 = jnp.float32
    anywhere = pl.BlockSpec(memory_space=pl.ANY)
    vmem = pl.BlockSpec(memory_space=pltpu.VMEM)
    smem = pl.BlockSpec(memory_space=pltpu.SMEM)
    hbm = pl.BlockSpec(memory_space=pltpu.HBM)

    def kernel(*refs):
        logits_kernel((len(text), len(images)), *refs)

    square = jax.ShapeDtypeStruct((SIDE, SIDE), f32)
    half = jax.ShapeDtypeStruct((SIDE, WIDTH), jnp.bfloat16)
    small = jax.ShapeDtypeStruct((GROUP, 2, SIDE + 128), f32)
    return pl.pallas_call(
        kernel,
        out_shape=(square, square, half, half, small, small),
        in_specs=[smem] + [anywhere] * (len(text) + len(images)),
        out_specs=(hbm,) * 4 + (vmem,) * 2,
        scratch_shapes=[
            pltpu.VMEM((SIDE, SIDE), f32),
            pltpu.VMEM((SIDE, SIDE), f32),
            pltpu.VMEM((SIDE, WIDTH), jnp.bfloat16),
            pltpu.VMEM((SIDE, WIDTH), jnp.bfloat16),
            pltpu.VMEM((SIDE, WIDTH), jnp.bfloat16),
            pltpu.VMEM((SIDE, WIDTH), jnp.bfloat16),
            pltpu.VMEM((SIDE, 128), f32),
            pltpu.VMEM((SIDE, 128), f32),
            pltpu.VMEM((SIDE, 128), f32),
            pltpu.VMEM((SIDE, 128), f32),
            pltpu.SemaphoreType.DMA((64,)),
            pltpu.SemaphoreType.DMA((4,)),
        ],
        compiler_params=pltpu.CompilerParams(vmem_limit_bytes=LOGITS_VMEM),
        cost_estimate=pl.CostEstimate(
            flops=4 * SIDE * SIDE * WIDTH, bytes_accessed=20 << 20, transcendentals=4 * SIDE * SIDE
        ),
    )(places_in, *text, *images)


def gradient_kernel(
    s_ref,
    t_ref,
    row_ref,
    col_ref,
    row_id_ref,
    col_id_ref,
    out_ref,
    factor_ref,
    part_ref,
    lse_ref,
    total_ref,
):
    step = pl.program_id(0)
    size = 16

    def joined(ref, which):
        values = ref[:, which, :SIDE]
        top = jnp.max(values, axis=0, keepdims=True)
        return top + jnp.log2(jnp.sum(jnp.exp2(values - top), axis=0, keepdims=True))

    @pl.when(step == 0)
    def _():
        s_row_all, t_row_all = joined(row_ref, 0), joined(row_ref, 1)
        s_col_all, t_col_all = joined(col_ref, 0), joined(col_ref, 1)
        shared = (s_row_all - 0.5 * t_row_all) + (s_col_all - 0.5 * t_col_all)
        lse_ref[0:1, :] = s_row_all
        lse_ref[1:2, :] = t_row_all + 1.0
        lse_ref[2:3, :] = s_col_all
        lse_ref[3:4, :] = t_col_all + 1.0
        lse_ref[4:5, :] = shared
        for k, ref in ((0, row_ref), (1, col_ref)):
            scale = 2.0 / jnp.maximum(jnp.max(ref[:, 0, SIDE : SIDE + 128]), 1e-30)
            scale = jnp.full((1, SIDE), scale, jnp.float32)
            factor_ref[k : k + 1, :] = scale
            factor_ref[k + 2 : k + 3, :] = SCALE / scale
        factor_ref[4:8, :] = jnp.zeros((4, SIDE), jnp.float32)
        total_ref[...] = jnp.zeros((size, 128), jnp.float32)

    def strip(i, total):
        base = pl.multiple_of(i * STRIP, STRIP)
        at = pl.multiple_of(step * ROWS + base, STRIP)
        turned = jnp.transpose(lse_ref[:, pl.ds(at, STRIP)])
        for g in range(STRIP // size):
            rows = pl.ds(pl.multiple_of(base + g * size, size), size)
            s_row = jnp.broadcast_to(turned[g * size : (g + 1) * size, 0:1], (size, 128))
            t_row = jnp.broadcast_to(turned[g * size : (g + 1) * size, 1:2], (size, 128))
            row_id = jnp.broadcast_to(row_id_ref[rows, :], (size, 128))
            for k in range(SIDE // 128):
                lanes = pl.ds(k * 128, 128)
                s = s_ref[rows, lanes]
                t = t_ref[rows, lanes]
                weights = jnp.exp2(t - t_row) + jnp.exp2(t - lse_ref[3:4, lanes])
                value = (jnp.exp2(s - s_row) + jnp.exp2(s - lse_ref[2:3, lanes])) - weights
                same = row_id == col_id_ref[:, lanes]
                out_ref[rows, lanes] = jnp.where(same, value - 1.0, value).astype(jnp.bfloat16)
                total = total + (weights * (t - s) - jnp.where(same, s, 0.0))
        return total

    total_ref[...] = lax.fori_loop(0, ROWS // STRIP, strip, total_ref[...])

    @pl.when(step == pl.num_programs(0) - 1)
    def _():
        part = jnp.sum(total_ref[...]) + jnp.sum(lse_ref[4:5, :]) * (1.0 / GROUP)
        part_ref[...] = jnp.full(part_ref.shape, LN2 * part, jnp.float32)


def gradient_of_logits(s, t, row, col, row_id, col_id):
    f32 = jnp.float32
    by_rows = pl.BlockSpec((ROWS, SIDE), lambda i: (i, 0))

    def whole(shape):
        return pl.BlockSpec(shape, lambda i: (0,) * len(shape))

    return pl.pallas_call(
        gradient_kernel,
        grid=(SIDE // ROWS,),
        out_shape=(
            jax.ShapeDtypeStruct((SIDE, SIDE), jnp.bfloat16),
            jax.ShapeDtypeStruct((8, SIDE), f32),
            jax.ShapeDtypeStruct((8, 128), f32),
        ),
        in_specs=[
            by_rows,
            by_rows,
            whole(row.shape),
            whole(col.shape),
            pl.BlockSpec((ROWS, 1), lambda i: (i, 0)),
            whole(col_id.shape),
        ],
        out_specs=(by_rows, whole((8, SIDE)), whole((8, 128))),
        scratch_shapes=[pltpu.VMEM((8, SIDE), f32), pltpu.VMEM((16, 128), f32)],
        compiler_params=pltpu.CompilerParams(vmem_limit_bytes=GRADIENT_VMEM),
        cost_estimate=pl.CostEstimate(
            flops=16 * SIDE * SIDE, bytes_accessed=10 << 20, transcendentals=4 * SIDE * SIDE
        ),
    )(s, t, row, col, row_id, col_id)


def exchanged(copies, axis):
    return lax.all_to_all(copies, axis, split_axis=0, concat_axis=0, tiled=True)


def body(image_student, text_student, image_teacher, text_teacher):
    y, zl, x, zh, c = (lax.axis_index(n) for n in NAMES)
    z = zh * 2 + zl
    text_pieces, image_pieces = gathered(
        jnp.concatenate([text_student, text_teacher], axis=1),
        jnp.concatenate([image_student, image_teacher], axis=1),
    )

    sign = 1 - 2 * c
    at = []
    for _, offsets in text_pieces:
        for du, dv in offsets:
            dx = jnp.where(c == 0, du, dv)
            dy = jnp.where(c == 0, dv, du)
            at.append(((y + dy) % 4) * 4 + (x + dx) % 4)
    for _, offsets in image_pieces:
        for swapped, step in offsets:
            core = c ^ swapped
            toward = sign if swapped == 0 else -sign
            at.append(core * 8 + (z + toward * step) % 8)
    where = jnp.stack(at).astype(jnp.int32)

    numbers = jnp.arange(SIDE, dtype=jnp.int32)
    slot, inner = numbers // BLOCK, numbers % BLOCK
    text_y, text_x = slot // 4, slot % 4
    col_id = (((text_x * 8 + zh * 2 + c) * 8) + text_y * 2 + zl) * BLOCK + inner
    image_c, image_z = slot // 8, slot % 8
    row_id = ((y * 2 + image_z % 2) * 32 + x * 8 + (image_z // 2) * 2 + image_c) * BLOCK + inner
    row_id, col_id = row_id[:, None], col_id[None, :]

    s, t, text_slab, image_slab, row_part, col_part = logits_and_statistics(
        where, [p for p, _ in text_pieces], [p for p, _ in image_pieces]
    )
    col_all = exchanged(col_part, TEXT_GROUP)
    row_all = exchanged(row_part, IMAGE_GROUP)
    gradient, factors, part = gradient_of_logits(s, t, row_all, col_all, row_id, col_id)
    text_scale, image_scale = factors[0:1], factors[1:2]
    image_factor, text_factor = factors[2:3], factors[3:4]

    everyone = lax.all_gather(part, NAMES, axis=0, tiled=True)
    loss = jnp.sum(everyone) * (1.0 / (256 * BLOCK * 8 * 128))

    half = SIDE // 2
    theirs = lax.dynamic_slice_in_dim(gradient, (1 - c) * half, half)
    mine = lax.dynamic_slice_in_dim(gradient, c * half, half)
    image_theirs = jnp.dot(theirs, text_slab, preferred_element_type=jnp.float32)
    arrived = moved((image_theirs * text_scale).astype(jnp.float16), other_core)
    text_part = (
        lax.dot_general(
            gradient, image_slab, (((0,), (0,)), ((), ())), preferred_element_type=jnp.float32
        )
        * image_scale
    ).astype(jnp.float16)
    text_blocks = lax.all_to_all(text_part.reshape(16, BLOCK, WIDTH), TEXT_GROUP, 0, 0, tiled=True)
    image_mine = (
        jnp.dot(mine, text_slab, preferred_element_type=jnp.float32) * text_scale
    ) + arrived.astype(jnp.float32)
    blocks = image_mine.astype(jnp.float16).reshape(8, BLOCK, WIDTH)

    def block(step):
        return lax.dynamic_index_in_dim(blocks, (z + sign * step) % 8, 0, keepdims=False).astype(
            jnp.float32
        )

    def narrow(v):
        return v.astype(jnp.float16)

    down = moved(narrow(block(4)), along_z(-1)).astype(jnp.float32)
    up = None
    for k in (3, 2, 1):
        first = narrow(block(-k) + down)
        second = block(k) if up is None else block(k) + up
        down = moved(first, along_z(-1)).astype(jnp.float32)
        up = moved(narrow(second), along_z(1)).astype(jnp.float32)
    image_grad = (block(0) + down + up) * image_factor
    text_grad = jnp.sum(text_blocks.astype(jnp.float32), axis=0) * text_factor
    return (loss, image_grad, text_grad)


def solution(mesh):
    finer = Mesh(mesh.devices.reshape(SIZES), NAMES)
    placed = (P(ROW_COL, None), P(COL_ROW, None), P(ROW_COL, None), P(COL_ROW, None))
    return jax.shard_map(
        body,
        mesh=finer,
        in_specs=placed,
        out_specs=(P(), P(ROW_COL, None), P(COL_ROW, None)),
        check_vma=False,
    )
```

```python
import functools
import itertools
import math

import jax
import jax.numpy as jnp
from jax import lax
from jax.experimental import pallas as pl
from jax.experimental.pallas import tpu as pltpu
from jax.sharding import Mesh
from jax.sharding import PartitionSpec as P

NAMES = ("y", "zl", "x", "zh", "c")
SIZES = (4, 2, 4, 4, 2)
ROW_COL = ("y", "zl", "x", "zh", "c")
COL_ROW = ("x", "zh", "c", "y", "zl")
TEXT_GROUP = ("y", "x")
IMAGE_GROUP = ("zl", "zh", "c")

LOG2E = math.log2(math.e)
LN2 = math.log(2.0)
SCALE = 100.0
BLOCK = 64
WIDTH = 1024
SIDE = 1024
STRIP = 128
CHUNK = 256
GROUP = 16
LOGITS_VMEM = 58 * 1024 * 1024
GRADIENT_VMEM = 56 * 1024 * 1024
ROWS = 256


def places():
    return list(itertools.product(*(range(n) for n in SIZES)))


def index_of(place):
    at = 0
    for value, size in zip(place, SIZES):
        at = at * size + value % size
    return at


def shifted(place, axis, by):
    y, zl, x, zh, c = place
    if axis == "z":
        z = (zh * 2 + zl + by) % 8
        return (y, z % 2, x, z // 2, c)
    if axis == "x":
        return (y, zl, (x + by) % 4, zh, c)
    if axis == "y":
        return ((y + by) % 4, zl, x, zh, c)
    return (y, zl, x, zh, (c + by) % 2)


def moved(value, to):
    pairs = [(index_of(p), index_of(to(p))) for p in places()]
    return lax.ppermute(value, NAMES, pairs)


def along_u(by):
    return lambda p: shifted(p, "x" if p[4] == 0 else "y", by)


def along_v(by):
    return lambda p: shifted(p, "y" if p[4] == 0 else "x", by)


def along_z(by):
    return lambda p: shifted(p, "z", by if p[4] == 0 else -by)


def other_core(p):
    return shifted(p, "c", 1)


def gathered(text, image):
    tie = lax.optimization_barrier
    back, ahead = moved(text, along_u(1)), moved(text, along_u(-1))
    partner = moved(image, other_core)
    back, ahead, partner = tie((back, ahead, partner))

    far = moved(back, along_u(1))
    chain = [jnp.concatenate([image, partner], axis=0)]
    chain.append(moved(chain[0], along_z(1)))
    far, text, back, ahead = tie((far, text, back, ahead))

    line = jnp.concatenate([text, back, ahead, far], axis=0)
    line_back, line_ahead = moved(line, along_v(1)), moved(line, along_v(-1))
    chain.append(moved(chain[1], along_z(1)))
    chain.append(moved(chain[2], along_z(1)))
    both = jnp.concatenate([chain[1], chain[2]], axis=0)
    both_other = moved(both, other_core)
    line_back, line_ahead, chain[3] = tie((line_back, line_ahead, chain[3]))

    first_far = moved(line_back[:128], along_v(1))
    second_far = moved(line_ahead[128:], along_v(-1))
    distant = moved(chain[3][:64], along_z(1))
    third_other = moved(chain[3], other_core)
    distant_other = moved(distant, other_core)
    us = (0, -1, 1, 2)
    return [
        (line, [(du, 0) for du in us]),
        (line_back, [(du, -1) for du in us]),
        (line_ahead, [(du, 1) for du in us]),
        (first_far, ((0, 2), (-1, 2))),
        (second_far, ((1, 2), (2, 2))),
    ], [
        (chain[0], ((0, 0), (1, 0))),
        (both, ((0, -1), (1, -1), (0, -2), (1, -2))),
        (both_other, ((1, 1), (0, 1), (1, 2), (0, 2))),
        (chain[3], ((0, -3), (1, -3))),
        (third_other, ((1, 3), (0, 3))),
        (distant, ((0, 4),)),
        (distant_other, ((1, 4),)),
    ]


def logits_kernel(counts, *refs):
    n_text, n_image = counts
    place_ref = refs[0]
    text_refs = refs[1 : 1 + n_text]
    image_refs = refs[1 + n_text : 1 + n_text + n_image]
    (s_hbm, t_hbm, text_hbm, image_hbm, row_ref, col_ref) = refs[
        1 + n_text + n_image : 7 + n_text + n_image
    ]
    (
        s_ref,
        t_ref,
        text_out,
        image_out,
        text_frozen,
        image_frozen,
        s_high,
        s_sum,
        t_high,
        t_sum,
        sems,
        out_sems,
    ) = refs[7 + n_text + n_image :]
    copies = []
    k = 0
    for group, out, frozen in (
        (text_refs, text_out, text_frozen),
        (image_refs, image_out, image_frozen),
    ):
        for ref in group:
            for b in range(ref.shape[0] // BLOCK):
                at = pl.multiple_of(place_ref[k] * BLOCK, BLOCK)
                for half, target in ((0, out), (1, frozen)):
                    copies.append(
                        pltpu.make_async_copy(
                            ref.at[pl.ds(b * BLOCK, BLOCK), pl.ds(half * WIDTH, WIDTH)],
                            target.at[pl.ds(at, BLOCK), :],
                            sems.at[2 * k + half],
                        )
                    )
                k += 1
    for copy in copies:
        copy.start()
    for copy in copies:
        copy.wait()
    slabs = [
        pltpu.make_async_copy(text_out, text_hbm, out_sems.at[2]),
        pltpu.make_async_copy(image_out, image_hbm, out_sems.at[3]),
    ]
    for copy in slabs:
        copy.start()

    @pl.loop(0, SIDE // CHUNK)
    def _(j):
        cols = pl.ds(pl.multiple_of(j * CHUNK, CHUNK), CHUNK)
        for which, left, right, out in (
            (0, image_out, text_out, s_ref),
            (1, image_frozen, text_frozen, t_ref),
        ):
            tile = (SCALE * LOG2E) * lax.dot_general(
                left[...],
                right[cols, :],
                (((1,), (1,)), ((), ())),
                preferred_element_type=jnp.float32,
            )
            out[:, cols] = tile
            tile = tile.reshape(SIDE // 8, 8, CHUNK)
            high = jnp.max(tile, axis=0)
            total = jnp.sum(jnp.exp2(tile - high), axis=0)
            top = jnp.max(high, axis=0, keepdims=True)
            total = jnp.sum(total * jnp.exp2(high - top), axis=0, keepdims=True)
            lse = top + jnp.log2(total)
            for n in range(GROUP):
                col_ref[n, which : which + 1, cols] = lse

    logits = [
        pltpu.make_async_copy(s_ref, s_hbm, out_sems.at[0]),
        pltpu.make_async_copy(t_ref, t_hbm, out_sems.at[1]),
    ]
    for copy in logits:
        copy.start()

    @pl.loop(0, SIDE // 64)
    def _(i):
        for g in range(8):
            rows = pl.ds(pl.multiple_of(i * 64 + g * 8, 8), 8)
            for ref, high_ref, sum_ref in ((s_ref, s_high, s_sum), (t_ref, t_high, t_sum)):
                tiles = [ref[rows, pl.ds(k * 128, 128)] for k in range(SIDE // 128)]
                high = functools.reduce(jnp.maximum, tiles)
                high_ref[rows, :] = high
                sum_ref[rows, :] = functools.reduce(jnp.add, [jnp.exp2(v - high) for v in tiles])

    @pl.loop(0, SIDE // 128)
    def _(i):
        rows = pl.ds(pl.multiple_of(i * 128, 128), 128)
        for which, high_ref, sum_ref in ((0, s_high, s_sum), (1, t_high, t_sum)):
            high = jnp.transpose(high_ref[rows, :])
            total = jnp.transpose(sum_ref[rows, :])
            top = jnp.max(high, axis=0, keepdims=True)
            total = jnp.sum(total * jnp.exp2(high - top), axis=0, keepdims=True)
            lse = top + jnp.log2(total)
            for n in range(GROUP):
                row_ref[n, which : which + 1, rows] = lse

    for slab, ref in ((text_out, row_ref), (image_out, col_ref)):
        largest = jnp.max(jnp.abs(slab[...]), axis=0, keepdims=True).astype(jnp.float32)
        largest = jnp.full((2, 128), jnp.max(largest), jnp.float32)
        for n in range(GROUP):
            ref[n, :, SIDE : SIDE + 128] = largest
    for copy in slabs + logits:
        copy.wait()


def logits_and_statistics(places_in, text, images):
    f32 = jnp.float32
    anywhere = pl.BlockSpec(memory_space=pl.ANY)
    vmem = pl.BlockSpec(memory_space=pltpu.VMEM)
    smem = pl.BlockSpec(memory_space=pltpu.SMEM)
    hbm = pl.BlockSpec(memory_space=pltpu.HBM)

    def kernel(*refs):
        logits_kernel((len(text), len(images)), *refs)

    square = jax.ShapeDtypeStruct((SIDE, SIDE), f32)
    half = jax.ShapeDtypeStruct((SIDE, WIDTH), jnp.bfloat16)
    small = jax.ShapeDtypeStruct((GROUP, 2, SIDE + 128), f32)
    return pl.pallas_call(
        kernel,
        out_shape=(square, square, half, half, small, small),
        in_specs=[smem] + [anywhere] * (len(text) + len(images)),
        out_specs=(hbm,) * 4 + (vmem,) * 2,
        scratch_shapes=[
            pltpu.VMEM((SIDE, SIDE), f32),
            pltpu.VMEM((SIDE, SIDE), f32),
            pltpu.VMEM((SIDE, WIDTH), jnp.bfloat16),
            pltpu.VMEM((SIDE, WIDTH), jnp.bfloat16),
            pltpu.VMEM((SIDE, WIDTH), jnp.bfloat16),
            pltpu.VMEM((SIDE, WIDTH), jnp.bfloat16),
            pltpu.VMEM((SIDE, 128), f32),
            pltpu.VMEM((SIDE, 128), f32),
            pltpu.VMEM((SIDE, 128), f32),
            pltpu.VMEM((SIDE, 128), f32),
            pltpu.SemaphoreType.DMA((64,)),
            pltpu.SemaphoreType.DMA((4,)),
        ],
        compiler_params=pltpu.CompilerParams(vmem_limit_bytes=LOGITS_VMEM),
        cost_estimate=pl.CostEstimate(
            flops=4 * SIDE * SIDE * WIDTH, bytes_accessed=20 << 20, transcendentals=4 * SIDE * SIDE
        ),
    )(places_in, *text, *images)


def gradient_kernel(
    s_ref,
    t_ref,
    row_ref,
    col_ref,
    row_id_ref,
    col_id_ref,
    out_ref,
    factor_ref,
    part_ref,
    lse_ref,
    total_ref,
):
    step = pl.program_id(0)
    size = 16

    def joined(ref, which):
        values = ref[:, which, :SIDE]
        top = jnp.max(values, axis=0, keepdims=True)
        return top + jnp.log2(jnp.sum(jnp.exp2(values - top), axis=0, keepdims=True))

    @pl.when(step == 0)
    def _():
        s_row_all, t_row_all = joined(row_ref, 0), joined(row_ref, 1)
        s_col_all, t_col_all = joined(col_ref, 0), joined(col_ref, 1)
        shared = (s_row_all - 0.5 * t_row_all) + (s_col_all - 0.5 * t_col_all)
        lse_ref[0:1, :] = s_row_all
        lse_ref[1:2, :] = t_row_all + 1.0
        lse_ref[2:3, :] = s_col_all
        lse_ref[3:4, :] = t_col_all + 1.0
        lse_ref[4:5, :] = shared
        for k, ref in ((0, row_ref), (1, col_ref)):
            scale = 2.0 / jnp.maximum(jnp.max(ref[:, 0, SIDE : SIDE + 128]), 1e-30)
            scale = jnp.full((1, SIDE), scale, jnp.float32)
            factor_ref[k : k + 1, :] = scale
            factor_ref[k + 2 : k + 3, :] = SCALE / scale
        factor_ref[4:8, :] = jnp.zeros((4, SIDE), jnp.float32)
        total_ref[...] = jnp.zeros((size, 128), jnp.float32)

    def strip(i, total):
        base = pl.multiple_of(i * STRIP, STRIP)
        at = pl.multiple_of(step * ROWS + base, STRIP)
        turned = jnp.transpose(lse_ref[:, pl.ds(at, STRIP)])
        for g in range(STRIP // size):
            rows = pl.ds(pl.multiple_of(base + g * size, size), size)
            s_row = jnp.broadcast_to(turned[g * size : (g + 1) * size, 0:1], (size, 128))
            t_row = jnp.broadcast_to(turned[g * size : (g + 1) * size, 1:2], (size, 128))
            row_id = jnp.broadcast_to(row_id_ref[rows, :], (size, 128))
            for k in range(SIDE // 128):
                lanes = pl.ds(k * 128, 128)
                s = s_ref[rows, lanes]
                t = t_ref[rows, lanes]
                weights = jnp.exp2(t - t_row) + jnp.exp2(t - lse_ref[3:4, lanes])
                value = (jnp.exp2(s - s_row) + jnp.exp2(s - lse_ref[2:3, lanes])) - weights
                same = row_id == col_id_ref[:, lanes]
                out_ref[rows, lanes] = jnp.where(same, value - 1.0, value).astype(jnp.bfloat16)
                total = total + (weights * (t - s) - jnp.where(same, s, 0.0))
        return total

    total_ref[...] = lax.fori_loop(0, ROWS // STRIP, strip, total_ref[...])

    @pl.when(step == pl.num_programs(0) - 1)
    def _():
        part = jnp.sum(total_ref[...]) + jnp.sum(lse_ref[4:5, :]) * (1.0 / GROUP)
        part_ref[...] = jnp.full(part_ref.shape, LN2 * part, jnp.float32)


def gradient_of_logits(s, t, row, col, row_id, col_id):
    f32 = jnp.float32
    by_rows = pl.BlockSpec((ROWS, SIDE), lambda i: (i, 0))

    def whole(shape):
        return pl.BlockSpec(shape, lambda i: (0,) * len(shape))

    return pl.pallas_call(
        gradient_kernel,
        grid=(SIDE // ROWS,),
        out_shape=(
            jax.ShapeDtypeStruct((SIDE, SIDE), jnp.bfloat16),
            jax.ShapeDtypeStruct((8, SIDE), f32),
            jax.ShapeDtypeStruct((GROUP, 8, 128), f32),
        ),
        in_specs=[
            by_rows,
            by_rows,
            whole(row.shape),
            whole(col.shape),
            pl.BlockSpec((ROWS, 1), lambda i: (i, 0)),
            whole(col_id.shape),
        ],
        out_specs=(by_rows, whole((8, SIDE)), whole((GROUP, 8, 128))),
        scratch_shapes=[pltpu.VMEM((8, SIDE), f32), pltpu.VMEM((16, 128), f32)],
        compiler_params=pltpu.CompilerParams(vmem_limit_bytes=GRADIENT_VMEM),
        cost_estimate=pl.CostEstimate(
            flops=16 * SIDE * SIDE, bytes_accessed=10 << 20, transcendentals=4 * SIDE * SIDE
        ),
    )(s, t, row, col, row_id, col_id)


def exchanged(copies, axis):
    return lax.all_to_all(copies, axis, split_axis=0, concat_axis=0, tiled=True)


def body(image_student, text_student, image_teacher, text_teacher):
    y, zl, x, zh, c = (lax.axis_index(n) for n in NAMES)
    z = zh * 2 + zl
    text_pieces, image_pieces = gathered(
        jnp.concatenate([text_student, text_teacher], axis=1),
        jnp.concatenate([image_student, image_teacher], axis=1),
    )

    sign = 1 - 2 * c
    at = []
    for _, offsets in text_pieces:
        for du, dv in offsets:
            dx = jnp.where(c == 0, du, dv)
            dy = jnp.where(c == 0, dv, du)
            at.append(((y + dy) % 4) * 4 + (x + dx) % 4)
    for _, offsets in image_pieces:
        for swapped, step in offsets:
            at.append((c ^ swapped) * 8 + (z + sign * step) % 8)
    where = jnp.stack(at).astype(jnp.int32)

    numbers = jnp.arange(SIDE, dtype=jnp.int32)
    slot, inner = numbers // BLOCK, numbers % BLOCK
    text_y, text_x = slot // 4, slot % 4
    col_id = (((text_x * 8 + zh * 2 + c) * 8) + text_y * 2 + zl) * BLOCK + inner
    image_c, image_z = slot // 8, slot % 8
    row_id = ((y * 2 + image_z % 2) * 32 + x * 8 + (image_z // 2) * 2 + image_c) * BLOCK + inner
    row_id, col_id = row_id[:, None], col_id[None, :]

    s, t, text_slab, image_slab, row_part, col_part = logits_and_statistics(
        where, [p for p, _ in text_pieces], [p for p, _ in image_pieces]
    )
    col_all = exchanged(col_part, TEXT_GROUP)
    row_all = exchanged(row_part, IMAGE_GROUP)
    gradient, factors, part = gradient_of_logits(s, t, row_all, col_all, row_id, col_id)
    text_scale, image_scale = factors[0:1], factors[1:2]
    image_factor, text_factor = factors[2:3], factors[3:4]

    value = jnp.sum(exchanged(part, TEXT_GROUP), axis=0)

    half = SIDE // 2
    theirs = lax.dynamic_slice_in_dim(gradient, (1 - c) * half, half)
    mine = lax.dynamic_slice_in_dim(gradient, c * half, half)
    image_theirs = jnp.dot(theirs, text_slab, preferred_element_type=jnp.float32)
    arrived = moved((image_theirs * text_scale).astype(jnp.float16), other_core)
    text_part = (
        lax.dot_general(
            gradient, image_slab, (((0,), (0,)), ((), ())), preferred_element_type=jnp.float32
        )
        * image_scale
    ).astype(jnp.float16)
    text_blocks = lax.all_to_all(text_part.reshape(16, BLOCK, WIDTH), TEXT_GROUP, 0, 0, tiled=True)
    image_mine = (
        jnp.dot(mine, text_slab, preferred_element_type=jnp.float32) * text_scale
    ) + arrived.astype(jnp.float32)
    blocks = image_mine.astype(jnp.float16).reshape(8, BLOCK, WIDTH)

    def block(step):
        return lax.dynamic_index_in_dim(blocks, (z + sign * step) % 8, 0, keepdims=False).astype(
            jnp.float32
        )

    def narrow(v):
        return v.astype(jnp.float16)

    tie = lax.optimization_barrier
    steps = [other_core] + [lambda p, k=k: flipped(p, k) for k in (1, 2, 4)]
    start, value = tie((narrow(block(4)), value))
    down, other = tie((moved(start, along_z(-1)), moved(value, steps[0])))
    value = value + other
    down = down.astype(jnp.float32)
    up = None
    for k in (3, 2, 1):
        first = narrow(block(-k) + down)
        second = narrow(block(k) if up is None else block(k) + up)
        down, up, other = tie(
            (moved(first, along_z(-1)), moved(second, along_z(1)), moved(value, steps[4 - k]))
        )
        value = value + other
        down, up = down.astype(jnp.float32), up.astype(jnp.float32)
    loss = value[0, 0] / (256 * BLOCK)
    image_grad = (block(0) + down + up) * image_factor
    text_grad = jnp.sum(text_blocks.astype(jnp.float32), axis=0) * text_factor
    return (loss, image_grad, text_grad)


def flipped(p, bit):
    y, zl, x, zh, c = p
    z = (zh * 2 + zl) ^ bit
    return (y, z % 2, x, z // 2, c)


def solution(mesh):
    finer = Mesh(mesh.devices.reshape(SIZES), NAMES)
    placed = (P(ROW_COL, None), P(COL_ROW, None), P(ROW_COL, None), P(COL_ROW, None))
    return jax.shard_map(
        body,
        mesh=finer,
        in_specs=placed,
        out_specs=(P(), P(ROW_COL, None), P(COL_ROW, None)),
        check_vma=False,
    )
```

```python
import functools
import itertools
import math

import jax
import jax.numpy as jnp
from jax import lax
from jax.experimental import pallas as pl
from jax.experimental.pallas import tpu as pltpu
from jax.sharding import Mesh
from jax.sharding import PartitionSpec as P

NAMES = ("y", "zl", "x", "zh", "c")
SIZES = (4, 2, 4, 4, 2)
ROW_COL = ("y", "zl", "x", "zh", "c")
COL_ROW = ("x", "zh", "c", "y", "zl")
TEXT_GROUP = ("y", "x")
IMAGE_GROUP = ("zl", "zh", "c")

LOG2E = math.log2(math.e)
LN2 = math.log(2.0)
SCALE = 100.0
BLOCK = 64
WIDTH = 1024
SIDE = 1024
STRIP = 128
CHUNK = 256
GROUP = 16
LOGITS_VMEM = 58 * 1024 * 1024
GRADIENT_VMEM = 56 * 1024 * 1024
ROWS = 256


def places():
    return list(itertools.product(*(range(n) for n in SIZES)))


def index_of(place):
    at = 0
    for value, size in zip(place, SIZES):
        at = at * size + value % size
    return at


def shifted(place, axis, by):
    y, zl, x, zh, c = place
    if axis == "z":
        z = (zh * 2 + zl + by) % 8
        return (y, z % 2, x, z // 2, c)
    if axis == "x":
        return (y, zl, (x + by) % 4, zh, c)
    if axis == "y":
        return ((y + by) % 4, zl, x, zh, c)
    return (y, zl, x, zh, (c + by) % 2)


def moved(value, to):
    pairs = [(index_of(p), index_of(to(p))) for p in places()]
    return lax.ppermute(value, NAMES, pairs)


def along_u(by):
    return lambda p: shifted(p, "x" if p[4] == 0 else "y", by)


def along_v(by):
    return lambda p: shifted(p, "y" if p[4] == 0 else "x", by)


def along_z(by):
    return lambda p: shifted(p, "z", by if p[4] == 0 else -by)


def other_core(p):
    return shifted(p, "c", 1)


def joined_halves(*halves):
    def kernel(*refs):
        sems = refs[6]
        copies = [
            pltpu.make_async_copy(
                refs[k], refs[4 + k // 2].at[:, pl.ds(k % 2 * WIDTH, WIDTH)], sems.at[k]
            )
            for k in range(4)
        ]
        for copy in copies:
            copy.start()
        for copy in copies:
            copy.wait()

    anywhere = pl.BlockSpec(memory_space=pl.ANY)
    pair = jax.ShapeDtypeStruct((BLOCK, 2 * WIDTH), jnp.bfloat16)
    return pl.pallas_call(
        kernel,
        out_shape=(pair, pair),
        in_specs=[anywhere] * 4,
        out_specs=(anywhere,) * 2,
        scratch_shapes=[pltpu.SemaphoreType.DMA((4,))],
        cost_estimate=pl.CostEstimate(flops=0, bytes_accessed=1 << 20, transcendentals=0),
    )(*halves)


def gathered(text, image):
    tie = lax.optimization_barrier
    back, ahead = moved(text, along_u(1)), moved(text, along_u(-1))
    far = moved(text, along_u(2))
    mine = [image, moved(image, along_z(1))]
    theirs = [moved(image, other_core)]
    back, ahead, far, mine[1], theirs[0] = tie((back, ahead, far, mine[1], theirs[0]))

    line = jnp.concatenate([text, back, ahead, far], axis=0)
    line, mine[1], theirs[0] = tie((line, mine[1], theirs[0]))
    line_back, line_ahead = moved(line, along_v(1)), moved(line, along_v(-1))
    mine.append(moved(mine[1], along_z(1)))
    theirs.append(moved(theirs[0], along_z(1)))
    mine[2], theirs[1] = tie((mine[2], theirs[1]))
    mine.append(moved(mine[2], along_z(1)))
    theirs.append(moved(theirs[1], along_z(1)))
    line_back, line_ahead, mine[3], theirs[2] = tie((line_back, line_ahead, mine[3], theirs[2]))

    first_far = moved(line_back[:128], along_v(1))
    second_far = moved(line_ahead[128:], along_v(-1))
    mine.append(moved(mine[3], along_z(1)))
    theirs.append(moved(theirs[2], along_z(1)))
    early = jnp.concatenate([mine[1], mine[2], mine[3], theirs[1], theirs[2]], axis=0)
    early_other = moved(early, other_core)
    mine[4], theirs[3] = tie((mine[4], theirs[3]))
    late = jnp.concatenate([mine[4], theirs[3]], axis=0)
    late_other = moved(late, other_core)
    us = (0, -1, 1, 2)
    return [
        (line, [(du, 0) for du in us]),
        (line_back, [(du, -1) for du in us]),
        (line_ahead, [(du, 1) for du in us]),
        (first_far, ((0, 2), (-1, 2))),
        (second_far, ((1, 2), (2, 2))),
    ], [
        (image, ((0, 0),)),
        (theirs[0], ((1, 0),)),
        (early, ((0, -1), (0, -2), (0, -3), (1, -1), (1, -2))),
        (early_other, ((1, 1), (1, 2), (1, 3), (0, 1), (0, 2))),
        (late, ((0, 4), (1, -3))),
        (late_other, ((1, 4), (0, 3))),
    ]


def logits_kernel(counts, *refs):
    n_text, n_image = counts
    place_ref = refs[0]
    text_refs = refs[1 : 1 + n_text]
    image_refs = refs[1 + n_text : 1 + n_text + n_image]
    (s_hbm, t_hbm, text_hbm, image_hbm, row_ref, col_ref) = refs[
        1 + n_text + n_image : 7 + n_text + n_image
    ]
    (
        s_ref,
        t_ref,
        text_out,
        image_out,
        text_frozen,
        image_frozen,
        s_high,
        s_sum,
        t_high,
        t_sum,
        sems,
        out_sems,
    ) = refs[7 + n_text + n_image :]
    copies = []
    k = 0
    for group, out, frozen in (
        (text_refs, text_out, text_frozen),
        (image_refs, image_out, image_frozen),
    ):
        for ref in group:
            for b in range(ref.shape[0] // BLOCK):
                at = pl.multiple_of(place_ref[k] * BLOCK, BLOCK)
                for half, target in ((0, out), (1, frozen)):
                    copies.append(
                        pltpu.make_async_copy(
                            ref.at[pl.ds(b * BLOCK, BLOCK), pl.ds(half * WIDTH, WIDTH)],
                            target.at[pl.ds(at, BLOCK), :],
                            sems.at[2 * k + half],
                        )
                    )
                k += 1
    for copy in copies:
        copy.start()
    for copy in copies:
        copy.wait()
    slabs = [
        pltpu.make_async_copy(text_out, text_hbm, out_sems.at[2]),
        pltpu.make_async_copy(image_out, image_hbm, out_sems.at[3]),
    ]
    for copy in slabs:
        copy.start()

    @pl.loop(0, SIDE // CHUNK)
    def _(j):
        cols = pl.ds(pl.multiple_of(j * CHUNK, CHUNK), CHUNK)
        for which, left, right, out in (
            (0, image_out, text_out, s_ref),
            (1, image_frozen, text_frozen, t_ref),
        ):
            tile = (SCALE * LOG2E) * lax.dot_general(
                left[...],
                right[cols, :],
                (((1,), (1,)), ((), ())),
                preferred_element_type=jnp.float32,
            )
            out[:, cols] = tile
            tile = tile.reshape(SIDE // 8, 8, CHUNK)
            high = jnp.max(tile, axis=0)
            total = jnp.sum(jnp.exp2(tile - high), axis=0)
            top = jnp.max(high, axis=0, keepdims=True)
            total = jnp.sum(total * jnp.exp2(high - top), axis=0, keepdims=True)
            lse = top + jnp.log2(total)
            for n in range(GROUP):
                col_ref[n, which : which + 1, cols] = lse

    logits = [
        pltpu.make_async_copy(s_ref, s_hbm, out_sems.at[0]),
        pltpu.make_async_copy(t_ref, t_hbm, out_sems.at[1]),
    ]
    for copy in logits:
        copy.start()

    @pl.loop(0, SIDE // 64)
    def _(i):
        for g in range(8):
            rows = pl.ds(pl.multiple_of(i * 64 + g * 8, 8), 8)
            for ref, high_ref, sum_ref in ((s_ref, s_high, s_sum), (t_ref, t_high, t_sum)):
                tiles = [ref[rows, pl.ds(k * 128, 128)] for k in range(SIDE // 128)]
                high = functools.reduce(jnp.maximum, tiles)
                high_ref[rows, :] = high
                sum_ref[rows, :] = functools.reduce(jnp.add, [jnp.exp2(v - high) for v in tiles])

    @pl.loop(0, SIDE // 128)
    def _(i):
        rows = pl.ds(pl.multiple_of(i * 128, 128), 128)
        for which, high_ref, sum_ref in ((0, s_high, s_sum), (1, t_high, t_sum)):
            high = jnp.transpose(high_ref[rows, :])
            total = jnp.transpose(sum_ref[rows, :])
            top = jnp.max(high, axis=0, keepdims=True)
            total = jnp.sum(total * jnp.exp2(high - top), axis=0, keepdims=True)
            lse = top + jnp.log2(total)
            for n in range(GROUP):
                row_ref[n, which : which + 1, rows] = lse

    for slab, ref in ((text_out, row_ref), (image_out, col_ref)):
        largest = jnp.max(jnp.abs(slab[...]), axis=0, keepdims=True).astype(jnp.float32)
        largest = jnp.full((2, 128), jnp.max(largest), jnp.float32)
        for n in range(GROUP):
            ref[n, :, SIDE : SIDE + 128] = largest
    for copy in slabs + logits:
        copy.wait()


def logits_and_statistics(places_in, text, images):
    f32 = jnp.float32
    anywhere = pl.BlockSpec(memory_space=pl.ANY)
    vmem = pl.BlockSpec(memory_space=pltpu.VMEM)
    smem = pl.BlockSpec(memory_space=pltpu.SMEM)
    hbm = pl.BlockSpec(memory_space=pltpu.HBM)

    def kernel(*refs):
        logits_kernel((len(text), len(images)), *refs)

    square = jax.ShapeDtypeStruct((SIDE, SIDE), f32)
    half = jax.ShapeDtypeStruct((SIDE, WIDTH), jnp.bfloat16)
    small = jax.ShapeDtypeStruct((GROUP, 2, SIDE + 128), f32)
    return pl.pallas_call(
        kernel,
        out_shape=(square, square, half, half, small, small),
        in_specs=[smem] + [anywhere] * (len(text) + len(images)),
        out_specs=(hbm,) * 4 + (vmem,) * 2,
        scratch_shapes=[
            pltpu.VMEM((SIDE, SIDE), f32),
            pltpu.VMEM((SIDE, SIDE), f32),
            pltpu.VMEM((SIDE, WIDTH), jnp.bfloat16),
            pltpu.VMEM((SIDE, WIDTH), jnp.bfloat16),
            pltpu.VMEM((SIDE, WIDTH), jnp.bfloat16),
            pltpu.VMEM((SIDE, WIDTH), jnp.bfloat16),
            pltpu.VMEM((SIDE, 128), f32),
            pltpu.VMEM((SIDE, 128), f32),
            pltpu.VMEM((SIDE, 128), f32),
            pltpu.VMEM((SIDE, 128), f32),
            pltpu.SemaphoreType.DMA((64,)),
            pltpu.SemaphoreType.DMA((4,)),
        ],
        compiler_params=pltpu.CompilerParams(vmem_limit_bytes=LOGITS_VMEM),
        cost_estimate=pl.CostEstimate(
            flops=4 * SIDE * SIDE * WIDTH, bytes_accessed=20 << 20, transcendentals=4 * SIDE * SIDE
        ),
    )(places_in, *text, *images)


def gradient_kernel(
    s_ref,
    t_ref,
    row_ref,
    col_ref,
    row_id_ref,
    col_id_ref,
    out_ref,
    factor_ref,
    part_ref,
    lse_ref,
    total_ref,
):
    step = pl.program_id(0)
    size = 16

    def joined(ref, which):
        values = ref[:, which, :SIDE]
        top = jnp.max(values, axis=0, keepdims=True)
        return top + jnp.log2(jnp.sum(jnp.exp2(values - top), axis=0, keepdims=True))

    @pl.when(step == 0)
    def _():
        s_row_all, t_row_all = joined(row_ref, 0), joined(row_ref, 1)
        s_col_all, t_col_all = joined(col_ref, 0), joined(col_ref, 1)
        shared = (s_row_all - 0.5 * t_row_all) + (s_col_all - 0.5 * t_col_all)
        lse_ref[0:1, :] = s_row_all
        lse_ref[1:2, :] = t_row_all + 1.0
        lse_ref[2:3, :] = s_col_all
        lse_ref[3:4, :] = t_col_all + 1.0
        lse_ref[4:5, :] = shared
        for k, ref in ((0, row_ref), (1, col_ref)):
            scale = 2.0 / jnp.maximum(jnp.max(ref[:, 0, SIDE : SIDE + 128]), 1e-30)
            scale = jnp.full((1, SIDE), scale, jnp.float32)
            factor_ref[k : k + 1, :] = scale
            factor_ref[k + 2 : k + 3, :] = SCALE / scale
        factor_ref[4:8, :] = jnp.zeros((4, SIDE), jnp.float32)
        total_ref[...] = jnp.zeros((size, 128), jnp.float32)

    def strip(i, total):
        base = pl.multiple_of(i * STRIP, STRIP)
        at = pl.multiple_of(step * ROWS + base, STRIP)
        turned = jnp.transpose(lse_ref[:, pl.ds(at, STRIP)])
        for g in range(STRIP // size):
            rows = pl.ds(pl.multiple_of(base + g * size, size), size)
            s_row = jnp.broadcast_to(turned[g * size : (g + 1) * size, 0:1], (size, 128))
            t_row = jnp.broadcast_to(turned[g * size : (g + 1) * size, 1:2], (size, 128))
            row_id = jnp.broadcast_to(row_id_ref[rows, :], (size, 128))
            for k in range(SIDE // 128):
                lanes = pl.ds(k * 128, 128)
                s = s_ref[rows, lanes]
                t = t_ref[rows, lanes]
                weights = jnp.exp2(t - t_row) + jnp.exp2(t - lse_ref[3:4, lanes])
                value = (jnp.exp2(s - s_row) + jnp.exp2(s - lse_ref[2:3, lanes])) - weights
                same = row_id == col_id_ref[:, lanes]
                out_ref[rows, lanes] = jnp.where(same, value - 1.0, value).astype(jnp.bfloat16)
                total = total + (weights * (t - s) - jnp.where(same, s, 0.0))
        return total

    total_ref[...] = lax.fori_loop(0, ROWS // STRIP, strip, total_ref[...])

    @pl.when(step == pl.num_programs(0) - 1)
    def _():
        part = jnp.sum(total_ref[...]) + jnp.sum(lse_ref[4:5, :]) * (1.0 / GROUP)
        part_ref[...] = jnp.full(part_ref.shape, LN2 * part, jnp.float32)


def gradient_of_logits(s, t, row, col, row_id, col_id):
    f32 = jnp.float32
    by_rows = pl.BlockSpec((ROWS, SIDE), lambda i: (i, 0))

    def whole(shape):
        return pl.BlockSpec(shape, lambda i: (0,) * len(shape))

    return pl.pallas_call(
        gradient_kernel,
        grid=(SIDE // ROWS,),
        out_shape=(
            jax.ShapeDtypeStruct((SIDE, SIDE), jnp.bfloat16),
            jax.ShapeDtypeStruct((8, SIDE), f32),
            jax.ShapeDtypeStruct((GROUP, 8, 128), f32),
        ),
        in_specs=[
            by_rows,
            by_rows,
            whole(row.shape),
            whole(col.shape),
            pl.BlockSpec((ROWS, 1), lambda i: (i, 0)),
            whole(col_id.shape),
        ],
        out_specs=(by_rows, whole((8, SIDE)), whole((GROUP, 8, 128))),
        scratch_shapes=[pltpu.VMEM((8, SIDE), f32), pltpu.VMEM((16, 128), f32)],
        compiler_params=pltpu.CompilerParams(vmem_limit_bytes=GRADIENT_VMEM),
        cost_estimate=pl.CostEstimate(
            flops=16 * SIDE * SIDE, bytes_accessed=10 << 20, transcendentals=4 * SIDE * SIDE
        ),
    )(s, t, row, col, row_id, col_id)


def exchanged(copies, axis):
    return lax.all_to_all(copies, axis, split_axis=0, concat_axis=0, tiled=True)


def body(image_student, text_student, image_teacher, text_teacher):
    y, zl, x, zh, c = (lax.axis_index(n) for n in NAMES)
    z = zh * 2 + zl
    text_pieces, image_pieces = gathered(
        *joined_halves(text_student, text_teacher, image_student, image_teacher)
    )

    sign = 1 - 2 * c
    at = []
    for _, offsets in text_pieces:
        for du, dv in offsets:
            dx = jnp.where(c == 0, du, dv)
            dy = jnp.where(c == 0, dv, du)
            at.append(((y + dy) % 4) * 4 + (x + dx) % 4)
    for _, offsets in image_pieces:
        for swapped, step in offsets:
            at.append((c ^ swapped) * 8 + (z + sign * step) % 8)
    where = jnp.stack(at).astype(jnp.int32)

    numbers = jnp.arange(SIDE, dtype=jnp.int32)
    slot, inner = numbers // BLOCK, numbers % BLOCK
    text_y, text_x = slot // 4, slot % 4
    col_id = (((text_x * 8 + zh * 2 + c) * 8) + text_y * 2 + zl) * BLOCK + inner
    image_c, image_z = slot // 8, slot % 8
    row_id = ((y * 2 + image_z % 2) * 32 + x * 8 + (image_z // 2) * 2 + image_c) * BLOCK + inner
    row_id, col_id = row_id[:, None], col_id[None, :]

    s, t, text_slab, image_slab, row_part, col_part = logits_and_statistics(
        where, [p for p, _ in text_pieces], [p for p, _ in image_pieces]
    )
    col_all = exchanged(col_part, TEXT_GROUP)
    row_all = exchanged(row_part, IMAGE_GROUP)
    gradient, factors, part = gradient_of_logits(s, t, row_all, col_all, row_id, col_id)
    text_scale, image_scale = factors[0:1], factors[1:2]
    image_factor, text_factor = factors[2:3], factors[3:4]

    value = jnp.sum(exchanged(part, TEXT_GROUP), axis=0)

    half = SIDE // 2
    theirs = lax.dynamic_slice_in_dim(gradient, (1 - c) * half, half)
    mine = lax.dynamic_slice_in_dim(gradient, c * half, half)
    image_theirs = jnp.dot(theirs, text_slab, preferred_element_type=jnp.float32)
    arrived = moved((image_theirs * text_scale).astype(jnp.float16), other_core)
    text_part = (
        lax.dot_general(
            gradient, image_slab, (((0,), (0,)), ((), ())), preferred_element_type=jnp.float32
        )
        * image_scale
    ).astype(jnp.float16)
    text_blocks = lax.all_to_all(text_part.reshape(16, BLOCK, WIDTH), TEXT_GROUP, 0, 0, tiled=True)
    image_mine = (
        jnp.dot(mine, text_slab, preferred_element_type=jnp.float32) * text_scale
    ) + arrived.astype(jnp.float32)
    blocks = image_mine.astype(jnp.float16).reshape(8, BLOCK, WIDTH)

    def block(step):
        return lax.dynamic_index_in_dim(blocks, (z + sign * step) % 8, 0, keepdims=False).astype(
            jnp.float32
        )

    def narrow(v):
        return v.astype(jnp.float16)

    tie = lax.optimization_barrier
    steps = [other_core] + [lambda p, k=k: flipped(p, k) for k in (1, 2, 4)]
    value, blocks = tie((value + moved(value, steps[0]), blocks))
    start, value = tie((narrow(block(4)), value))
    down = moved(start, along_z(-1)).astype(jnp.float32)
    value = value + moved(value, steps[1])
    up = None
    for k in (3, 2, 1):
        first = narrow(block(-k) + down)
        second = narrow(block(k) if up is None else block(k) + up)
        first, second, value = tie((first, second, value))
        down = moved(first, along_z(-1)).astype(jnp.float32)
        up = moved(second, along_z(1)).astype(jnp.float32)
        if k > 1:
            value = value + moved(value, steps[5 - k])
    loss = value[0, 0] / (256 * BLOCK)
    image_grad = (block(0) + down + up) * image_factor
    text_grad = jnp.sum(text_blocks.astype(jnp.float32), axis=0) * text_factor
    return (loss, image_grad, text_grad)


def flipped(p, bit):
    y, zl, x, zh, c = p
    z = (zh * 2 + zl) ^ bit
    return (y, z % 2, x, z // 2, c)


def solution(mesh):
    finer = Mesh(mesh.devices.reshape(SIZES), NAMES)
    placed = (P(ROW_COL, None), P(COL_ROW, None), P(ROW_COL, None), P(COL_ROW, None))
    return jax.shard_map(
        body,
        mesh=finer,
        in_specs=placed,
        out_specs=(P(), P(ROW_COL, None), P(COL_ROW, None)),
        check_vma=False,
    )
```

```python
import functools
import itertools
import math

import jax
import jax.numpy as jnp
from jax import lax
from jax.experimental import pallas as pl
from jax.experimental.pallas import tpu as pltpu
from jax.sharding import Mesh
from jax.sharding import PartitionSpec as P

NAMES = ("y", "zl", "x", "zh", "c")
SIZES = (4, 2, 4, 4, 2)
ROW_COL = ("y", "zl", "x", "zh", "c")
COL_ROW = ("x", "zh", "c", "y", "zl")
TEXT_GROUP = ("y", "x")
IMAGE_GROUP = ("zl", "zh", "c")

LOG2E = math.log2(math.e)
LN2 = math.log(2.0)
SCALE = 100.0
BLOCK = 64
WIDTH = 1024
SIDE = 1024
STRIP = 128
CHUNK = 256
GROUP = 16
LOGITS_VMEM = 58 * 1024 * 1024
GRADIENT_VMEM = 56 * 1024 * 1024
ROWS = 256


def places():
    return list(itertools.product(*(range(n) for n in SIZES)))


def index_of(place):
    at = 0
    for value, size in zip(place, SIZES):
        at = at * size + value % size
    return at


def shifted(place, axis, by):
    y, zl, x, zh, c = place
    if axis == "z":
        z = (zh * 2 + zl + by) % 8
        return (y, z % 2, x, z // 2, c)
    if axis == "x":
        return (y, zl, (x + by) % 4, zh, c)
    if axis == "y":
        return ((y + by) % 4, zl, x, zh, c)
    return (y, zl, x, zh, (c + by) % 2)


def moved(value, to):
    pairs = [(index_of(p), index_of(to(p))) for p in places()]
    return lax.ppermute(value, NAMES, pairs)


def along_u(by):
    return lambda p: shifted(p, "x" if p[4] == 0 else "y", by)


def along_v(by):
    return lambda p: shifted(p, "y" if p[4] == 0 else "x", by)


def along_z(by):
    return lambda p: shifted(p, "z", by if p[4] == 0 else -by)


def other_core(p):
    return shifted(p, "c", 1)


def joined_halves(*halves):
    def kernel(*refs):
        for k in range(4):
            refs[4 + k // 2][:, k % 2 * WIDTH : (k % 2 + 1) * WIDTH] = refs[k][...]

    vmem = pl.BlockSpec(memory_space=pltpu.VMEM)
    pair = jax.ShapeDtypeStruct((BLOCK, 2 * WIDTH), jnp.bfloat16)
    return pl.pallas_call(
        kernel,
        out_shape=(pair, pair),
        in_specs=[vmem] * 4,
        out_specs=(vmem,) * 2,
        cost_estimate=pl.CostEstimate(flops=0, bytes_accessed=1 << 20, transcendentals=0),
    )(*halves)


def gathered(text, image):
    tie = lax.optimization_barrier
    back, ahead = moved(text, along_u(1)), moved(text, along_u(-1))
    far = moved(text, along_u(2))
    mine = [image, moved(image, along_z(1))]
    theirs = [moved(image, other_core)]
    back, ahead, far, mine[1], theirs[0] = tie((back, ahead, far, mine[1], theirs[0]))

    line = jnp.concatenate([text, back, ahead, far], axis=0)
    line, mine[1], theirs[0] = tie((line, mine[1], theirs[0]))
    line_back, line_ahead = moved(line, along_v(1)), moved(line, along_v(-1))
    mine.append(moved(mine[1], along_z(1)))
    theirs.append(moved(theirs[0], along_z(1)))
    mine[2], theirs[1] = tie((mine[2], theirs[1]))
    mine.append(moved(mine[2], along_z(1)))
    theirs.append(moved(theirs[1], along_z(1)))
    line_back, line_ahead, mine[3], theirs[2] = tie((line_back, line_ahead, mine[3], theirs[2]))

    first_far = moved(line_back[:128], along_v(1))
    second_far = moved(line_ahead[128:], along_v(-1))
    mine.append(moved(mine[3], along_z(1)))
    theirs.append(moved(theirs[2], along_z(1)))
    early = jnp.concatenate([mine[1], mine[2], mine[3], theirs[1], theirs[2]], axis=0)
    early_other = moved(early, other_core)
    mine[4], theirs[3] = tie((mine[4], theirs[3]))
    late = jnp.concatenate([mine[4], theirs[3]], axis=0)
    late_other = moved(late, other_core)
    us = (0, -1, 1, 2)
    return [
        (line, [(du, 0) for du in us]),
        (line_back, [(du, -1) for du in us]),
        (line_ahead, [(du, 1) for du in us]),
        (first_far, ((0, 2), (-1, 2))),
        (second_far, ((1, 2), (2, 2))),
    ], [
        (image, ((0, 0),)),
        (theirs[0], ((1, 0),)),
        (early, ((0, -1), (0, -2), (0, -3), (1, -1), (1, -2))),
        (early_other, ((1, 1), (1, 2), (1, 3), (0, 1), (0, 2))),
        (late, ((0, 4), (1, -3))),
        (late_other, ((1, 4), (0, 3))),
    ]


def logits_kernel(counts, *refs):
    n_text, n_image = counts
    place_ref = refs[0]
    text_refs = refs[1 : 1 + n_text]
    image_refs = refs[1 + n_text : 1 + n_text + n_image]
    (s_hbm, t_hbm, text_hbm, image_hbm, row_ref, col_ref) = refs[
        1 + n_text + n_image : 7 + n_text + n_image
    ]
    (
        s_ref,
        t_ref,
        text_out,
        image_out,
        text_frozen,
        image_frozen,
        s_high,
        s_sum,
        t_high,
        t_sum,
        sems,
        out_sems,
    ) = refs[7 + n_text + n_image :]
    copies = []
    k = 0
    for group, out, frozen in (
        (text_refs, text_out, text_frozen),
        (image_refs, image_out, image_frozen),
    ):
        for ref in group:
            for b in range(ref.shape[0] // BLOCK):
                at = pl.multiple_of(place_ref[k] * BLOCK, BLOCK)
                for half, target in ((0, out), (1, frozen)):
                    copies.append(
                        pltpu.make_async_copy(
                            ref.at[pl.ds(b * BLOCK, BLOCK), pl.ds(half * WIDTH, WIDTH)],
                            target.at[pl.ds(at, BLOCK), :],
                            sems.at[2 * k + half],
                        )
                    )
                k += 1
    for half in (0, 1):
        for copy in copies[half::2]:
            copy.start()
    outward = [
        pltpu.make_async_copy(text_out, text_hbm, out_sems.at[2]),
        pltpu.make_async_copy(image_out, image_hbm, out_sems.at[3]),
        pltpu.make_async_copy(s_ref, s_hbm, out_sems.at[0]),
        pltpu.make_async_copy(t_ref, t_hbm, out_sems.at[1]),
    ]

    for which, left, right, out in (
        (0, image_out, text_out, s_ref),
        (1, image_frozen, text_frozen, t_ref),
    ):
        for copy in copies[which::2]:
            copy.wait()

        @pl.loop(0, SIDE // CHUNK)
        def _(j):
            cols = pl.ds(pl.multiple_of(j * CHUNK, CHUNK), CHUNK)
            tile = (SCALE * LOG2E) * lax.dot_general(
                left[...],
                right[cols, :],
                (((1,), (1,)), ((), ())),
                preferred_element_type=jnp.float32,
            )
            out[:, cols] = tile
            tile = tile.reshape(SIDE // 8, 8, CHUNK)
            high = jnp.max(tile, axis=0)
            total = jnp.sum(jnp.exp2(tile - high), axis=0)
            top = jnp.max(high, axis=0, keepdims=True)
            total = jnp.sum(total * jnp.exp2(high - top), axis=0, keepdims=True)
            lse = top + jnp.log2(total)
            for n in range(GROUP):
                col_ref[n, which : which + 1, cols] = lse

        for copy in outward[:3] if which == 0 else outward[3:]:
            copy.start()

    @pl.loop(0, SIDE // 64)
    def _(i):
        for g in range(8):
            rows = pl.ds(pl.multiple_of(i * 64 + g * 8, 8), 8)
            for ref, high_ref, sum_ref in ((s_ref, s_high, s_sum), (t_ref, t_high, t_sum)):
                tiles = [ref[rows, pl.ds(k * 128, 128)] for k in range(SIDE // 128)]
                high = functools.reduce(jnp.maximum, tiles)
                high_ref[rows, :] = high
                sum_ref[rows, :] = functools.reduce(jnp.add, [jnp.exp2(v - high) for v in tiles])

    @pl.loop(0, SIDE // 128)
    def _(i):
        rows = pl.ds(pl.multiple_of(i * 128, 128), 128)
        for which, high_ref, sum_ref in ((0, s_high, s_sum), (1, t_high, t_sum)):
            high = jnp.transpose(high_ref[rows, :])
            total = jnp.transpose(sum_ref[rows, :])
            top = jnp.max(high, axis=0, keepdims=True)
            total = jnp.sum(total * jnp.exp2(high - top), axis=0, keepdims=True)
            lse = top + jnp.log2(total)
            for n in range(GROUP):
                row_ref[n, which : which + 1, rows] = lse

    for slab, ref in ((text_out, row_ref), (image_out, col_ref)):
        largest = jnp.max(jnp.abs(slab[...]), axis=0, keepdims=True).astype(jnp.float32)
        largest = jnp.full((2, 128), jnp.max(largest), jnp.float32)
        for n in range(GROUP):
            ref[n, :, SIDE : SIDE + 128] = largest
    for copy in outward:
        copy.wait()


def logits_and_statistics(places_in, text, images):
    f32 = jnp.float32
    anywhere = pl.BlockSpec(memory_space=pl.ANY)
    vmem = pl.BlockSpec(memory_space=pltpu.VMEM)
    smem = pl.BlockSpec(memory_space=pltpu.SMEM)
    hbm = pl.BlockSpec(memory_space=pltpu.HBM)

    def kernel(*refs):
        logits_kernel((len(text), len(images)), *refs)

    square = jax.ShapeDtypeStruct((SIDE, SIDE), f32)
    half = jax.ShapeDtypeStruct((SIDE, WIDTH), jnp.bfloat16)
    small = jax.ShapeDtypeStruct((GROUP, 2, SIDE + 128), f32)
    return pl.pallas_call(
        kernel,
        out_shape=(square, square, half, half, small, small),
        in_specs=[smem] + [anywhere] * (len(text) + len(images)),
        out_specs=(hbm,) * 4 + (vmem,) * 2,
        scratch_shapes=[
            pltpu.VMEM((SIDE, SIDE), f32),
            pltpu.VMEM((SIDE, SIDE), f32),
            pltpu.VMEM((SIDE, WIDTH), jnp.bfloat16),
            pltpu.VMEM((SIDE, WIDTH), jnp.bfloat16),
            pltpu.VMEM((SIDE, WIDTH), jnp.bfloat16),
            pltpu.VMEM((SIDE, WIDTH), jnp.bfloat16),
            pltpu.VMEM((SIDE, 128), f32),
            pltpu.VMEM((SIDE, 128), f32),
            pltpu.VMEM((SIDE, 128), f32),
            pltpu.VMEM((SIDE, 128), f32),
            pltpu.SemaphoreType.DMA((64,)),
            pltpu.SemaphoreType.DMA((4,)),
        ],
        compiler_params=pltpu.CompilerParams(vmem_limit_bytes=LOGITS_VMEM),
        cost_estimate=pl.CostEstimate(
            flops=4 * SIDE * SIDE * WIDTH, bytes_accessed=20 << 20, transcendentals=4 * SIDE * SIDE
        ),
    )(places_in, *text, *images)


def gradient_kernel(
    s_ref,
    t_ref,
    row_ref,
    col_ref,
    row_id_ref,
    col_id_ref,
    out_ref,
    factor_ref,
    part_ref,
    lse_ref,
    total_ref,
):
    step = pl.program_id(0)
    size = 16

    def joined(ref, which):
        values = ref[:, which, :SIDE]
        top = jnp.max(values, axis=0, keepdims=True)
        return top + jnp.log2(jnp.sum(jnp.exp2(values - top), axis=0, keepdims=True))

    @pl.when(step == 0)
    def _():
        s_row_all, t_row_all = joined(row_ref, 0), joined(row_ref, 1)
        s_col_all, t_col_all = joined(col_ref, 0), joined(col_ref, 1)
        shared = (s_row_all - 0.5 * t_row_all) + (s_col_all - 0.5 * t_col_all)
        lse_ref[0:1, :] = s_row_all
        lse_ref[1:2, :] = t_row_all + 1.0
        lse_ref[2:3, :] = s_col_all
        lse_ref[3:4, :] = t_col_all + 1.0
        lse_ref[4:5, :] = shared
        for k, ref in ((0, row_ref), (1, col_ref)):
            scale = 2.0 / jnp.maximum(jnp.max(ref[:, 0, SIDE : SIDE + 128]), 1e-30)
            scale = jnp.full((1, SIDE), scale, jnp.float32)
            factor_ref[k : k + 1, :] = scale
            factor_ref[k + 2 : k + 3, :] = SCALE / scale
        factor_ref[4:8, :] = jnp.zeros((4, SIDE), jnp.float32)
        total_ref[...] = jnp.zeros((size, 128), jnp.float32)

    def strip(i, total):
        base = pl.multiple_of(i * STRIP, STRIP)
        at = pl.multiple_of(step * ROWS + base, STRIP)
        turned = jnp.transpose(lse_ref[:, pl.ds(at, STRIP)])
        for g in range(STRIP // size):
            rows = pl.ds(pl.multiple_of(base + g * size, size), size)
            s_row = jnp.broadcast_to(turned[g * size : (g + 1) * size, 0:1], (size, 128))
            t_row = jnp.broadcast_to(turned[g * size : (g + 1) * size, 1:2], (size, 128))
            row_id = jnp.broadcast_to(row_id_ref[rows, :], (size, 128))
            for k in range(SIDE // 128):
                lanes = pl.ds(k * 128, 128)
                s = s_ref[rows, lanes]
                t = t_ref[rows, lanes]
                weights = jnp.exp2(t - t_row) + jnp.exp2(t - lse_ref[3:4, lanes])
                value = (jnp.exp2(s - s_row) + jnp.exp2(s - lse_ref[2:3, lanes])) - weights
                same = row_id == col_id_ref[:, lanes]
                out_ref[rows, lanes] = jnp.where(same, value - 1.0, value).astype(jnp.bfloat16)
                total = total + (weights * (t - s) - jnp.where(same, s, 0.0))
        return total

    total_ref[...] = lax.fori_loop(0, ROWS // STRIP, strip, total_ref[...])

    @pl.when(step == pl.num_programs(0) - 1)
    def _():
        part = jnp.sum(total_ref[...]) + jnp.sum(lse_ref[4:5, :]) * (1.0 / GROUP)
        part_ref[...] = jnp.full(part_ref.shape, LN2 * part, jnp.float32)


def gradient_of_logits(s, t, row, col, row_id, col_id):
    f32 = jnp.float32
    by_rows = pl.BlockSpec((ROWS, SIDE), lambda i: (i, 0))

    def whole(shape):
        return pl.BlockSpec(shape, lambda i: (0,) * len(shape))

    return pl.pallas_call(
        gradient_kernel,
        grid=(SIDE // ROWS,),
        out_shape=(
            jax.ShapeDtypeStruct((SIDE, SIDE), jnp.bfloat16),
            jax.ShapeDtypeStruct((8, SIDE), f32),
            jax.ShapeDtypeStruct((GROUP, 8, 128), f32),
        ),
        in_specs=[
            by_rows,
            by_rows,
            whole(row.shape),
            whole(col.shape),
            pl.BlockSpec((ROWS, 1), lambda i: (i, 0)),
            whole(col_id.shape),
        ],
        out_specs=(by_rows, whole((8, SIDE)), whole((GROUP, 8, 128))),
        scratch_shapes=[pltpu.VMEM((8, SIDE), f32), pltpu.VMEM((16, 128), f32)],
        compiler_params=pltpu.CompilerParams(vmem_limit_bytes=GRADIENT_VMEM),
        cost_estimate=pl.CostEstimate(
            flops=16 * SIDE * SIDE, bytes_accessed=10 << 20, transcendentals=4 * SIDE * SIDE
        ),
    )(s, t, row, col, row_id, col_id)


def exchanged(copies, axis):
    return lax.all_to_all(copies, axis, split_axis=0, concat_axis=0, tiled=True)


def body(image_student, text_student, image_teacher, text_teacher):
    y, zl, x, zh, c = (lax.axis_index(n) for n in NAMES)
    z = zh * 2 + zl
    text_pieces, image_pieces = gathered(
        *joined_halves(text_student, text_teacher, image_student, image_teacher)
    )

    sign = 1 - 2 * c
    at = []
    for _, offsets in text_pieces:
        for du, dv in offsets:
            dx = jnp.where(c == 0, du, dv)
            dy = jnp.where(c == 0, dv, du)
            at.append(((y + dy) % 4) * 4 + (x + dx) % 4)
    for _, offsets in image_pieces:
        for swapped, step in offsets:
            at.append((c ^ swapped) * 8 + (z + sign * step) % 8)
    where = jnp.stack(at).astype(jnp.int32)

    numbers = jnp.arange(SIDE, dtype=jnp.int32)
    slot, inner = numbers // BLOCK, numbers % BLOCK
    text_y, text_x = slot // 4, slot % 4
    col_id = (((text_x * 8 + zh * 2 + c) * 8) + text_y * 2 + zl) * BLOCK + inner
    image_c, image_z = slot // 8, slot % 8
    row_id = ((y * 2 + image_z % 2) * 32 + x * 8 + (image_z // 2) * 2 + image_c) * BLOCK + inner
    row_id, col_id = row_id[:, None], col_id[None, :]

    s, t, text_slab, image_slab, row_part, col_part = logits_and_statistics(
        where, [p for p, _ in text_pieces], [p for p, _ in image_pieces]
    )
    col_all = exchanged(col_part, TEXT_GROUP)
    row_all = exchanged(row_part, IMAGE_GROUP)
    gradient, factors, part = gradient_of_logits(s, t, row_all, col_all, row_id, col_id)
    text_scale, image_scale = factors[0:1], factors[1:2]
    image_factor, text_factor = factors[2:3], factors[3:4]

    half = SIDE // 2
    theirs = lax.dynamic_slice_in_dim(gradient, (1 - c) * half, half)
    mine = lax.dynamic_slice_in_dim(gradient, c * half, half)
    image_theirs = jnp.dot(theirs, text_slab, preferred_element_type=jnp.float32)
    arrived = moved((image_theirs * text_scale).astype(jnp.float16), other_core)
    image_mine = (
        jnp.dot(mine, text_slab, preferred_element_type=jnp.float32) * text_scale
    ) + arrived.astype(jnp.float32)
    blocks = image_mine.astype(jnp.float16).reshape(8, BLOCK, WIDTH)

    def block(step):
        return lax.dynamic_index_in_dim(blocks, (z + sign * step) % 8, 0, keepdims=False).astype(
            jnp.float32
        )

    def narrow(v):
        return v.astype(jnp.float16)

    tie = lax.optimization_barrier
    steps = [other_core] + [lambda p, k=k: flipped(p, k) for k in (1, 2, 4)]
    start, gradient, part = tie((narrow(block(4)), gradient, part))
    down = moved(start, along_z(-1))
    value = jnp.sum(exchanged(part, TEXT_GROUP), axis=0)
    text_part = (
        lax.dot_general(
            gradient, image_slab, (((0,), (0,)), ((), ())), preferred_element_type=jnp.float32
        )
        * image_scale
    ).astype(jnp.float16)
    down, value, text_part = tie((down, value, text_part))
    text_blocks = lax.all_to_all(text_part.reshape(16, BLOCK, WIDTH), TEXT_GROUP, 0, 0, tiled=True)
    down = down.astype(jnp.float32)
    up = None
    for k in (3, 2, 1):
        first = narrow(block(-k) + down)
        second = narrow(block(k) if up is None else block(k) + up)
        first, second, value = tie((first, second, value))
        down = moved(first, along_z(-1)).astype(jnp.float32)
        up = moved(second, along_z(1)).astype(jnp.float32)
        value = value + moved(value, steps[3 - k])
    value = value + moved(value, steps[3])
    loss = value[0, 0] / (256 * BLOCK)
    image_grad = (block(0) + down + up) * image_factor
    text_grad = jnp.sum(text_blocks.astype(jnp.float32), axis=0) * text_factor
    return (loss, image_grad, text_grad)


def flipped(p, bit):
    y, zl, x, zh, c = p
    z = (zh * 2 + zl) ^ bit
    return (y, z % 2, x, z // 2, c)


def solution(mesh):
    finer = Mesh(mesh.devices.reshape(SIZES), NAMES)
    placed = (P(ROW_COL, None), P(COL_ROW, None), P(ROW_COL, None), P(COL_ROW, None))
    return jax.shard_map(
        body,
        mesh=finer,
        in_specs=placed,
        out_specs=(P(), P(ROW_COL, None), P(COL_ROW, None)),
        check_vma=False,
    )
```

```python
import functools
import itertools
import math

import jax
import jax.numpy as jnp
from jax import lax
from jax.experimental import pallas as pl
from jax.experimental.pallas import tpu as pltpu
from jax.sharding import Mesh
from jax.sharding import PartitionSpec as P

NAMES = ("y", "zl", "x", "zh", "c")
SIZES = (4, 2, 4, 4, 2)
ROW_COL = ("y", "zl", "x", "zh", "c")
COL_ROW = ("x", "zh", "c", "y", "zl")
TEXT_GROUP = ("y", "x")

LOG2E = math.log2(math.e)
LN2 = math.log(2.0)
SCALE = 100.0
BLOCK = 64
WIDTH = 1024
SIDE = 1024
STRIP = 128
CHUNK = 256
GROUP = 16
LOGITS_VMEM = 26 * 1024 * 1024
GRADIENT_VMEM = 56 * 1024 * 1024
ROWS = 256


def places():
    return list(itertools.product(*(range(n) for n in SIZES)))


def index_of(place):
    at = 0
    for value, size in zip(place, SIZES):
        at = at * size + value % size
    return at


def shifted(place, axis, by):
    y, zl, x, zh, c = place
    if axis == "z":
        z = (zh * 2 + zl + by) % 8
        return (y, z % 2, x, z // 2, c)
    if axis == "x":
        return (y, zl, (x + by) % 4, zh, c)
    if axis == "y":
        return ((y + by) % 4, zl, x, zh, c)
    return (y, zl, x, zh, (c + by) % 2)


def moved(value, to):
    pairs = [(index_of(p), index_of(to(p))) for p in places()]
    return lax.ppermute(value, NAMES, pairs)


def along_u(by):
    return lambda p: shifted(p, "x" if p[4] == 0 else "y", by)


def along_v(by):
    return lambda p: shifted(p, "y" if p[4] == 0 else "x", by)


def along_z(by):
    return lambda p: shifted(p, "z", by if p[4] == 0 else -by)


def other_core(p):
    return shifted(p, "c", 1)


def joined_halves(*halves):
    def kernel(*refs):
        for k in range(4):
            refs[4 + k // 2][:, k % 2 * WIDTH : (k % 2 + 1) * WIDTH] = refs[k][...]

    vmem = pl.BlockSpec(memory_space=pltpu.VMEM)
    pair = jax.ShapeDtypeStruct((BLOCK, 2 * WIDTH), jnp.bfloat16)
    return pl.pallas_call(
        kernel,
        out_shape=(pair, pair),
        in_specs=[vmem] * 4,
        out_specs=(vmem,) * 2,
        cost_estimate=pl.CostEstimate(flops=0, bytes_accessed=1 << 20, transcendentals=0),
    )(*halves)


def gathered(text, image):
    tie = lax.optimization_barrier
    back, ahead = moved(text, along_u(1)), moved(text, along_u(-1))
    far = moved(text, along_u(2))
    mine = [image, moved(image, along_z(1))]
    theirs = [moved(image, other_core)]
    back, ahead, far, mine[1], theirs[0] = tie((back, ahead, far, mine[1], theirs[0]))

    line = jnp.concatenate([text, back, ahead, far], axis=0)
    line, mine[1], theirs[0] = tie((line, mine[1], theirs[0]))
    line_back, line_ahead = moved(line, along_v(1)), moved(line, along_v(-1))
    mine.append(moved(mine[1], along_z(1)))
    theirs.append(moved(theirs[0], along_z(1)))
    mine[2], theirs[1] = tie((mine[2], theirs[1]))
    mine.append(moved(mine[2], along_z(1)))
    theirs.append(moved(theirs[1], along_z(1)))
    line_back, line_ahead, mine[3], theirs[2] = tie((line_back, line_ahead, mine[3], theirs[2]))

    first_far = moved(line_back[:128], along_v(1))
    second_far = moved(line_ahead[128:], along_v(-1))
    mine.append(moved(mine[3], along_z(1)))
    theirs.append(moved(theirs[2], along_z(1)))
    early = jnp.concatenate([mine[1], mine[2], mine[3], theirs[1], theirs[2]], axis=0)
    early_other = moved(early, other_core)
    mine[4], theirs[3] = tie((mine[4], theirs[3]))
    late = jnp.concatenate([mine[4], theirs[3]], axis=0)
    late_other = moved(late, other_core)
    us = (0, -1, 1, 2)
    return [
        (line, [(du, 0) for du in us]),
        (line_back, [(du, -1) for du in us]),
        (line_ahead, [(du, 1) for du in us]),
        (first_far, ((0, 2), (-1, 2))),
        (second_far, ((1, 2), (2, 2))),
    ], [
        (image, ((0, 0),)),
        (theirs[0], ((1, 0),)),
        (early, ((0, -1), (0, -2), (0, -3), (1, -1), (1, -2))),
        (early_other, ((1, 1), (1, 2), (1, 3), (0, 1), (0, 2))),
        (late, ((0, 4), (1, -3))),
        (late_other, ((1, 4), (0, 3))),
    ]


def logits_kernel(counts, *refs):
    n_text, n_image = counts
    place_ref = refs[0]
    text_refs = refs[1 : 1 + n_text]
    image_refs = refs[1 + n_text : 1 + n_text + n_image]
    (s_hbm, t_hbm, text_hbm, image_hbm, row_ref, col_ref) = refs[
        1 + n_text + n_image : 7 + n_text + n_image
    ]
    (
        s_ref,
        t_ref,
        text_out,
        image_out,
        text_frozen,
        image_frozen,
        s_high,
        s_sum,
        t_high,
        t_sum,
        sems,
        out_sems,
    ) = refs[7 + n_text + n_image :]
    copies = []
    k = 0
    for group, out, frozen in (
        (text_refs, text_out, text_frozen),
        (image_refs, image_out, image_frozen),
    ):
        for ref in group:
            for b in range(ref.shape[0] // BLOCK):
                at = pl.multiple_of(place_ref[k] * BLOCK, BLOCK)
                for half, target in ((0, out), (1, frozen)):
                    copies.append(
                        pltpu.make_async_copy(
                            ref.at[pl.ds(b * BLOCK, BLOCK), pl.ds(half * WIDTH, WIDTH)],
                            target.at[pl.ds(at, BLOCK), :],
                            sems.at[2 * k + half],
                        )
                    )
                k += 1
    for half in (0, 1):
        for copy in copies[half::2]:
            copy.start()
    outward = [
        pltpu.make_async_copy(text_out, text_hbm, out_sems.at[2]),
        pltpu.make_async_copy(image_out, image_hbm, out_sems.at[3]),
        pltpu.make_async_copy(s_ref, s_hbm, out_sems.at[0]),
        pltpu.make_async_copy(t_ref, t_hbm, out_sems.at[1]),
    ]

    for which, left, right, out in (
        (0, image_out, text_out, s_ref),
        (1, image_frozen, text_frozen, t_ref),
    ):
        for copy in copies[which::2]:
            copy.wait()

        @pl.loop(0, SIDE // CHUNK)
        def _(j):
            cols = pl.ds(pl.multiple_of(j * CHUNK, CHUNK), CHUNK)
            tile = (SCALE * LOG2E) * lax.dot_general(
                left[...],
                right[cols, :],
                (((1,), (1,)), ((), ())),
                preferred_element_type=jnp.float32,
            )
            out[:, cols] = tile
            tile = tile.reshape(SIDE // 8, 8, CHUNK)
            high = jnp.max(tile, axis=0)
            total = jnp.sum(jnp.exp2(tile - high), axis=0)
            top = jnp.max(high, axis=0, keepdims=True)
            total = jnp.sum(total * jnp.exp2(high - top), axis=0, keepdims=True)
            lse = top + jnp.log2(total)
            for n in range(GROUP):
                col_ref[n, which : which + 1, cols] = lse

        for copy in outward[:3] if which == 0 else outward[3:]:
            copy.start()

    @pl.loop(0, SIDE // 64)
    def _(i):
        for g in range(8):
            rows = pl.ds(pl.multiple_of(i * 64 + g * 8, 8), 8)
            for ref, high_ref, sum_ref in ((s_ref, s_high, s_sum), (t_ref, t_high, t_sum)):
                tiles = [ref[rows, pl.ds(k * 128, 128)] for k in range(SIDE // 128)]
                high = functools.reduce(jnp.maximum, tiles)
                high_ref[rows, :] = high
                sum_ref[rows, :] = functools.reduce(jnp.add, [jnp.exp2(v - high) for v in tiles])

    @pl.loop(0, SIDE // 128)
    def _(i):
        rows = pl.ds(pl.multiple_of(i * 128, 128), 128)
        for which, high_ref, sum_ref in ((0, s_high, s_sum), (1, t_high, t_sum)):
            high = jnp.transpose(high_ref[rows, :])
            total = jnp.transpose(sum_ref[rows, :])
            top = jnp.max(high, axis=0, keepdims=True)
            total = jnp.sum(total * jnp.exp2(high - top), axis=0, keepdims=True)
            lse = top + jnp.log2(total)
            row_ref[which : which + 1, rows] = lse

    largest = [
        jnp.full((2, 128), jnp.max(jnp.max(jnp.abs(slab[...]), axis=0).astype(jnp.float32)))
        for slab in (text_out, image_out)
    ]
    row_ref[:, SIDE : SIDE + 128] = largest[0]
    for n in range(GROUP):
        col_ref[n, :, SIDE : SIDE + 128] = largest[1]
    for copy in outward:
        copy.wait()


def logits_and_statistics(places_in, text, images):
    f32 = jnp.float32
    anywhere = pl.BlockSpec(memory_space=pl.ANY)
    vmem = pl.BlockSpec(memory_space=pltpu.VMEM)
    smem = pl.BlockSpec(memory_space=pltpu.SMEM)
    hbm = pl.BlockSpec(memory_space=pltpu.HBM)

    def kernel(*refs):
        logits_kernel((len(text), len(images)), *refs)

    square = pltpu.HBM((SIDE, SIDE), f32)
    half = pltpu.HBM((SIDE, WIDTH), jnp.bfloat16)
    one = jax.ShapeDtypeStruct((2, SIDE + 128), f32)
    small = jax.ShapeDtypeStruct((GROUP, 2, SIDE + 128), f32)
    return pl.pallas_call(
        kernel,
        out_shape=(square, square, half, half, one, small),
        in_specs=[smem] + [anywhere] * (len(text) + len(images)),
        out_specs=(hbm,) * 4 + (vmem,) * 2,
        scratch_shapes=[
            pltpu.VMEM((SIDE, SIDE), f32),
            pltpu.VMEM((SIDE, SIDE), f32),
            pltpu.VMEM((SIDE, WIDTH), jnp.bfloat16),
            pltpu.VMEM((SIDE, WIDTH), jnp.bfloat16),
            pltpu.VMEM((SIDE, WIDTH), jnp.bfloat16),
            pltpu.VMEM((SIDE, WIDTH), jnp.bfloat16),
            pltpu.VMEM((SIDE, 128), f32),
            pltpu.VMEM((SIDE, 128), f32),
            pltpu.VMEM((SIDE, 128), f32),
            pltpu.VMEM((SIDE, 128), f32),
            pltpu.SemaphoreType.DMA((64,)),
            pltpu.SemaphoreType.DMA((4,)),
        ],
        compiler_params=pltpu.CompilerParams(vmem_limit_bytes=LOGITS_VMEM),
        cost_estimate=pl.CostEstimate(
            flops=4 * SIDE * SIDE * WIDTH, bytes_accessed=20 << 20, transcendentals=4 * SIDE * SIDE
        ),
    )(places_in, *text, *images)


def gradient_kernel(
    s_ref,
    t_ref,
    row_ref,
    col_ref,
    row_id_ref,
    col_id_ref,
    out_ref,
    factor_ref,
    part_ref,
    lse_ref,
    total_ref,
):
    step = pl.program_id(0)
    size = 16

    def joined(ref, which):
        values = ref[:, which, :SIDE]
        top = jnp.max(values, axis=0, keepdims=True)
        return top + jnp.log2(jnp.sum(jnp.exp2(values - top), axis=0, keepdims=True))

    @pl.when(step == 0)
    def _():
        s_row_all, t_row_all = row_ref[0:1, :SIDE], row_ref[1:2, :SIDE]
        s_col_all, t_col_all = joined(col_ref, 0), joined(col_ref, 1)
        shared = (s_row_all - 0.5 * t_row_all) + (s_col_all - 0.5 * t_col_all)
        lse_ref[0:1, :] = s_row_all
        lse_ref[1:2, :] = t_row_all + 1.0
        lse_ref[2:3, :] = s_col_all
        lse_ref[3:4, :] = t_col_all + 1.0
        lse_ref[4:5, :] = shared
        tops = (jnp.max(row_ref[:, SIDE:]), jnp.max(col_ref[:, 0, SIDE:]))
        for k, top in enumerate(tops):
            scale = 2.0 / jnp.maximum(top, 1e-30)
            scale = jnp.full((1, SIDE), scale, jnp.float32)
            factor_ref[k : k + 1, :] = scale
            factor_ref[k + 2 : k + 3, :] = SCALE / scale
        factor_ref[4:8, :] = jnp.zeros((4, SIDE), jnp.float32)
        total_ref[...] = jnp.zeros((size, 128), jnp.float32)

    def strip(i, total):
        base = pl.multiple_of(i * STRIP, STRIP)
        at = pl.multiple_of(step * ROWS + base, STRIP)
        turned = jnp.transpose(lse_ref[:, pl.ds(at, STRIP)])
        for g in range(STRIP // size):
            rows = pl.ds(pl.multiple_of(base + g * size, size), size)
            s_row = jnp.broadcast_to(turned[g * size : (g + 1) * size, 0:1], (size, 128))
            t_row = jnp.broadcast_to(turned[g * size : (g + 1) * size, 1:2], (size, 128))
            row_id = jnp.broadcast_to(row_id_ref[rows, :], (size, 128))
            for k in range(SIDE // 128):
                lanes = pl.ds(k * 128, 128)
                s = s_ref[rows, lanes]
                t = t_ref[rows, lanes]
                weights = jnp.exp2(t - t_row) + jnp.exp2(t - lse_ref[3:4, lanes])
                value = (jnp.exp2(s - s_row) + jnp.exp2(s - lse_ref[2:3, lanes])) - weights
                same = row_id == col_id_ref[:, lanes]
                out_ref[rows, lanes] = jnp.where(same, value - 1.0, value).astype(jnp.bfloat16)
                total = total + (weights * (t - s) - jnp.where(same, s, 0.0))
        return total

    total_ref[...] = lax.fori_loop(0, ROWS // STRIP, strip, total_ref[...])

    @pl.when(step == pl.num_programs(0) - 1)
    def _():
        part = jnp.sum(total_ref[...]) + jnp.sum(lse_ref[4:5, :]) * (1.0 / GROUP)
        part_ref[...] = jnp.full(part_ref.shape, LN2 * part, jnp.float32)


def gradient_of_logits(s, t, row, col, row_id, col_id):
    f32 = jnp.float32
    by_rows = pl.BlockSpec((ROWS, SIDE), lambda i: (i, 0))

    def whole(shape):
        return pl.BlockSpec(shape, lambda i: (0,) * len(shape))

    return pl.pallas_call(
        gradient_kernel,
        grid=(SIDE // ROWS,),
        out_shape=(
            jax.ShapeDtypeStruct((SIDE, SIDE), jnp.bfloat16),
            jax.ShapeDtypeStruct((8, SIDE), f32),
            jax.ShapeDtypeStruct((GROUP, 8, 128), f32),
        ),
        in_specs=[
            by_rows,
            by_rows,
            whole(row.shape),
            whole(col.shape),
            pl.BlockSpec((ROWS, 1), lambda i: (i, 0)),
            whole(col_id.shape),
        ],
        out_specs=(by_rows, whole((8, SIDE)), whole((GROUP, 8, 128))),
        scratch_shapes=[pltpu.VMEM((8, SIDE), f32), pltpu.VMEM((16, 128), f32)],
        compiler_params=pltpu.CompilerParams(vmem_limit_bytes=GRADIENT_VMEM),
        cost_estimate=pl.CostEstimate(
            flops=16 * SIDE * SIDE, bytes_accessed=10 << 20, transcendentals=4 * SIDE * SIDE
        ),
    )(s, t, row, col, row_id, col_id)


def merged(one, other):
    high, low = jnp.maximum(one, other), jnp.minimum(one, other)
    sums = lax.broadcasted_iota(jnp.int32, one.shape, 1) < SIDE
    return jnp.where(sums, high + jnp.log2(1.0 + jnp.exp2(low - high)), high)


def exchanged(copies, axis):
    return lax.all_to_all(copies, axis, split_axis=0, concat_axis=0, tiled=True)


def body(image_student, text_student, image_teacher, text_teacher):
    y, zl, x, zh, c = (lax.axis_index(n) for n in NAMES)
    z = zh * 2 + zl
    text_pieces, image_pieces = gathered(
        *joined_halves(text_student, text_teacher, image_student, image_teacher)
    )

    sign = 1 - 2 * c
    at = []
    for _, offsets in text_pieces:
        for du, dv in offsets:
            dx = jnp.where(c == 0, du, dv)
            dy = jnp.where(c == 0, dv, du)
            at.append(((y + dy) % 4) * 4 + (x + dx) % 4)
    for _, offsets in image_pieces:
        for swapped, step in offsets:
            at.append((c ^ swapped) * 8 + (z + sign * step) % 8)
    where = jnp.stack(at).astype(jnp.int32)

    numbers = jnp.arange(SIDE, dtype=jnp.int32)
    slot, inner = numbers // BLOCK, numbers % BLOCK
    text_y, text_x = slot // 4, slot % 4
    col_id = (((text_x * 8 + zh * 2 + c) * 8) + text_y * 2 + zl) * BLOCK + inner
    image_c, image_z = slot // 8, slot % 8
    row_id = ((y * 2 + image_z % 2) * 32 + x * 8 + (image_z // 2) * 2 + image_c) * BLOCK + inner
    row_id, col_id = row_id[:, None], col_id[None, :]

    s, t, text_slab, image_slab, row_part, col_part = logits_and_statistics(
        where, [p for p, _ in text_pieces], [p for p, _ in image_pieces]
    )
    pairs = [other_core] + [lambda p, k=k: flipped(p, k) for k in (1, 2, 4)]
    col_all = exchanged(col_part, TEXT_GROUP)
    row_all = row_part
    for to in pairs[:2]:
        row_all = merged(row_all, moved(row_all, to))
    row_all, col_all = lax.optimization_barrier((row_all, col_all))
    for to in pairs[2:]:
        row_all = merged(row_all, moved(row_all, to))
    gradient, factors, part = gradient_of_logits(s, t, row_all, col_all, row_id, col_id)
    text_scale, image_scale = factors[0:1], factors[1:2]
    image_factor, text_factor = factors[2:3], factors[3:4]

    tie = lax.optimization_barrier
    value = jnp.sum(exchanged(part, TEXT_GROUP), axis=0)
    text_part = (
        lax.dot_general(
            gradient, image_slab, (((0,), (0,)), ((), ())), preferred_element_type=jnp.float32
        )
        * image_scale
    ).astype(jnp.float16)
    text_part, gradient, value = tie((text_part, gradient, value))
    text_blocks = lax.all_to_all(text_part.reshape(16, BLOCK, WIDTH), TEXT_GROUP, 0, 0, tiled=True)

    half = SIDE // 2
    theirs = lax.dynamic_slice_in_dim(gradient, (1 - c) * half, half)
    mine = lax.dynamic_slice_in_dim(gradient, c * half, half)
    image_theirs = jnp.dot(theirs, text_slab, preferred_element_type=jnp.float32)
    arrived = moved((image_theirs * text_scale).astype(jnp.float16), other_core)
    image_mine = (
        jnp.dot(mine, text_slab, preferred_element_type=jnp.float32) * text_scale
    ) + arrived.astype(jnp.float32)
    blocks = image_mine.astype(jnp.float16).reshape(8, BLOCK, WIDTH)

    def block(step):
        return lax.dynamic_index_in_dim(blocks, (z + sign * step) % 8, 0, keepdims=False).astype(
            jnp.float32
        )

    def narrow(v):
        return v.astype(jnp.float16)

    blocks, value = tie((blocks, value + moved(value, pairs[0])))
    down = moved(narrow(block(4)), along_z(-1))
    value = value + moved(value, pairs[1])
    down = down.astype(jnp.float32)
    up = None
    for k in (3, 2, 1):
        first = narrow(block(-k) + down)
        second = narrow(block(k) if up is None else block(k) + up)
        first, second, value = tie((first, second, value))
        down = moved(first, along_z(-1)).astype(jnp.float32)
        up = moved(second, along_z(1)).astype(jnp.float32)
        if k > 1:
            value = value + moved(value, pairs[5 - k])
    loss = value[0, 0] / (256 * BLOCK)
    image_grad = (block(0) + down + up) * image_factor
    text_grad = jnp.sum(text_blocks.astype(jnp.float32), axis=0) * text_factor
    return (loss, image_grad, text_grad)


def flipped(p, bit):
    y, zl, x, zh, c = p
    z = (zh * 2 + zl) ^ bit
    return (y, z % 2, x, z // 2, c)


def solution(mesh):
    finer = Mesh(mesh.devices.reshape(SIZES), NAMES)
    placed = (P(ROW_COL, None), P(COL_ROW, None), P(ROW_COL, None), P(COL_ROW, None))
    return jax.shard_map(
        body,
        mesh=finer,
        in_specs=placed,
        out_specs=(P(), P(ROW_COL, None), P(COL_ROW, None)),
        check_vma=False,
    )
```

```python
import functools
import itertools
import math

import jax
import jax.numpy as jnp
from jax import lax
from jax.experimental import pallas as pl
from jax.experimental.pallas import tpu as pltpu
from jax.sharding import Mesh
from jax.sharding import PartitionSpec as P

NAMES = ("y", "zl", "x", "zh", "c")
SIZES = (4, 2, 4, 4, 2)
ROW_COL = ("y", "zl", "x", "zh", "c")
COL_ROW = ("x", "zh", "c", "y", "zl")
TEXT_GROUP = ("y", "x")
IMAGE_GROUP = ("zl", "zh", "c")

LOG2E = math.log2(math.e)
LN2 = math.log(2.0)
SCALE = 100.0
BLOCK = 64
WIDTH = 1024
SIDE = 1024
STRIP = 128
CHUNK = 256
GROUP = 16
LOGITS_VMEM = 58 * 1024 * 1024
GRADIENT_VMEM = 20 * 1024 * 1024
ROWS = 256


def places():
    return list(itertools.product(*(range(n) for n in SIZES)))


def index_of(place):
    at = 0
    for value, size in zip(place, SIZES):
        at = at * size + value % size
    return at


def shifted(place, axis, by):
    y, zl, x, zh, c = place
    if axis == "z":
        z = (zh * 2 + zl + by) % 8
        return (y, z % 2, x, z // 2, c)
    if axis == "x":
        return (y, zl, (x + by) % 4, zh, c)
    if axis == "y":
        return ((y + by) % 4, zl, x, zh, c)
    return (y, zl, x, zh, (c + by) % 2)


def moved(value, to):
    pairs = [(index_of(p), index_of(to(p))) for p in places()]
    return lax.ppermute(value, NAMES, pairs)


def along_u(by):
    return lambda p: shifted(p, "x" if p[4] == 0 else "y", by)


def along_v(by):
    return lambda p: shifted(p, "y" if p[4] == 0 else "x", by)


def along_z(by):
    return lambda p: shifted(p, "z", by if p[4] == 0 else -by)


def other_core(p):
    return shifted(p, "c", 1)


def joined_halves(*halves):
    def kernel(*refs):
        for k in range(4):
            refs[4 + k // 2][:, k % 2 * WIDTH : (k % 2 + 1) * WIDTH] = refs[k][...]

    vmem = pl.BlockSpec(memory_space=pltpu.VMEM)
    pair = jax.ShapeDtypeStruct((BLOCK, 2 * WIDTH), jnp.bfloat16)
    return pl.pallas_call(
        kernel,
        out_shape=(pair, pair),
        in_specs=[vmem] * 4,
        out_specs=(vmem,) * 2,
        cost_estimate=pl.CostEstimate(flops=0, bytes_accessed=1 << 20, transcendentals=0),
    )(*halves)


def gathered(text, image):
    tie = lax.optimization_barrier
    back, ahead = moved(text, along_u(1)), moved(text, along_u(-1))
    far = moved(text, along_u(2))
    mine = [image, moved(image, along_z(1))]
    theirs = [moved(image, other_core)]
    back, ahead, far, mine[1], theirs[0] = tie((back, ahead, far, mine[1], theirs[0]))

    line = jnp.concatenate([text, back, ahead, far], axis=0)
    line, mine[1], theirs[0] = tie((line, mine[1], theirs[0]))
    line_back, line_ahead = moved(line, along_v(1)), moved(line, along_v(-1))
    mine.append(moved(mine[1], along_z(1)))
    theirs.append(moved(theirs[0], along_z(1)))
    mine[2], theirs[1] = tie((mine[2], theirs[1]))
    mine.append(moved(mine[2], along_z(1)))
    theirs.append(moved(theirs[1], along_z(1)))
    line_back, line_ahead, mine[3], theirs[2] = tie((line_back, line_ahead, mine[3], theirs[2]))

    first_far = moved(line_back[:128], along_v(1))
    second_far = moved(line_ahead[128:], along_v(-1))
    mine.append(moved(mine[3], along_z(1)))
    theirs.append(moved(theirs[2], along_z(1)))
    early = jnp.concatenate([mine[1], mine[2], mine[3], theirs[1], theirs[2]], axis=0)
    early_other = moved(early, other_core)
    mine[4], theirs[3] = tie((mine[4], theirs[3]))
    late = jnp.concatenate([mine[4], theirs[3]], axis=0)
    late_other = moved(late, other_core)
    us = (0, -1, 1, 2)
    return [
        (line, [(du, 0) for du in us]),
        (line_back, [(du, -1) for du in us]),
        (line_ahead, [(du, 1) for du in us]),
        (first_far, ((0, 2), (-1, 2))),
        (second_far, ((1, 2), (2, 2))),
    ], [
        (image, ((0, 0),)),
        (theirs[0], ((1, 0),)),
        (early, ((0, -1), (0, -2), (0, -3), (1, -1), (1, -2))),
        (early_other, ((1, 1), (1, 2), (1, 3), (0, 1), (0, 2))),
        (late, ((0, 4), (1, -3))),
        (late_other, ((1, 4), (0, 3))),
    ]


def logits_kernel(counts, *refs):
    n_text, n_image = counts
    place_ref = refs[0]
    text_refs = refs[1 : 1 + n_text]
    image_refs = refs[1 + n_text : 1 + n_text + n_image]
    (s_hbm, t_hbm, text_hbm, image_hbm, row_ref, col_ref) = refs[
        1 + n_text + n_image : 7 + n_text + n_image
    ]
    (
        s_ref,
        t_ref,
        text_out,
        image_out,
        text_frozen,
        image_frozen,
        s_high,
        s_sum,
        t_high,
        t_sum,
        sems,
        out_sems,
    ) = refs[7 + n_text + n_image :]
    copies = []
    k = 0
    for group, out, frozen in (
        (text_refs, text_out, text_frozen),
        (image_refs, image_out, image_frozen),
    ):
        for ref in group:
            for b in range(ref.shape[0] // BLOCK):
                at = pl.multiple_of(place_ref[k] * BLOCK, BLOCK)
                for half, target in ((0, out), (1, frozen)):
                    copies.append(
                        pltpu.make_async_copy(
                            ref.at[pl.ds(b * BLOCK, BLOCK), pl.ds(half * WIDTH, WIDTH)],
                            target.at[pl.ds(at, BLOCK), :],
                            sems.at[2 * k + half],
                        )
                    )
                k += 1
    for half in (0, 1):
        for copy in copies[half::2]:
            copy.start()
    outward = [
        pltpu.make_async_copy(text_out, text_hbm, out_sems.at[2]),
        pltpu.make_async_copy(image_out, image_hbm, out_sems.at[3]),
        pltpu.make_async_copy(s_ref, s_hbm, out_sems.at[0]),
        pltpu.make_async_copy(t_ref, t_hbm, out_sems.at[1]),
    ]

    for which, left, right, out in (
        (0, image_out, text_out, s_ref),
        (1, image_frozen, text_frozen, t_ref),
    ):
        for copy in copies[which::2]:
            copy.wait()

        @pl.loop(0, SIDE // CHUNK)
        def _(j):
            cols = pl.ds(pl.multiple_of(j * CHUNK, CHUNK), CHUNK)
            tile = (SCALE * LOG2E) * lax.dot_general(
                left[...],
                right[cols, :],
                (((1,), (1,)), ((), ())),
                preferred_element_type=jnp.float32,
            )
            out[:, cols] = tile
            tile = tile.reshape(SIDE // 8, 8, CHUNK)
            high = jnp.max(tile, axis=0)
            total = jnp.sum(jnp.exp2(tile - high), axis=0)
            top = jnp.max(high, axis=0, keepdims=True)
            total = jnp.sum(total * jnp.exp2(high - top), axis=0, keepdims=True)
            lse = top + jnp.log2(total)
            for n in range(GROUP):
                col_ref[n, which : which + 1, cols] = lse

        for copy in outward[:3] if which == 0 else outward[3:]:
            copy.start()

    @pl.loop(0, SIDE // 64)
    def _(i):
        for g in range(8):
            rows = pl.ds(pl.multiple_of(i * 64 + g * 8, 8), 8)
            for ref, high_ref, sum_ref in ((s_ref, s_high, s_sum), (t_ref, t_high, t_sum)):
                tiles = [ref[rows, pl.ds(k * 128, 128)] for k in range(SIDE // 128)]
                high = functools.reduce(jnp.maximum, tiles)
                high_ref[rows, :] = high
                sum_ref[rows, :] = functools.reduce(jnp.add, [jnp.exp2(v - high) for v in tiles])

    @pl.loop(0, SIDE // 128)
    def _(i):
        rows = pl.ds(pl.multiple_of(i * 128, 128), 128)
        for which, high_ref, sum_ref in ((0, s_high, s_sum), (1, t_high, t_sum)):
            high = jnp.transpose(high_ref[rows, :])
            total = jnp.transpose(sum_ref[rows, :])
            top = jnp.max(high, axis=0, keepdims=True)
            total = jnp.sum(total * jnp.exp2(high - top), axis=0, keepdims=True)
            lse = top + jnp.log2(total)
            for n in range(GROUP):
                row_ref[n, which : which + 1, rows] = lse

    for slab, ref in ((text_out, row_ref), (image_out, col_ref)):
        largest = jnp.max(jnp.abs(slab[...]), axis=0, keepdims=True).astype(jnp.float32)
        largest = jnp.full((2, 128), jnp.max(largest), jnp.float32)
        for n in range(GROUP):
            ref[n, :, SIDE : SIDE + 128] = largest
    for copy in outward:
        copy.wait()


def logits_and_statistics(places_in, text, images):
    f32 = jnp.float32
    anywhere = pl.BlockSpec(memory_space=pl.ANY)
    vmem = pl.BlockSpec(memory_space=pltpu.VMEM)
    smem = pl.BlockSpec(memory_space=pltpu.SMEM)
    hbm = pl.BlockSpec(memory_space=pltpu.HBM)

    def kernel(*refs):
        logits_kernel((len(text), len(images)), *refs)

    square = pltpu.HBM((SIDE, SIDE), f32)
    half = jax.ShapeDtypeStruct((SIDE, WIDTH), jnp.bfloat16)
    small = jax.ShapeDtypeStruct((GROUP, 2, SIDE + 128), f32)
    return pl.pallas_call(
        kernel,
        out_shape=(square, square, half, half, small, small),
        in_specs=[smem] + [anywhere] * (len(text) + len(images)),
        out_specs=(hbm,) * 4 + (vmem,) * 2,
        scratch_shapes=[
            pltpu.VMEM((SIDE, SIDE), f32),
            pltpu.VMEM((SIDE, SIDE), f32),
            pltpu.VMEM((SIDE, WIDTH), jnp.bfloat16),
            pltpu.VMEM((SIDE, WIDTH), jnp.bfloat16),
            pltpu.VMEM((SIDE, WIDTH), jnp.bfloat16),
            pltpu.VMEM((SIDE, WIDTH), jnp.bfloat16),
            pltpu.VMEM((SIDE, 128), f32),
            pltpu.VMEM((SIDE, 128), f32),
            pltpu.VMEM((SIDE, 128), f32),
            pltpu.VMEM((SIDE, 128), f32),
            pltpu.SemaphoreType.DMA((64,)),
            pltpu.SemaphoreType.DMA((4,)),
        ],
        compiler_params=pltpu.CompilerParams(vmem_limit_bytes=LOGITS_VMEM),
        cost_estimate=pl.CostEstimate(
            flops=4 * SIDE * SIDE * WIDTH, bytes_accessed=20 << 20, transcendentals=4 * SIDE * SIDE
        ),
    )(places_in, *text, *images)


def gradient_kernel(
    s_ref,
    t_ref,
    row_ref,
    col_ref,
    row_id_ref,
    col_id_ref,
    out_ref,
    factor_ref,
    part_ref,
    lse_ref,
    total_ref,
):
    step = pl.program_id(0)
    size = 16

    def joined(ref, which):
        values = ref[:, which, :SIDE]
        top = jnp.max(values, axis=0, keepdims=True)
        return top + jnp.log2(jnp.sum(jnp.exp2(values - top), axis=0, keepdims=True))

    @pl.when(step == 0)
    def _():
        s_row_all, t_row_all = joined(row_ref, 0), joined(row_ref, 1)
        s_col_all, t_col_all = joined(col_ref, 0), joined(col_ref, 1)
        shared = (s_row_all - 0.5 * t_row_all) + (s_col_all - 0.5 * t_col_all)
        lse_ref[0:1, :] = s_row_all
        lse_ref[1:2, :] = t_row_all + 1.0
        lse_ref[2:3, :] = s_col_all
        lse_ref[3:4, :] = t_col_all + 1.0
        lse_ref[4:5, :] = shared
        for k, ref in ((0, row_ref), (1, col_ref)):
            scale = 2.0 / jnp.maximum(jnp.max(ref[:, 0, SIDE : SIDE + 128]), 1e-30)
            scale = jnp.full((1, SIDE), scale, jnp.float32)
            factor_ref[k : k + 1, :] = scale
            factor_ref[k + 2 : k + 3, :] = SCALE / scale
        factor_ref[4:8, :] = jnp.zeros((4, SIDE), jnp.float32)
        total_ref[...] = jnp.zeros((size, 128), jnp.float32)

    def strip(i, total):
        base = pl.multiple_of(i * STRIP, STRIP)
        at = pl.multiple_of(step * ROWS + base, STRIP)
        turned = jnp.transpose(lse_ref[:, pl.ds(at, STRIP)])
        for g in range(STRIP // size):
            rows = pl.ds(pl.multiple_of(base + g * size, size), size)
            s_row = jnp.broadcast_to(turned[g * size : (g + 1) * size, 0:1], (size, 128))
            t_row = jnp.broadcast_to(turned[g * size : (g + 1) * size, 1:2], (size, 128))
            row_id = jnp.broadcast_to(row_id_ref[rows, :], (size, 128))
            for k in range(SIDE // 128):
                lanes = pl.ds(k * 128, 128)
                s = s_ref[rows, lanes]
                t = t_ref[rows, lanes]
                weights = jnp.exp2(t - t_row) + jnp.exp2(t - lse_ref[3:4, lanes])
                value = (jnp.exp2(s - s_row) + jnp.exp2(s - lse_ref[2:3, lanes])) - weights
                same = row_id == col_id_ref[:, lanes]
                out_ref[rows, lanes] = jnp.where(same, value - 1.0, value).astype(jnp.bfloat16)
                total = total + (weights * (t - s) - jnp.where(same, s, 0.0))
        return total

    total_ref[...] = lax.fori_loop(0, ROWS // STRIP, strip, total_ref[...])

    @pl.when(step == pl.num_programs(0) - 1)
    def _():
        part = jnp.sum(total_ref[...]) + jnp.sum(lse_ref[4:5, :]) * (1.0 / GROUP)
        part_ref[...] = jnp.full(part_ref.shape, LN2 * part, jnp.float32)


def gradient_of_logits(s, t, row, col, row_id, col_id):
    f32 = jnp.float32
    by_rows = pl.BlockSpec((ROWS, SIDE), lambda i: (i, 0))

    def whole(shape):
        return pl.BlockSpec(shape, lambda i: (0,) * len(shape))

    return pl.pallas_call(
        gradient_kernel,
        grid=(SIDE // ROWS,),
        out_shape=(
            jax.ShapeDtypeStruct((SIDE, SIDE), jnp.bfloat16),
            jax.ShapeDtypeStruct((8, SIDE), f32),
            jax.ShapeDtypeStruct((GROUP, 8, 128), f32),
        ),
        in_specs=[
            by_rows,
            by_rows,
            whole(row.shape),
            whole(col.shape),
            pl.BlockSpec((ROWS, 1), lambda i: (i, 0)),
            whole(col_id.shape),
        ],
        out_specs=(by_rows, whole((8, SIDE)), whole((GROUP, 8, 128))),
        scratch_shapes=[pltpu.VMEM((8, SIDE), f32), pltpu.VMEM((16, 128), f32)],
        compiler_params=pltpu.CompilerParams(vmem_limit_bytes=GRADIENT_VMEM),
        cost_estimate=pl.CostEstimate(
            flops=16 * SIDE * SIDE, bytes_accessed=10 << 20, transcendentals=4 * SIDE * SIDE
        ),
    )(*(pltpu.with_memory_space_constraint(v, pltpu.HBM) for v in (s, t)), row, col, row_id, col_id)


def exchanged(copies, axis):
    return lax.all_to_all(copies, axis, split_axis=0, concat_axis=0, tiled=True)


def body(image_student, text_student, image_teacher, text_teacher):
    y, zl, x, zh, c = (lax.axis_index(n) for n in NAMES)
    z = zh * 2 + zl
    text_pieces, image_pieces = gathered(
        *joined_halves(text_student, text_teacher, image_student, image_teacher)
    )

    sign = 1 - 2 * c
    at = []
    for _, offsets in text_pieces:
        for du, dv in offsets:
            dx = jnp.where(c == 0, du, dv)
            dy = jnp.where(c == 0, dv, du)
            at.append(((y + dy) % 4) * 4 + (x + dx) % 4)
    for _, offsets in image_pieces:
        for swapped, step in offsets:
            at.append((c ^ swapped) * 8 + (z + sign * step) % 8)
    where = jnp.stack(at).astype(jnp.int32)

    numbers = jnp.arange(SIDE, dtype=jnp.int32)
    slot, inner = numbers // BLOCK, numbers % BLOCK
    text_y, text_x = slot // 4, slot % 4
    col_id = (((text_x * 8 + zh * 2 + c) * 8) + text_y * 2 + zl) * BLOCK + inner
    image_c, image_z = slot // 8, slot % 8
    row_id = ((y * 2 + image_z % 2) * 32 + x * 8 + (image_z // 2) * 2 + image_c) * BLOCK + inner
    row_id, col_id = row_id[:, None], col_id[None, :]

    s, t, text_slab, image_slab, row_part, col_part = logits_and_statistics(
        where, [p for p, _ in text_pieces], [p for p, _ in image_pieces]
    )
    col_all = exchanged(col_part, TEXT_GROUP)
    row_all = exchanged(row_part, IMAGE_GROUP)
    gradient, factors, part = gradient_of_logits(s, t, row_all, col_all, row_id, col_id)
    text_scale, image_scale = factors[0:1], factors[1:2]
    image_factor, text_factor = factors[2:3], factors[3:4]

    tie = lax.optimization_barrier
    value = jnp.sum(exchanged(part, TEXT_GROUP), axis=0)
    text_part = (
        lax.dot_general(
            gradient, image_slab, (((0,), (0,)), ((), ())), preferred_element_type=jnp.float32
        )
        * image_scale
    ).astype(jnp.float16)
    text_part, gradient, value = tie((text_part, gradient, value))
    text_blocks = lax.all_to_all(text_part.reshape(16, BLOCK, WIDTH), TEXT_GROUP, 0, 0, tiled=True)

    half = SIDE // 2
    theirs = lax.dynamic_slice_in_dim(gradient, (1 - c) * half, half)
    mine = lax.dynamic_slice_in_dim(gradient, c * half, half)
    image_theirs = jnp.dot(theirs, text_slab, preferred_element_type=jnp.float32)
    arrived = moved((image_theirs * text_scale).astype(jnp.float16), other_core)
    image_mine = (
        jnp.dot(mine, text_slab, preferred_element_type=jnp.float32) * text_scale
    ) + arrived.astype(jnp.float32)
    blocks = image_mine.astype(jnp.float16).reshape(8, BLOCK, WIDTH)

    def block(step):
        return lax.dynamic_index_in_dim(blocks, (z + sign * step) % 8, 0, keepdims=False).astype(
            jnp.float32
        )

    def narrow(v):
        return v.astype(jnp.float16)

    down = moved(narrow(block(4)), along_z(-1)).astype(jnp.float32)
    copies = jnp.broadcast_to(value, (GROUP, 8, 128))
    value = jnp.sum(exchanged(copies, IMAGE_GROUP), axis=0)
    up = None
    for k in (3, 2, 1):
        first = narrow(block(-k) + down)
        second = narrow(block(k) if up is None else block(k) + up)
        down = moved(first, along_z(-1)).astype(jnp.float32)
        up = moved(second, along_z(1)).astype(jnp.float32)
    loss = value[0, 0] / (256 * BLOCK)
    image_grad = (block(0) + down + up) * image_factor
    text_grad = jnp.sum(text_blocks.astype(jnp.float32), axis=0) * text_factor
    return (loss, image_grad, text_grad)


def solution(mesh):
    finer = Mesh(mesh.devices.reshape(SIZES), NAMES)
    placed = (P(ROW_COL, None), P(COL_ROW, None), P(ROW_COL, None), P(COL_ROW, None))
    return jax.shard_map(
        body,
        mesh=finer,
        in_specs=placed,
        out_specs=(P(), P(ROW_COL, None), P(COL_ROW, None)),
        check_vma=False,
    )
```

```python
import functools
import itertools
import math

import jax
import jax.numpy as jnp
from jax import lax
from jax.experimental import pallas as pl
from jax.experimental.pallas import tpu as pltpu
from jax.sharding import Mesh
from jax.sharding import PartitionSpec as P

NAMES = ("y", "zl", "x", "zh", "c")
SIZES = (4, 2, 4, 4, 2)
ROW_COL = ("y", "zl", "x", "zh", "c")
COL_ROW = ("x", "zh", "c", "y", "zl")
TEXT_GROUP = ("y", "x")
IMAGE_GROUP = ("zl", "zh", "c")

LOG2E = math.log2(math.e)
LN2 = math.log(2.0)
SCALE = 100.0
BLOCK = 64
WIDTH = 1024
SIDE = 1024
STRIP = 128
CHUNK = 256
GROUP = 16
LOGITS_VMEM = 58 * 1024 * 1024
GRADIENT_VMEM = 20 * 1024 * 1024
ROWS = 256


def places():
    return list(itertools.product(*(range(n) for n in SIZES)))


def index_of(place):
    at = 0
    for value, size in zip(place, SIZES):
        at = at * size + value % size
    return at


def shifted(place, axis, by):
    y, zl, x, zh, c = place
    if axis == "z":
        z = (zh * 2 + zl + by) % 8
        return (y, z % 2, x, z // 2, c)
    if axis == "x":
        return (y, zl, (x + by) % 4, zh, c)
    if axis == "y":
        return ((y + by) % 4, zl, x, zh, c)
    return (y, zl, x, zh, (c + by) % 2)


def moved(value, to):
    pairs = [(index_of(p), index_of(to(p))) for p in places()]
    return lax.ppermute(value, NAMES, pairs)


def along_u(by):
    return lambda p: shifted(p, "x" if p[4] == 0 else "y", by)


def along_v(by):
    return lambda p: shifted(p, "y" if p[4] == 0 else "x", by)


def along_z(by):
    return lambda p: shifted(p, "z", by if p[4] == 0 else -by)


def other_core(p):
    return shifted(p, "c", 1)


def joined_halves(*halves):
    def kernel(*refs):
        for k in range(4):
            refs[4 + k // 2][:, k % 2 * WIDTH : (k % 2 + 1) * WIDTH] = refs[k][...]

    vmem = pl.BlockSpec(memory_space=pltpu.VMEM)
    pair = jax.ShapeDtypeStruct((BLOCK, 2 * WIDTH), jnp.bfloat16)
    return pl.pallas_call(
        kernel,
        out_shape=(pair, pair),
        in_specs=[vmem] * 4,
        out_specs=(vmem,) * 2,
        cost_estimate=pl.CostEstimate(flops=0, bytes_accessed=1 << 20, transcendentals=0),
    )(*halves)


def gathered(text, image):
    tie = lax.optimization_barrier
    back, ahead = moved(text, along_u(1)), moved(text, along_u(-1))
    far = moved(text, along_u(2))
    mine = [image, moved(image, along_z(1))]
    theirs = [moved(image, other_core)]
    back, ahead, far, mine[1], theirs[0] = tie((back, ahead, far, mine[1], theirs[0]))

    line = jnp.concatenate([text, back, ahead, far], axis=0)
    line, mine[1], theirs[0] = tie((line, mine[1], theirs[0]))
    line_back, line_ahead = moved(line, along_v(1)), moved(line, along_v(-1))
    mine.append(moved(mine[1], along_z(1)))
    theirs.append(moved(theirs[0], along_z(1)))
    mine[2], theirs[1] = tie((mine[2], theirs[1]))
    mine.append(moved(mine[2], along_z(1)))
    theirs.append(moved(theirs[1], along_z(1)))
    line_back, line_ahead, mine[3], theirs[2] = tie((line_back, line_ahead, mine[3], theirs[2]))

    first_far = moved(line_back[:128], along_v(1))
    second_far = moved(line_ahead[128:], along_v(-1))
    mine.append(moved(mine[3], along_z(1)))
    theirs.append(moved(theirs[2], along_z(1)))
    early = jnp.concatenate([mine[1], mine[2], mine[3], theirs[1], theirs[2]], axis=0)
    early_other = moved(early, other_core)
    mine[4], theirs[3] = tie((mine[4], theirs[3]))
    late = jnp.concatenate([mine[4], theirs[3]], axis=0)
    late_other = moved(late, other_core)
    us = (0, -1, 1, 2)
    return [
        (line, [(du, 0) for du in us]),
        (line_back, [(du, -1) for du in us]),
        (line_ahead, [(du, 1) for du in us]),
        (first_far, ((0, 2), (-1, 2))),
        (second_far, ((1, 2), (2, 2))),
    ], [
        (image, ((0, 0),)),
        (theirs[0], ((1, 0),)),
        (early, ((0, -1), (0, -2), (0, -3), (1, -1), (1, -2))),
        (early_other, ((1, 1), (1, 2), (1, 3), (0, 1), (0, 2))),
        (late, ((0, 4), (1, -3))),
        (late_other, ((1, 4), (0, 3))),
    ]


def logits_kernel(counts, *refs):
    n_text, n_image = counts
    place_ref = refs[0]
    text_refs = refs[1 : 1 + n_text]
    image_refs = refs[1 + n_text : 1 + n_text + n_image]
    (s_hbm, t_hbm, text_hbm, image_hbm, row_ref, col_ref) = refs[
        1 + n_text + n_image : 7 + n_text + n_image
    ]
    (
        s_ref,
        t_ref,
        text_out,
        image_out,
        text_frozen,
        image_frozen,
        s_high,
        s_sum,
        t_high,
        t_sum,
        sems,
        out_sems,
    ) = refs[7 + n_text + n_image :]
    copies = []
    k = 0
    for group, out, frozen in (
        (text_refs, text_out, text_frozen),
        (image_refs, image_out, image_frozen),
    ):
        for ref in group:
            for b in range(ref.shape[0] // BLOCK):
                at = pl.multiple_of(place_ref[k] * BLOCK, BLOCK)
                for half, target in ((0, out), (1, frozen)):
                    copies.append(
                        pltpu.make_async_copy(
                            ref.at[pl.ds(b * BLOCK, BLOCK), pl.ds(half * WIDTH, WIDTH)],
                            target.at[pl.ds(at, BLOCK), :],
                            sems.at[2 * k + half],
                        )
                    )
                k += 1
    for half in (0, 1):
        for copy in copies[half::2]:
            copy.start()
    outward = [
        pltpu.make_async_copy(text_out, text_hbm, out_sems.at[2]),
        pltpu.make_async_copy(image_out, image_hbm, out_sems.at[3]),
        pltpu.make_async_copy(s_ref, s_hbm, out_sems.at[0]),
        pltpu.make_async_copy(t_ref, t_hbm, out_sems.at[1]),
    ]

    for which, left, right, out in (
        (0, image_out, text_out, s_ref),
        (1, image_frozen, text_frozen, t_ref),
    ):
        for copy in copies[which::2]:
            copy.wait()

        @pl.loop(0, SIDE // CHUNK)
        def _(j):
            cols = pl.ds(pl.multiple_of(j * CHUNK, CHUNK), CHUNK)
            tile = (SCALE * LOG2E) * lax.dot_general(
                left[...],
                right[cols, :],
                (((1,), (1,)), ((), ())),
                preferred_element_type=jnp.float32,
            )
            out[:, cols] = tile
            tile = tile.reshape(SIDE // 8, 8, CHUNK)
            high = jnp.max(tile, axis=0)
            total = jnp.sum(jnp.exp2(tile - high), axis=0)
            top = jnp.max(high, axis=0, keepdims=True)
            total = jnp.sum(total * jnp.exp2(high - top), axis=0, keepdims=True)
            lse = top + jnp.log2(total)
            for n in range(GROUP):
                col_ref[n, which : which + 1, cols] = lse

        for copy in outward[:3] if which == 0 else outward[3:]:
            copy.start()

    @pl.loop(0, SIDE // 64)
    def _(i):
        for g in range(8):
            rows = pl.ds(pl.multiple_of(i * 64 + g * 8, 8), 8)
            for ref, high_ref, sum_ref in ((s_ref, s_high, s_sum), (t_ref, t_high, t_sum)):
                tiles = [ref[rows, pl.ds(k * 128, 128)] for k in range(SIDE // 128)]
                high = functools.reduce(jnp.maximum, tiles)
                high_ref[rows, :] = high
                sum_ref[rows, :] = functools.reduce(jnp.add, [jnp.exp2(v - high) for v in tiles])

    @pl.loop(0, SIDE // 128)
    def _(i):
        rows = pl.ds(pl.multiple_of(i * 128, 128), 128)
        for which, high_ref, sum_ref in ((0, s_high, s_sum), (1, t_high, t_sum)):
            high = jnp.transpose(high_ref[rows, :])
            total = jnp.transpose(sum_ref[rows, :])
            top = jnp.max(high, axis=0, keepdims=True)
            total = jnp.sum(total * jnp.exp2(high - top), axis=0, keepdims=True)
            lse = top + jnp.log2(total)
            for n in range(GROUP):
                row_ref[n, which : which + 1, rows] = lse

    for slab, ref in ((text_out, row_ref), (image_out, col_ref)):
        largest = jnp.max(jnp.abs(slab[...]), axis=0, keepdims=True).astype(jnp.float32)
        largest = jnp.full((2, 128), jnp.max(largest), jnp.float32)
        for n in range(GROUP):
            ref[n, :, SIDE : SIDE + 128] = largest
    for copy in outward:
        copy.wait()


def logits_and_statistics(places_in, text, images):
    f32 = jnp.float32
    anywhere = pl.BlockSpec(memory_space=pl.ANY)
    vmem = pl.BlockSpec(memory_space=pltpu.VMEM)
    smem = pl.BlockSpec(memory_space=pltpu.SMEM)
    hbm = pl.BlockSpec(memory_space=pltpu.HBM)

    def kernel(*refs):
        logits_kernel((len(text), len(images)), *refs)

    square = pltpu.HBM((SIDE, SIDE), f32)
    half = jax.ShapeDtypeStruct((SIDE, WIDTH), jnp.bfloat16)
    small = jax.ShapeDtypeStruct((GROUP, 2, SIDE + 128), f32)
    return pl.pallas_call(
        kernel,
        out_shape=(square, square, half, half, small, small),
        in_specs=[smem] + [anywhere] * (len(text) + len(images)),
        out_specs=(hbm,) * 4 + (vmem,) * 2,
        scratch_shapes=[
            pltpu.VMEM((SIDE, SIDE), f32),
            pltpu.VMEM((SIDE, SIDE), f32),
            pltpu.VMEM((SIDE, WIDTH), jnp.bfloat16),
            pltpu.VMEM((SIDE, WIDTH), jnp.bfloat16),
            pltpu.VMEM((SIDE, WIDTH), jnp.bfloat16),
            pltpu.VMEM((SIDE, WIDTH), jnp.bfloat16),
            pltpu.VMEM((SIDE, 128), f32),
            pltpu.VMEM((SIDE, 128), f32),
            pltpu.VMEM((SIDE, 128), f32),
            pltpu.VMEM((SIDE, 128), f32),
            pltpu.SemaphoreType.DMA((64,)),
            pltpu.SemaphoreType.DMA((4,)),
        ],
        compiler_params=pltpu.CompilerParams(vmem_limit_bytes=LOGITS_VMEM),
        cost_estimate=pl.CostEstimate(
            flops=4 * SIDE * SIDE * WIDTH, bytes_accessed=20 << 20, transcendentals=4 * SIDE * SIDE
        ),
    )(places_in, *text, *images)


def gradient_kernel(
    s_ref,
    t_ref,
    row_ref,
    col_ref,
    row_id_ref,
    col_id_ref,
    out_ref,
    factor_ref,
    part_ref,
    lse_ref,
    total_ref,
):
    step = pl.program_id(0)
    size = 16

    def joined(ref, which):
        values = ref[:, which, :SIDE]
        top = jnp.max(values, axis=0, keepdims=True)
        return top + jnp.log2(jnp.sum(jnp.exp2(values - top), axis=0, keepdims=True))

    @pl.when(step == 0)
    def _():
        s_row_all, t_row_all = joined(row_ref, 0), joined(row_ref, 1)
        s_col_all, t_col_all = joined(col_ref, 0), joined(col_ref, 1)
        shared = (s_row_all - 0.5 * t_row_all) + (s_col_all - 0.5 * t_col_all)
        lse_ref[0:1, :] = s_row_all
        lse_ref[1:2, :] = t_row_all + 1.0
        lse_ref[2:3, :] = s_col_all
        lse_ref[3:4, :] = t_col_all + 1.0
        lse_ref[4:5, :] = shared
        for k, ref in ((0, row_ref), (1, col_ref)):
            scale = 2.0 / jnp.maximum(jnp.max(ref[:, 0, SIDE : SIDE + 128]), 1e-30)
            scale = jnp.full((1, SIDE), scale, jnp.float32)
            factor_ref[k : k + 1, :] = scale
            factor_ref[k + 2 : k + 3, :] = SCALE / scale
        factor_ref[4:8, :] = jnp.zeros((4, SIDE), jnp.float32)
        total_ref[...] = jnp.zeros((size, 128), jnp.float32)

    def strip(i, total):
        base = pl.multiple_of(i * STRIP, STRIP)
        at = pl.multiple_of(step * ROWS + base, STRIP)
        turned = jnp.transpose(lse_ref[:, pl.ds(at, STRIP)])
        for g in range(STRIP // size):
            rows = pl.ds(pl.multiple_of(base + g * size, size), size)
            s_row = jnp.broadcast_to(turned[g * size : (g + 1) * size, 0:1], (size, 128))
            t_row = jnp.broadcast_to(turned[g * size : (g + 1) * size, 1:2], (size, 128))
            row_id = jnp.broadcast_to(row_id_ref[rows, :], (size, 128))
            for k in range(SIDE // 128):
                lanes = pl.ds(k * 128, 128)
                s = s_ref[rows, lanes]
                t = t_ref[rows, lanes]
                weights = jnp.exp2(t - t_row) + jnp.exp2(t - lse_ref[3:4, lanes])
                value = (jnp.exp2(s - s_row) + jnp.exp2(s - lse_ref[2:3, lanes])) - weights
                same = row_id == col_id_ref[:, lanes]
                out_ref[rows, lanes] = jnp.where(same, value - 1.0, value).astype(jnp.bfloat16)
                total = total + (weights * (t - s) - jnp.where(same, s, 0.0))
        return total

    total_ref[...] = lax.fori_loop(0, ROWS // STRIP, strip, total_ref[...])

    @pl.when(step == pl.num_programs(0) - 1)
    def _():
        part = jnp.sum(total_ref[...]) + jnp.sum(lse_ref[4:5, :]) * (1.0 / GROUP)
        part_ref[...] = jnp.full(part_ref.shape, LN2 * part, jnp.float32)


def gradient_of_logits(s, t, row, col, row_id, col_id):
    f32 = jnp.float32
    by_rows = pl.BlockSpec((ROWS, SIDE), lambda i: (i, 0))

    def whole(shape):
        return pl.BlockSpec(shape, lambda i: (0,) * len(shape))

    return pl.pallas_call(
        gradient_kernel,
        grid=(SIDE // ROWS,),
        out_shape=(
            jax.ShapeDtypeStruct((SIDE, SIDE), jnp.bfloat16),
            jax.ShapeDtypeStruct((8, SIDE), f32),
            jax.ShapeDtypeStruct((GROUP, 8, 128), f32),
        ),
        in_specs=[
            by_rows,
            by_rows,
            whole(row.shape),
            whole(col.shape),
            pl.BlockSpec((ROWS, 1), lambda i: (i, 0)),
            whole(col_id.shape),
        ],
        out_specs=(by_rows, whole((8, SIDE)), whole((GROUP, 8, 128))),
        scratch_shapes=[pltpu.VMEM((8, SIDE), f32), pltpu.VMEM((16, 128), f32)],
        compiler_params=pltpu.CompilerParams(vmem_limit_bytes=GRADIENT_VMEM),
        cost_estimate=pl.CostEstimate(
            flops=16 * SIDE * SIDE, bytes_accessed=10 << 20, transcendentals=4 * SIDE * SIDE
        ),
    )(
        *(pltpu.with_memory_space_constraint(v, pltpu.HBM) for v in (s, t)),
        row,
        col,
        row_id,
        col_id,
    )


def exchanged(copies, axis):
    return lax.all_to_all(copies, axis, split_axis=0, concat_axis=0, tiled=True)


def body(image_student, text_student, image_teacher, text_teacher):
    y, zl, x, zh, c = (lax.axis_index(n) for n in NAMES)
    z = zh * 2 + zl
    text_pieces, image_pieces = gathered(
        *joined_halves(text_student, text_teacher, image_student, image_teacher)
    )

    sign = 1 - 2 * c
    at = []
    for _, offsets in text_pieces:
        for du, dv in offsets:
            dx = jnp.where(c == 0, du, dv)
            dy = jnp.where(c == 0, dv, du)
            at.append(((y + dy) % 4) * 4 + (x + dx) % 4)
    for _, offsets in image_pieces:
        for swapped, step in offsets:
            at.append((c ^ swapped) * 8 + (z + sign * step) % 8)
    where = jnp.stack(at).astype(jnp.int32)

    numbers = jnp.arange(SIDE, dtype=jnp.int32)
    slot, inner = numbers // BLOCK, numbers % BLOCK
    text_y, text_x = slot // 4, slot % 4
    col_id = (((text_x * 8 + zh * 2 + c) * 8) + text_y * 2 + zl) * BLOCK + inner
    image_c, image_z = slot // 8, slot % 8
    row_id = ((y * 2 + image_z % 2) * 32 + x * 8 + (image_z // 2) * 2 + image_c) * BLOCK + inner
    row_id, col_id = row_id[:, None], col_id[None, :]

    s, t, text_slab, image_slab, row_part, col_part = logits_and_statistics(
        where, [p for p, _ in text_pieces], [p for p, _ in image_pieces]
    )
    col_all = exchanged(col_part, TEXT_GROUP)
    row_all = exchanged(row_part, IMAGE_GROUP)
    gradient, factors, part = gradient_of_logits(s, t, row_all, col_all, row_id, col_id)
    text_scale, image_scale = factors[0:1], factors[1:2]
    image_factor, text_factor = factors[2:3], factors[3:4]

    half = SIDE // 2
    theirs = lax.dynamic_slice_in_dim(gradient, (1 - c) * half, half)
    mine = lax.dynamic_slice_in_dim(gradient, c * half, half)
    image_theirs = jnp.dot(theirs, text_slab, preferred_element_type=jnp.float32)
    arrived = moved((image_theirs * text_scale).astype(jnp.float16), other_core)
    image_mine = (
        jnp.dot(mine, text_slab, preferred_element_type=jnp.float32) * text_scale
    ) + arrived.astype(jnp.float32)
    blocks = image_mine.astype(jnp.float16).reshape(8, BLOCK, WIDTH)

    def block(step):
        return lax.dynamic_index_in_dim(blocks, (z + sign * step) % 8, 0, keepdims=False).astype(
            jnp.float32
        )

    def narrow(v):
        return v.astype(jnp.float16)

    tie = lax.optimization_barrier
    steps = [lambda p, k=k: flipped(p, k) for k in (4, 2, 1)] + [other_core]
    start, gradient, part = tie((narrow(block(4)), gradient, part))
    down = moved(start, along_z(-1))
    value = jnp.sum(exchanged(part, TEXT_GROUP), axis=0)
    text_part = (
        lax.dot_general(
            gradient, image_slab, (((0,), (0,)), ((), ())), preferred_element_type=jnp.float32
        )
        * image_scale
    ).astype(jnp.float16)
    down, value, text_part = tie((down, value, text_part))
    text_blocks = lax.all_to_all(text_part.reshape(16, BLOCK, WIDTH), TEXT_GROUP, 0, 0, tiled=True)
    down = down.astype(jnp.float32)
    value = value + moved(value, steps[0])
    up = None
    for k in (3, 2, 1):
        first = narrow(block(-k) + down)
        second = narrow(block(k) if up is None else block(k) + up)
        if k < 3:
            first, second, value = tie((first, second, value))
        down = moved(first, along_z(-1)).astype(jnp.float32)
        up = moved(second, along_z(1)).astype(jnp.float32)
        if k < 3:
            value = value + moved(value, steps[3 - k])
    value = value + moved(value, steps[3])
    loss = value[0, 0] / (256 * BLOCK)
    image_grad = (block(0) + down + up) * image_factor
    text_grad = jnp.sum(text_blocks.astype(jnp.float32), axis=0) * text_factor
    return (loss, image_grad, text_grad)


def flipped(p, bit):
    y, zl, x, zh, c = p
    z = (zh * 2 + zl) ^ bit
    return (y, z % 2, x, z // 2, c)


def solution(mesh):
    finer = Mesh(mesh.devices.reshape(SIZES), NAMES)
    placed = (P(ROW_COL, None), P(COL_ROW, None), P(ROW_COL, None), P(COL_ROW, None))
    return jax.shard_map(
        body,
        mesh=finer,
        in_specs=placed,
        out_specs=(P(), P(ROW_COL, None), P(COL_ROW, None)),
        check_vma=False,
    )
```

```python
import functools
import itertools
import math

import jax
import jax.numpy as jnp
from jax import lax
from jax.experimental import pallas as pl
from jax.experimental.pallas import tpu as pltpu
from jax.sharding import Mesh
from jax.sharding import PartitionSpec as P

NAMES = ("y", "zl", "x", "zh", "c")
SIZES = (4, 2, 4, 4, 2)
ROW_COL = ("y", "zl", "x", "zh", "c")
COL_ROW = ("x", "zh", "c", "y", "zl")
TEXT_GROUP = ("y", "x")
IMAGE_GROUP = ("zl", "zh", "c")

LOG2E = math.log2(math.e)
LN2 = math.log(2.0)
SCALE = 100.0
BLOCK = 64
WIDTH = 1024
SIDE = 1024
STRIP = 128
CHUNK = 256
GROUP = 16
LOGITS_VMEM = 58 * 1024 * 1024
GRADIENT_VMEM = 20 * 1024 * 1024
ROWS = 256


def places():
    return list(itertools.product(*(range(n) for n in SIZES)))


def index_of(place):
    at = 0
    for value, size in zip(place, SIZES):
        at = at * size + value % size
    return at


def shifted(place, axis, by):
    y, zl, x, zh, c = place
    if axis == "z":
        z = (zh * 2 + zl + by) % 8
        return (y, z % 2, x, z // 2, c)
    if axis == "x":
        return (y, zl, (x + by) % 4, zh, c)
    if axis == "y":
        return ((y + by) % 4, zl, x, zh, c)
    return (y, zl, x, zh, (c + by) % 2)


def moved(value, to):
    pairs = [(index_of(p), index_of(to(p))) for p in places()]
    return lax.ppermute(value, NAMES, pairs)


def along_u(by):
    return lambda p: shifted(p, "x" if p[4] == 0 else "y", by)


def along_v(by):
    return lambda p: shifted(p, "y" if p[4] == 0 else "x", by)


def along_z(by):
    return lambda p: shifted(p, "z", by if p[4] == 0 else -by)


def other_core(p):
    return shifted(p, "c", 1)


def joined_halves(*halves):
    def kernel(*refs):
        for k in range(4):
            refs[4 + k // 2][:, k % 2 * WIDTH : (k % 2 + 1) * WIDTH] = refs[k][...]

    vmem = pl.BlockSpec(memory_space=pltpu.VMEM)
    pair = jax.ShapeDtypeStruct((BLOCK, 2 * WIDTH), jnp.bfloat16)
    return pl.pallas_call(
        kernel,
        out_shape=(pair, pair),
        in_specs=[vmem] * 4,
        out_specs=(vmem,) * 2,
        cost_estimate=pl.CostEstimate(flops=0, bytes_accessed=1 << 20, transcendentals=0),
    )(*halves)


def gathered(text, image):
    tie = lax.optimization_barrier
    back, ahead = moved(text, along_u(1)), moved(text, along_u(-1))
    far = moved(text, along_u(2))
    mine = [image, moved(image, along_z(1))]
    theirs = [moved(image, other_core)]
    back, ahead, far, mine[1], theirs[0] = tie((back, ahead, far, mine[1], theirs[0]))

    line = jnp.concatenate([text, back, ahead, far], axis=0)
    line, mine[1], theirs[0] = tie((line, mine[1], theirs[0]))
    line_back, line_ahead = moved(line, along_v(1)), moved(line, along_v(-1))
    mine.append(moved(mine[1], along_z(1)))
    theirs.append(moved(theirs[0], along_z(1)))
    mine[2], theirs[1] = tie((mine[2], theirs[1]))
    mine.append(moved(mine[2], along_z(1)))
    theirs.append(moved(theirs[1], along_z(1)))
    line_back, line_ahead, mine[3], theirs[2] = tie((line_back, line_ahead, mine[3], theirs[2]))

    first_far = moved(line_back[:128], along_v(1))
    second_far = moved(line_ahead[128:], along_v(-1))
    mine.append(moved(mine[3], along_z(1)))
    theirs.append(moved(theirs[2], along_z(1)))
    early = jnp.concatenate([mine[1], mine[2], mine[3], theirs[1], theirs[2]], axis=0)
    early_other = moved(early, other_core)
    mine[4], theirs[3] = tie((mine[4], theirs[3]))
    late = jnp.concatenate([mine[4], theirs[3]], axis=0)
    late_other = moved(late, other_core)
    us = (0, -1, 1, 2)
    return [
        (line, [(du, 0) for du in us]),
        (line_back, [(du, -1) for du in us]),
        (line_ahead, [(du, 1) for du in us]),
        (first_far, ((0, 2), (-1, 2))),
        (second_far, ((1, 2), (2, 2))),
    ], [
        (image, ((0, 0),)),
        (theirs[0], ((1, 0),)),
        (early, ((0, -1), (0, -2), (0, -3), (1, -1), (1, -2))),
        (early_other, ((1, 1), (1, 2), (1, 3), (0, 1), (0, 2))),
        (late, ((0, 4), (1, -3))),
        (late_other, ((1, 4), (0, 3))),
    ]


def logits_kernel(counts, *refs):
    n_text, n_image = counts
    place_ref = refs[0]
    text_refs = refs[1 : 1 + n_text]
    image_refs = refs[1 + n_text : 1 + n_text + n_image]
    (s_hbm, t_hbm, text_hbm, image_hbm, row_ref, col_ref) = refs[
        1 + n_text + n_image : 7 + n_text + n_image
    ]
    (
        s_ref,
        t_ref,
        text_out,
        image_out,
        text_frozen,
        image_frozen,
        s_high,
        s_sum,
        t_high,
        t_sum,
        sems,
        out_sems,
    ) = refs[7 + n_text + n_image :]
    copies = []
    k = 0
    for group, out, frozen in (
        (text_refs, text_out, text_frozen),
        (image_refs, image_out, image_frozen),
    ):
        for ref in group:
            for b in range(ref.shape[0] // BLOCK):
                at = pl.multiple_of(place_ref[k] * BLOCK, BLOCK)
                for half, target in ((0, out), (1, frozen)):
                    copies.append(
                        pltpu.make_async_copy(
                            ref.at[pl.ds(b * BLOCK, BLOCK), pl.ds(half * WIDTH, WIDTH)],
                            target.at[pl.ds(at, BLOCK), :],
                            sems.at[2 * k + half],
                        )
                    )
                k += 1
    for half in (0, 1):
        for copy in copies[half::2]:
            copy.start()
    outward = [
        pltpu.make_async_copy(text_out, text_hbm, out_sems.at[2]),
        pltpu.make_async_copy(image_out, image_hbm, out_sems.at[3]),
        pltpu.make_async_copy(s_ref, s_hbm, out_sems.at[0]),
        pltpu.make_async_copy(t_ref, t_hbm, out_sems.at[1]),
    ]

    for which, left, right, out in (
        (0, image_out, text_out, s_ref),
        (1, image_frozen, text_frozen, t_ref),
    ):
        for copy in copies[which::2]:
            copy.wait()

        @pl.loop(0, SIDE // CHUNK)
        def _(j):
            cols = pl.ds(pl.multiple_of(j * CHUNK, CHUNK), CHUNK)
            tile = (SCALE * LOG2E) * lax.dot_general(
                left[...],
                right[cols, :],
                (((1,), (1,)), ((), ())),
                preferred_element_type=jnp.float32,
            )
            out[:, cols] = tile
            tile = tile.reshape(SIDE // 8, 8, CHUNK)
            high = jnp.max(tile, axis=0)
            total = jnp.sum(jnp.exp2(tile - high), axis=0)
            top = jnp.max(high, axis=0, keepdims=True)
            total = jnp.sum(total * jnp.exp2(high - top), axis=0, keepdims=True)
            lse = top + jnp.log2(total)
            for n in range(GROUP):
                col_ref[n, which : which + 1, cols] = lse

        for copy in outward[:3] if which == 0 else outward[3:]:
            copy.start()

    @pl.loop(0, SIDE // 64)
    def _(i):
        for g in range(8):
            rows = pl.ds(pl.multiple_of(i * 64 + g * 8, 8), 8)
            for ref, high_ref, sum_ref in ((s_ref, s_high, s_sum), (t_ref, t_high, t_sum)):
                tiles = [ref[rows, pl.ds(k * 128, 128)] for k in range(SIDE // 128)]
                high = functools.reduce(jnp.maximum, tiles)
                high_ref[rows, :] = high
                sum_ref[rows, :] = functools.reduce(jnp.add, [jnp.exp2(v - high) for v in tiles])

    @pl.loop(0, SIDE // 128)
    def _(i):
        rows = pl.ds(pl.multiple_of(i * 128, 128), 128)
        for which, high_ref, sum_ref in ((0, s_high, s_sum), (1, t_high, t_sum)):
            high = jnp.transpose(high_ref[rows, :])
            total = jnp.transpose(sum_ref[rows, :])
            top = jnp.max(high, axis=0, keepdims=True)
            total = jnp.sum(total * jnp.exp2(high - top), axis=0, keepdims=True)
            lse = top + jnp.log2(total)
            for n in range(GROUP):
                row_ref[n, which : which + 1, rows] = lse

    for slab, ref in ((text_out, row_ref), (image_out, col_ref)):
        largest = jnp.max(jnp.abs(slab[...]), axis=0, keepdims=True).astype(jnp.float32)
        largest = jnp.full((2, 128), jnp.max(largest), jnp.float32)
        for n in range(GROUP):
            ref[n, :, SIDE : SIDE + 128] = largest
    for copy in outward:
        copy.wait()


def logits_and_statistics(places_in, text, images):
    f32 = jnp.float32
    anywhere = pl.BlockSpec(memory_space=pl.ANY)
    vmem = pl.BlockSpec(memory_space=pltpu.VMEM)
    smem = pl.BlockSpec(memory_space=pltpu.SMEM)
    hbm = pl.BlockSpec(memory_space=pltpu.HBM)

    def kernel(*refs):
        logits_kernel((len(text), len(images)), *refs)

    square = pltpu.HBM((SIDE, SIDE), f32)
    half = jax.ShapeDtypeStruct((SIDE, WIDTH), jnp.bfloat16)
    small = jax.ShapeDtypeStruct((GROUP, 2, SIDE + 128), f32)
    return pl.pallas_call(
        kernel,
        out_shape=(square, square, half, half, small, small),
        in_specs=[smem] + [anywhere] * (len(text) + len(images)),
        out_specs=(hbm,) * 4 + (vmem,) * 2,
        scratch_shapes=[
            pltpu.VMEM((SIDE, SIDE), f32),
            pltpu.VMEM((SIDE, SIDE), f32),
            pltpu.VMEM((SIDE, WIDTH), jnp.bfloat16),
            pltpu.VMEM((SIDE, WIDTH), jnp.bfloat16),
            pltpu.VMEM((SIDE, WIDTH), jnp.bfloat16),
            pltpu.VMEM((SIDE, WIDTH), jnp.bfloat16),
            pltpu.VMEM((SIDE, 128), f32),
            pltpu.VMEM((SIDE, 128), f32),
            pltpu.VMEM((SIDE, 128), f32),
            pltpu.VMEM((SIDE, 128), f32),
            pltpu.SemaphoreType.DMA((64,)),
            pltpu.SemaphoreType.DMA((4,)),
        ],
        compiler_params=pltpu.CompilerParams(vmem_limit_bytes=LOGITS_VMEM),
        cost_estimate=pl.CostEstimate(
            flops=4 * SIDE * SIDE * WIDTH, bytes_accessed=20 << 20, transcendentals=4 * SIDE * SIDE
        ),
    )(places_in, *text, *images)


def gradient_kernel(
    s_ref,
    t_ref,
    row_ref,
    col_ref,
    row_id_ref,
    col_id_ref,
    out_ref,
    factor_ref,
    part_ref,
    lse_ref,
    total_ref,
):
    step = pl.program_id(0)
    size = 16

    def joined(ref, which):
        values = ref[:, which, :SIDE]
        top = jnp.max(values, axis=0, keepdims=True)
        return top + jnp.log2(jnp.sum(jnp.exp2(values - top), axis=0, keepdims=True))

    @pl.when(step == 0)
    def _():
        s_row_all, t_row_all = joined(row_ref, 0), joined(row_ref, 1)
        s_col_all, t_col_all = joined(col_ref, 0), joined(col_ref, 1)
        shared = (s_row_all - 0.5 * t_row_all) + (s_col_all - 0.5 * t_col_all)
        lse_ref[0:1, :] = s_row_all
        lse_ref[1:2, :] = t_row_all + 1.0
        lse_ref[2:3, :] = s_col_all
        lse_ref[3:4, :] = t_col_all + 1.0
        lse_ref[4:5, :] = shared
        for k, ref in ((0, row_ref), (1, col_ref)):
            scale = 2.0 / jnp.maximum(jnp.max(ref[:, 0, SIDE : SIDE + 128]), 1e-30)
            scale = jnp.full((1, SIDE), scale, jnp.float32)
            factor_ref[k : k + 1, :] = scale
            factor_ref[k + 2 : k + 3, :] = SCALE / scale
        factor_ref[4:8, :] = jnp.zeros((4, SIDE), jnp.float32)
        total_ref[...] = jnp.zeros((size, 128), jnp.float32)

    def strip(i, total):
        base = pl.multiple_of(i * STRIP, STRIP)
        at = pl.multiple_of(step * ROWS + base, STRIP)
        turned = jnp.transpose(lse_ref[:, pl.ds(at, STRIP)])
        for g in range(STRIP // size):
            rows = pl.ds(pl.multiple_of(base + g * size, size), size)
            s_row = jnp.broadcast_to(turned[g * size : (g + 1) * size, 0:1], (size, 128))
            t_row = jnp.broadcast_to(turned[g * size : (g + 1) * size, 1:2], (size, 128))
            row_id = jnp.broadcast_to(row_id_ref[rows, :], (size, 128))
            for k in range(SIDE // 128):
                lanes = pl.ds(k * 128, 128)
                s = s_ref[rows, lanes]
                t = t_ref[rows, lanes]
                weights = jnp.exp2(t - t_row) + jnp.exp2(t - lse_ref[3:4, lanes])
                value = (jnp.exp2(s - s_row) + jnp.exp2(s - lse_ref[2:3, lanes])) - weights
                same = row_id == col_id_ref[:, lanes]
                out_ref[rows, lanes] = jnp.where(same, value - 1.0, value).astype(jnp.bfloat16)
                total = total + (weights * (t - s) - jnp.where(same, s, 0.0))
        return total

    total_ref[...] = lax.fori_loop(0, ROWS // STRIP, strip, total_ref[...])

    @pl.when(step == pl.num_programs(0) - 1)
    def _():
        part = jnp.sum(total_ref[...]) + jnp.sum(lse_ref[4:5, :]) * (1.0 / GROUP)
        part_ref[...] = jnp.full(part_ref.shape, LN2 * part, jnp.float32)


def gradient_of_logits(s, t, row, col, row_id, col_id):
    f32 = jnp.float32
    by_rows = pl.BlockSpec((ROWS, SIDE), lambda i: (i, 0))

    def whole(shape):
        return pl.BlockSpec(shape, lambda i: (0,) * len(shape))

    return pl.pallas_call(
        gradient_kernel,
        grid=(SIDE // ROWS,),
        out_shape=(
            jax.ShapeDtypeStruct((SIDE, SIDE), jnp.bfloat16),
            jax.ShapeDtypeStruct((8, SIDE), f32),
            jax.ShapeDtypeStruct((GROUP, 8, 128), f32),
        ),
        in_specs=[
            by_rows,
            by_rows,
            whole(row.shape),
            whole(col.shape),
            pl.BlockSpec((ROWS, 1), lambda i: (i, 0)),
            whole(col_id.shape),
        ],
        out_specs=(by_rows, whole((8, SIDE)), whole((GROUP, 8, 128))),
        scratch_shapes=[pltpu.VMEM((8, SIDE), f32), pltpu.VMEM((16, 128), f32)],
        compiler_params=pltpu.CompilerParams(vmem_limit_bytes=GRADIENT_VMEM),
        cost_estimate=pl.CostEstimate(
            flops=16 * SIDE * SIDE, bytes_accessed=10 << 20, transcendentals=4 * SIDE * SIDE
        ),
    )(
        *(pltpu.with_memory_space_constraint(v, pltpu.HBM) for v in (s, t)),
        row,
        col,
        row_id,
        col_id,
    )


def exchanged(copies, axis):
    return lax.all_to_all(copies, axis, split_axis=0, concat_axis=0, tiled=True)


def body(image_student, text_student, image_teacher, text_teacher):
    y, zl, x, zh, c = (lax.axis_index(n) for n in NAMES)
    z = zh * 2 + zl
    text_pieces, image_pieces = gathered(
        *joined_halves(text_student, text_teacher, image_student, image_teacher)
    )

    sign = 1 - 2 * c
    at = []
    for _, offsets in text_pieces:
        for du, dv in offsets:
            dx = jnp.where(c == 0, du, dv)
            dy = jnp.where(c == 0, dv, du)
            at.append(((y + dy) % 4) * 4 + (x + dx) % 4)
    for _, offsets in image_pieces:
        for swapped, step in offsets:
            at.append((c ^ swapped) * 8 + (z + sign * step) % 8)
    where = jnp.stack(at).astype(jnp.int32)

    numbers = jnp.arange(SIDE, dtype=jnp.int32)
    slot, inner = numbers // BLOCK, numbers % BLOCK
    text_y, text_x = slot // 4, slot % 4
    col_id = (((text_x * 8 + zh * 2 + c) * 8) + text_y * 2 + zl) * BLOCK + inner
    image_c, image_z = slot // 8, slot % 8
    row_id = ((y * 2 + image_z % 2) * 32 + x * 8 + (image_z // 2) * 2 + image_c) * BLOCK + inner
    row_id, col_id = row_id[:, None], col_id[None, :]

    s, t, text_slab, image_slab, row_part, col_part = logits_and_statistics(
        where, [p for p, _ in text_pieces], [p for p, _ in image_pieces]
    )
    col_all = exchanged(col_part, TEXT_GROUP)
    row_all = exchanged(row_part, IMAGE_GROUP)
    gradient, factors, part = gradient_of_logits(s, t, row_all, col_all, row_id, col_id)
    text_scale, image_scale = factors[0:1], factors[1:2]
    image_factor, text_factor = factors[2:3], factors[3:4]

    half = SIDE // 2
    theirs = lax.dynamic_slice_in_dim(gradient, (1 - c) * half, half)
    mine = lax.dynamic_slice_in_dim(gradient, c * half, half)
    image_theirs = jnp.dot(theirs, text_slab, preferred_element_type=jnp.float32)
    arrived = moved((image_theirs * text_scale).astype(jnp.float16), other_core)
    image_mine = (
        jnp.dot(mine, text_slab, preferred_element_type=jnp.float32) * text_scale
    ) + arrived.astype(jnp.float32)
    blocks = image_mine.astype(jnp.float16).reshape(8, BLOCK, WIDTH)

    def block(step):
        return lax.dynamic_index_in_dim(blocks, (z + sign * step) % 8, 0, keepdims=False).astype(
            jnp.float32
        )

    def narrow(v):
        return v.astype(jnp.float16)

    tie = lax.optimization_barrier
    steps = [lambda p, k=k: flipped(p, k) for k in (4, 2, 1)] + [other_core]
    start, part = tie((narrow(block(4)), part))
    down = moved(start, along_z(-1)).astype(jnp.float32)
    value = jnp.sum(exchanged(part, TEXT_GROUP), axis=0)

    first, second, gradient = tie((narrow(block(-3) + down), narrow(block(3)), gradient))
    down = moved(first, along_z(-1)).astype(jnp.float32)
    up = moved(second, along_z(1)).astype(jnp.float32)
    text_part = (
        lax.dot_general(
            gradient, image_slab, (((0,), (0,)), ((), ())), preferred_element_type=jnp.float32
        )
        * image_scale
    ).astype(jnp.float16)
    first, second, text_part = tie((narrow(block(-2) + down), narrow(block(2) + up), text_part))
    down = moved(first, along_z(-1)).astype(jnp.float32)
    up = moved(second, along_z(1)).astype(jnp.float32)
    text_blocks = lax.all_to_all(text_part.reshape(16, BLOCK, WIDTH), TEXT_GROUP, 0, 0, tiled=True)
    first, second, value = tie((narrow(block(-1) + down), narrow(block(1) + up), value))
    down = moved(first, along_z(-1)).astype(jnp.float32)
    up = moved(second, along_z(1)).astype(jnp.float32)
    for to in steps:
        value = value + moved(value, to)
    loss = value[0, 0] / (256 * BLOCK)
    image_grad = (block(0) + down + up) * image_factor
    text_grad = jnp.sum(text_blocks.astype(jnp.float32), axis=0) * text_factor
    return (loss, image_grad, text_grad)


def flipped(p, bit):
    y, zl, x, zh, c = p
    z = (zh * 2 + zl) ^ bit
    return (y, z % 2, x, z // 2, c)


def solution(mesh):
    finer = Mesh(mesh.devices.reshape(SIZES), NAMES)
    placed = (P(ROW_COL, None), P(COL_ROW, None), P(ROW_COL, None), P(COL_ROW, None))
    return jax.shard_map(
        body,
        mesh=finer,
        in_specs=placed,
        out_specs=(P(), P(ROW_COL, None), P(COL_ROW, None)),
        check_vma=False,
    )
```

```python
import functools
import itertools
import math

import jax
import jax.numpy as jnp
from jax import lax
from jax.experimental import pallas as pl
from jax.experimental.pallas import tpu as pltpu
from jax.sharding import Mesh
from jax.sharding import PartitionSpec as P

NAMES = ("y", "zl", "x", "zh", "c")
SIZES = (4, 2, 4, 4, 2)
ROW_COL = ("y", "zl", "x", "zh", "c")
COL_ROW = ("x", "zh", "c", "y", "zl")
TEXT_GROUP = ("y", "x")
IMAGE_GROUP = ("zl", "zh", "c")

LOG2E = math.log2(math.e)
LN2 = math.log(2.0)
SCALE = 100.0
BLOCK = 64
WIDTH = 1024
SIDE = 1024
STRIP = 128
CHUNK = 256
GROUP = 16
LOGITS_VMEM = 58 * 1024 * 1024
GRADIENT_VMEM = 20 * 1024 * 1024
ROWS = 256


def places():
    return list(itertools.product(*(range(n) for n in SIZES)))


def index_of(place):
    at = 0
    for value, size in zip(place, SIZES):
        at = at * size + value % size
    return at


def shifted(place, axis, by):
    y, zl, x, zh, c = place
    if axis == "z":
        z = (zh * 2 + zl + by) % 8
        return (y, z % 2, x, z // 2, c)
    if axis == "x":
        return (y, zl, (x + by) % 4, zh, c)
    if axis == "y":
        return ((y + by) % 4, zl, x, zh, c)
    return (y, zl, x, zh, (c + by) % 2)


def moved(value, to):
    pairs = [(index_of(p), index_of(to(p))) for p in places()]
    return lax.ppermute(value, NAMES, pairs)


def along_u(by):
    return lambda p: shifted(p, "x" if p[4] == 0 else "y", by)


def along_v(by):
    return lambda p: shifted(p, "y" if p[4] == 0 else "x", by)


def along_z(by):
    return lambda p: shifted(p, "z", by if p[4] == 0 else -by)


def other_core(p):
    return shifted(p, "c", 1)


def joined_halves(*halves):
    def kernel(*refs):
        for k in range(4):
            refs[4 + k // 2][:, k % 2 * WIDTH : (k % 2 + 1) * WIDTH] = refs[k][...]

    vmem = pl.BlockSpec(memory_space=pltpu.VMEM)
    pair = jax.ShapeDtypeStruct((BLOCK, 2 * WIDTH), jnp.bfloat16)
    return pl.pallas_call(
        kernel,
        out_shape=(pair, pair),
        in_specs=[vmem] * 4,
        out_specs=(vmem,) * 2,
        cost_estimate=pl.CostEstimate(flops=0, bytes_accessed=1 << 20, transcendentals=0),
    )(*halves)


def gathered(text, image):
    tie = lax.optimization_barrier
    back, ahead = moved(text, along_u(1)), moved(text, along_u(-1))
    far = moved(text, along_u(2))
    mine = [image, moved(image, along_z(1))]
    theirs = [moved(image, other_core)]
    back, ahead, far, mine[1], theirs[0] = tie((back, ahead, far, mine[1], theirs[0]))

    line = jnp.concatenate([text, back, ahead, far], axis=0)
    line, mine[1], theirs[0] = tie((line, mine[1], theirs[0]))
    line_back, line_ahead = moved(line, along_v(1)), moved(line, along_v(-1))
    mine.append(moved(mine[1], along_z(1)))
    theirs.append(moved(theirs[0], along_z(1)))
    mine[2], theirs[1] = tie((mine[2], theirs[1]))
    mine.append(moved(mine[2], along_z(1)))
    theirs.append(moved(theirs[1], along_z(1)))
    line_back, line_ahead, mine[3], theirs[2] = tie((line_back, line_ahead, mine[3], theirs[2]))

    first_far = moved(line_back[:128], along_v(1))
    second_far = moved(line_ahead[128:], along_v(-1))
    mine.append(moved(mine[3], along_z(1)))
    theirs.append(moved(theirs[2], along_z(1)))
    early = jnp.concatenate([mine[1], mine[2], mine[3], theirs[1], theirs[2]], axis=0)
    early_other = moved(early, other_core)
    mine[4], theirs[3] = tie((mine[4], theirs[3]))
    late = jnp.concatenate([mine[4], theirs[3]], axis=0)
    late_other = moved(late, other_core)
    us = (0, -1, 1, 2)
    return [
        (line, [(du, 0) for du in us]),
        (line_back, [(du, -1) for du in us]),
        (line_ahead, [(du, 1) for du in us]),
        (first_far, ((0, 2), (-1, 2))),
        (second_far, ((1, 2), (2, 2))),
    ], [
        (image, ((0, 0),)),
        (theirs[0], ((1, 0),)),
        (early, ((0, -1), (0, -2), (0, -3), (1, -1), (1, -2))),
        (early_other, ((1, 1), (1, 2), (1, 3), (0, 1), (0, 2))),
        (late, ((0, 4), (1, -3))),
        (late_other, ((1, 4), (0, 3))),
    ]


def logits_kernel(counts, *refs):
    n_text, n_image = counts
    place_ref = refs[0]
    text_refs = refs[1 : 1 + n_text]
    image_refs = refs[1 + n_text : 1 + n_text + n_image]
    (s_hbm, t_hbm, text_hbm, image_hbm, row_ref, col_ref) = refs[
        1 + n_text + n_image : 7 + n_text + n_image
    ]
    (
        s_ref,
        t_ref,
        text_out,
        image_out,
        text_frozen,
        image_frozen,
        s_high,
        s_sum,
        t_high,
        t_sum,
        sems,
        out_sems,
    ) = refs[7 + n_text + n_image :]
    copies = []
    k = 0
    for group, out, frozen in (
        (text_refs, text_out, text_frozen),
        (image_refs, image_out, image_frozen),
    ):
        for ref in group:
            for b in range(ref.shape[0] // BLOCK):
                at = pl.multiple_of(place_ref[k] * BLOCK, BLOCK)
                for half, target in ((0, out), (1, frozen)):
                    copies.append(
                        pltpu.make_async_copy(
                            ref.at[pl.ds(b * BLOCK, BLOCK), pl.ds(half * WIDTH, WIDTH)],
                            target.at[pl.ds(at, BLOCK), :],
                            sems.at[2 * k + half],
                        )
                    )
                k += 1
    for half in (0, 1):
        for copy in copies[half::2]:
            copy.start()
    outward = [
        pltpu.make_async_copy(text_out, text_hbm, out_sems.at[2]),
        pltpu.make_async_copy(image_out, image_hbm, out_sems.at[3]),
        pltpu.make_async_copy(s_ref, s_hbm, out_sems.at[0]),
        pltpu.make_async_copy(t_ref, t_hbm, out_sems.at[1]),
    ]

    for which, left, right, out in (
        (0, image_out, text_out, s_ref),
        (1, image_frozen, text_frozen, t_ref),
    ):
        for copy in copies[which::2]:
            copy.wait()

        @pl.loop(0, SIDE // CHUNK)
        def _(j):
            cols = pl.ds(pl.multiple_of(j * CHUNK, CHUNK), CHUNK)
            tile = (SCALE * LOG2E) * lax.dot_general(
                left[...],
                right[cols, :],
                (((1,), (1,)), ((), ())),
                preferred_element_type=jnp.float32,
            )
            out[:, cols] = tile
            tile = tile.reshape(SIDE // 8, 8, CHUNK)
            high = jnp.max(tile, axis=0)
            total = jnp.sum(jnp.exp2(tile - high), axis=0)
            top = jnp.max(high, axis=0, keepdims=True)
            total = jnp.sum(total * jnp.exp2(high - top), axis=0, keepdims=True)
            lse = top + jnp.log2(total)
            for n in range(GROUP):
                col_ref[n, which : which + 1, cols] = lse

        for copy in outward[:3] if which == 0 else outward[3:]:
            copy.start()

    @pl.loop(0, SIDE // 64)
    def _(i):
        for g in range(8):
            rows = pl.ds(pl.multiple_of(i * 64 + g * 8, 8), 8)
            for ref, high_ref, sum_ref in ((s_ref, s_high, s_sum), (t_ref, t_high, t_sum)):
                tiles = [ref[rows, pl.ds(k * 128, 128)] for k in range(SIDE // 128)]
                high = functools.reduce(jnp.maximum, tiles)
                high_ref[rows, :] = high
                sum_ref[rows, :] = functools.reduce(jnp.add, [jnp.exp2(v - high) for v in tiles])

    @pl.loop(0, SIDE // 128)
    def _(i):
        rows = pl.ds(pl.multiple_of(i * 128, 128), 128)
        for which, high_ref, sum_ref in ((0, s_high, s_sum), (1, t_high, t_sum)):
            high = jnp.transpose(high_ref[rows, :])
            total = jnp.transpose(sum_ref[rows, :])
            top = jnp.max(high, axis=0, keepdims=True)
            total = jnp.sum(total * jnp.exp2(high - top), axis=0, keepdims=True)
            lse = top + jnp.log2(total)
            for n in range(GROUP):
                row_ref[n, which : which + 1, rows] = lse

    for slab, ref in ((text_out, row_ref), (image_out, col_ref)):
        largest = jnp.max(jnp.abs(slab[...]), axis=0, keepdims=True).astype(jnp.float32)
        largest = jnp.full((2, 128), jnp.max(largest), jnp.float32)
        for n in range(GROUP):
            ref[n, :, SIDE : SIDE + 128] = largest
    for copy in outward:
        copy.wait()


def logits_and_statistics(places_in, text, images):
    f32 = jnp.float32
    anywhere = pl.BlockSpec(memory_space=pl.ANY)
    vmem = pl.BlockSpec(memory_space=pltpu.VMEM)
    smem = pl.BlockSpec(memory_space=pltpu.SMEM)
    hbm = pl.BlockSpec(memory_space=pltpu.HBM)

    def kernel(*refs):
        logits_kernel((len(text), len(images)), *refs)

    square = pltpu.HBM((SIDE, SIDE), f32)
    half = jax.ShapeDtypeStruct((SIDE, WIDTH), jnp.bfloat16)
    small = jax.ShapeDtypeStruct((GROUP, 2, SIDE + 128), f32)
    return pl.pallas_call(
        kernel,
        out_shape=(square, square, half, half, small, small),
        in_specs=[smem] + [anywhere] * (len(text) + len(images)),
        out_specs=(hbm,) * 4 + (vmem,) * 2,
        scratch_shapes=[
            pltpu.VMEM((SIDE, SIDE), f32),
            pltpu.VMEM((SIDE, SIDE), f32),
            pltpu.VMEM((SIDE, WIDTH), jnp.bfloat16),
            pltpu.VMEM((SIDE, WIDTH), jnp.bfloat16),
            pltpu.VMEM((SIDE, WIDTH), jnp.bfloat16),
            pltpu.VMEM((SIDE, WIDTH), jnp.bfloat16),
            pltpu.VMEM((SIDE, 128), f32),
            pltpu.VMEM((SIDE, 128), f32),
            pltpu.VMEM((SIDE, 128), f32),
            pltpu.VMEM((SIDE, 128), f32),
            pltpu.SemaphoreType.DMA((64,)),
            pltpu.SemaphoreType.DMA((4,)),
        ],
        compiler_params=pltpu.CompilerParams(vmem_limit_bytes=LOGITS_VMEM),
        cost_estimate=pl.CostEstimate(
            flops=4 * SIDE * SIDE * WIDTH, bytes_accessed=20 << 20, transcendentals=4 * SIDE * SIDE
        ),
    )(places_in, *text, *images)


def gradient_kernel(
    s_ref,
    t_ref,
    row_ref,
    col_ref,
    row_id_ref,
    col_id_ref,
    out_ref,
    factor_ref,
    part_ref,
    lse_ref,
    total_ref,
):
    step = pl.program_id(0)
    size = 16

    def joined(ref, which):
        values = ref[:, which, :SIDE]
        top = jnp.max(values, axis=0, keepdims=True)
        return top + jnp.log2(jnp.sum(jnp.exp2(values - top), axis=0, keepdims=True))

    @pl.when(step == 0)
    def _():
        s_row_all, t_row_all = joined(row_ref, 0), joined(row_ref, 1)
        s_col_all, t_col_all = joined(col_ref, 0), joined(col_ref, 1)
        shared = (s_row_all - 0.5 * t_row_all) + (s_col_all - 0.5 * t_col_all)
        lse_ref[0:1, :] = s_row_all
        lse_ref[1:2, :] = t_row_all + 1.0
        lse_ref[2:3, :] = s_col_all
        lse_ref[3:4, :] = t_col_all + 1.0
        lse_ref[4:5, :] = shared
        for k, ref in ((0, row_ref), (1, col_ref)):
            scale = 2.0 / jnp.maximum(jnp.max(ref[:, 0, SIDE : SIDE + 128]), 1e-30)
            scale = jnp.full((1, SIDE), scale, jnp.float32)
            factor_ref[k : k + 1, :] = scale
            factor_ref[k + 2 : k + 3, :] = SCALE / scale
        factor_ref[4:8, :] = jnp.zeros((4, SIDE), jnp.float32)
        total_ref[...] = jnp.zeros((size, 128), jnp.float32)

    def strip(i, total):
        base = pl.multiple_of(i * STRIP, STRIP)
        at = pl.multiple_of(step * ROWS + base, STRIP)
        turned = jnp.transpose(lse_ref[:, pl.ds(at, STRIP)])
        for g in range(STRIP // size):
            rows = pl.ds(pl.multiple_of(base + g * size, size), size)
            s_row = jnp.broadcast_to(turned[g * size : (g + 1) * size, 0:1], (size, 128))
            t_row = jnp.broadcast_to(turned[g * size : (g + 1) * size, 1:2], (size, 128))
            row_id = jnp.broadcast_to(row_id_ref[rows, :], (size, 128))
            for k in range(SIDE // 128):
                lanes = pl.ds(k * 128, 128)
                s = s_ref[rows, lanes]
                t = t_ref[rows, lanes]
                weights = jnp.exp2(t - t_row) + jnp.exp2(t - lse_ref[3:4, lanes])
                value = (jnp.exp2(s - s_row) + jnp.exp2(s - lse_ref[2:3, lanes])) - weights
                same = row_id == col_id_ref[:, lanes]
                out_ref[rows, lanes] = jnp.where(same, value - 1.0, value).astype(jnp.bfloat16)
                total = total + (weights * (t - s) - jnp.where(same, s, 0.0))
        return total

    total_ref[...] = lax.fori_loop(0, ROWS // STRIP, strip, total_ref[...])

    @pl.when(step == pl.num_programs(0) - 1)
    def _():
        part = jnp.sum(total_ref[...]) + jnp.sum(lse_ref[4:5, :]) * (1.0 / GROUP)
        part_ref[...] = jnp.full(part_ref.shape, LN2 * part, jnp.float32)


def gradient_of_logits(s, t, row, col, row_id, col_id):
    f32 = jnp.float32
    by_rows = pl.BlockSpec((ROWS, SIDE), lambda i: (i, 0))

    def whole(shape):
        return pl.BlockSpec(shape, lambda i: (0,) * len(shape))

    return pl.pallas_call(
        gradient_kernel,
        grid=(SIDE // ROWS,),
        out_shape=(
            jax.ShapeDtypeStruct((SIDE, SIDE), jnp.bfloat16),
            jax.ShapeDtypeStruct((8, SIDE), f32),
            jax.ShapeDtypeStruct((GROUP, 8, 128), f32),
        ),
        in_specs=[
            by_rows,
            by_rows,
            whole(row.shape),
            whole(col.shape),
            pl.BlockSpec((ROWS, 1), lambda i: (i, 0)),
            whole(col_id.shape),
        ],
        out_specs=(by_rows, whole((8, SIDE)), whole((GROUP, 8, 128))),
        scratch_shapes=[pltpu.VMEM((8, SIDE), f32), pltpu.VMEM((16, 128), f32)],
        compiler_params=pltpu.CompilerParams(vmem_limit_bytes=GRADIENT_VMEM),
        cost_estimate=pl.CostEstimate(
            flops=16 * SIDE * SIDE, bytes_accessed=10 << 20, transcendentals=4 * SIDE * SIDE
        ),
    )(
        *(pltpu.with_memory_space_constraint(v, pltpu.HBM) for v in (s, t)),
        row,
        col,
        row_id,
        col_id,
    )


def exchanged(copies, axis):
    return lax.all_to_all(copies, axis, split_axis=0, concat_axis=0, tiled=True)


def body(image_student, text_student, image_teacher, text_teacher):
    y, zl, x, zh, c = (lax.axis_index(n) for n in NAMES)
    z = zh * 2 + zl
    text_pieces, image_pieces = gathered(
        *joined_halves(text_student, text_teacher, image_student, image_teacher)
    )

    sign = 1 - 2 * c
    at = []
    for _, offsets in text_pieces:
        for du, dv in offsets:
            dx = jnp.where(c == 0, du, dv)
            dy = jnp.where(c == 0, dv, du)
            at.append(((y + dy) % 4) * 4 + (x + dx) % 4)
    for _, offsets in image_pieces:
        for swapped, step in offsets:
            at.append((c ^ swapped) * 8 + (z + sign * step) % 8)
    where = jnp.stack(at).astype(jnp.int32)

    numbers = jnp.arange(SIDE, dtype=jnp.int32)
    slot, inner = numbers // BLOCK, numbers % BLOCK
    text_y, text_x = slot // 4, slot % 4
    col_id = (((text_x * 8 + zh * 2 + c) * 8) + text_y * 2 + zl) * BLOCK + inner
    image_c, image_z = slot // 8, slot % 8
    row_id = ((y * 2 + image_z % 2) * 32 + x * 8 + (image_z // 2) * 2 + image_c) * BLOCK + inner
    row_id, col_id = row_id[:, None], col_id[None, :]

    s, t, text_slab, image_slab, row_part, col_part = logits_and_statistics(
        where, [p for p, _ in text_pieces], [p for p, _ in image_pieces]
    )
    col_all = exchanged(col_part, TEXT_GROUP)
    row_all = exchanged(row_part, IMAGE_GROUP)
    gradient, factors, part = gradient_of_logits(s, t, row_all, col_all, row_id, col_id)
    text_scale, image_scale = factors[0:1], factors[1:2]
    image_factor, text_factor = factors[2:3], factors[3:4]

    half = SIDE // 2
    theirs = lax.dynamic_slice_in_dim(gradient, (1 - c) * half, half)
    mine = lax.dynamic_slice_in_dim(gradient, c * half, half)
    image_theirs = jnp.dot(theirs, text_slab, preferred_element_type=jnp.float32)
    arrived = moved((image_theirs * text_scale).astype(jnp.float16), other_core)
    image_mine = (
        jnp.dot(mine, text_slab, preferred_element_type=jnp.float32) * text_scale
    ) + arrived.astype(jnp.float32)
    blocks = image_mine.astype(jnp.float16).reshape(8, BLOCK, WIDTH)

    def block(step):
        return lax.dynamic_index_in_dim(blocks, (z + sign * step) % 8, 0, keepdims=False).astype(
            jnp.float32
        )

    def narrow(v):
        return v.astype(jnp.float16)

    tie = lax.optimization_barrier
    steps = [lambda p, k=k: flipped(p, k) for k in (4, 2, 1)] + [other_core]
    start, part = tie((narrow(block(4)), part))
    down = moved(start, along_z(-1)).astype(jnp.float32)
    value = jnp.sum(exchanged(part, TEXT_GROUP), axis=0)

    first, second, gradient = tie((narrow(block(-3) + down), narrow(block(3)), gradient))
    down = moved(first, along_z(-1)).astype(jnp.float32)
    up = moved(second, along_z(1)).astype(jnp.float32)
    text_part = (
        lax.dot_general(
            gradient, image_slab, (((0,), (0,)), ((), ())), preferred_element_type=jnp.float32
        )
        * image_scale
    ).astype(jnp.float16)
    first, second, text_part = tie((narrow(block(-2) + down), narrow(block(2) + up), text_part))
    down = moved(first, along_z(-1)).astype(jnp.float32)
    up = moved(second, along_z(1)).astype(jnp.float32)
    text_blocks = lax.all_to_all(text_part.reshape(16, BLOCK, WIDTH), TEXT_GROUP, 0, 0, tiled=True)
    value = value + moved(value, steps[0])
    first, second, value = tie((narrow(block(-1) + down), narrow(block(1) + up), value))
    down = moved(first, along_z(-1)).astype(jnp.float32)
    up = moved(second, along_z(1)).astype(jnp.float32)
    for to in steps[1:]:
        value = value + moved(value, to)
    loss = value[0, 0] / (256 * BLOCK)
    image_grad = (block(0) + down + up) * image_factor
    text_grad = jnp.sum(text_blocks.astype(jnp.float32) * text_factor, axis=0)
    return (loss, image_grad, text_grad)


def flipped(p, bit):
    y, zl, x, zh, c = p
    z = (zh * 2 + zl) ^ bit
    return (y, z % 2, x, z // 2, c)


def solution(mesh):
    finer = Mesh(mesh.devices.reshape(SIZES), NAMES)
    placed = (P(ROW_COL, None), P(COL_ROW, None), P(ROW_COL, None), P(COL_ROW, None))
    return jax.shard_map(
        body,
        mesh=finer,
        in_specs=placed,
        out_specs=(P(), P(ROW_COL, None), P(COL_ROW, None)),
        check_vma=False,
    )
```

```python
import functools
import itertools
import math

import jax
import jax.numpy as jnp
from jax import lax
from jax.experimental import pallas as pl
from jax.experimental.pallas import tpu as pltpu
from jax.sharding import Mesh
from jax.sharding import PartitionSpec as P

NAMES = ("y", "zl", "x", "zh", "c")
SIZES = (4, 2, 4, 4, 2)
ROW_COL = ("y", "zl", "x", "zh", "c")
COL_ROW = ("x", "zh", "c", "y", "zl")
TEXT_GROUP = ("y", "x")
IMAGE_GROUP = ("zl", "zh", "c")

LOG2E = math.log2(math.e)
LN2 = math.log(2.0)
SCALE = 100.0
BLOCK = 64
WIDTH = 1024
SIDE = 1024
STRIP = 128
CHUNK = 256
GROUP = 16
LOGITS_VMEM = 58 * 1024 * 1024
GRADIENT_VMEM = 20 * 1024 * 1024
ROWS = 256


def places():
    return list(itertools.product(*(range(n) for n in SIZES)))


def index_of(place):
    at = 0
    for value, size in zip(place, SIZES):
        at = at * size + value % size
    return at


def shifted(place, axis, by):
    y, zl, x, zh, c = place
    if axis == "z":
        z = (zh * 2 + zl + by) % 8
        return (y, z % 2, x, z // 2, c)
    if axis == "x":
        return (y, zl, (x + by) % 4, zh, c)
    if axis == "y":
        return ((y + by) % 4, zl, x, zh, c)
    return (y, zl, x, zh, (c + by) % 2)


def moved(value, to):
    pairs = [(index_of(p), index_of(to(p))) for p in places()]
    return lax.ppermute(value, NAMES, pairs)


def along_u(by):
    return lambda p: shifted(p, "x" if p[4] == 0 else "y", by)


def along_v(by):
    return lambda p: shifted(p, "y" if p[4] == 0 else "x", by)


def along_z(by):
    return lambda p: shifted(p, "z", by if p[4] == 0 else -by)


def other_core(p):
    return shifted(p, "c", 1)


def joined_halves(*halves):
    def kernel(*refs):
        for k in range(4):
            refs[4 + k // 2][:, k % 2 * WIDTH : (k % 2 + 1) * WIDTH] = refs[k][...]

    vmem = pl.BlockSpec(memory_space=pltpu.VMEM)
    pair = jax.ShapeDtypeStruct((BLOCK, 2 * WIDTH), jnp.bfloat16)
    return pl.pallas_call(
        kernel,
        out_shape=(pair, pair),
        in_specs=[vmem] * 4,
        out_specs=(vmem,) * 2,
        cost_estimate=pl.CostEstimate(flops=0, bytes_accessed=1 << 20, transcendentals=0),
    )(*halves)


def gathered(text, image):
    tie = lax.optimization_barrier
    back, ahead = moved(text, along_u(1)), moved(text, along_u(-1))
    far = moved(text, along_u(2))
    mine = [image, moved(image, along_z(1))]
    theirs = [moved(image, other_core)]
    back, ahead, far, mine[1], theirs[0] = tie((back, ahead, far, mine[1], theirs[0]))

    line = jnp.concatenate([text, back, ahead, far], axis=0)
    line, mine[1], theirs[0] = tie((line, mine[1], theirs[0]))
    line_back, line_ahead = moved(line, along_v(1)), moved(line, along_v(-1))
    mine.append(moved(mine[1], along_z(1)))
    theirs.append(moved(theirs[0], along_z(1)))
    mine[2], theirs[1] = tie((mine[2], theirs[1]))
    mine.append(moved(mine[2], along_z(1)))
    theirs.append(moved(theirs[1], along_z(1)))
    line_back, line_ahead, mine[3], theirs[2] = tie((line_back, line_ahead, mine[3], theirs[2]))

    first_far = moved(line_back[:128], along_v(1))
    second_far = moved(line_ahead[128:], along_v(-1))
    mine.append(moved(mine[3], along_z(1)))
    theirs.append(moved(theirs[2], along_z(1)))
    early = jnp.concatenate([mine[1], mine[2], mine[3], theirs[1], theirs[2]], axis=0)
    early_other = moved(early, other_core)
    mine[4], theirs[3] = tie((mine[4], theirs[3]))
    late = jnp.concatenate([mine[4], theirs[3]], axis=0)
    late_other = moved(late, other_core)
    us = (0, -1, 1, 2)
    return [
        (line, [(du, 0) for du in us]),
        (line_back, [(du, -1) for du in us]),
        (line_ahead, [(du, 1) for du in us]),
        (first_far, ((0, 2), (-1, 2))),
        (second_far, ((1, 2), (2, 2))),
    ], [
        (image, ((0, 0),)),
        (theirs[0], ((1, 0),)),
        (early, ((0, -1), (0, -2), (0, -3), (1, -1), (1, -2))),
        (early_other, ((1, 1), (1, 2), (1, 3), (0, 1), (0, 2))),
        (late, ((0, 4), (1, -3))),
        (late_other, ((1, 4), (0, 3))),
    ]


def logits_kernel(counts, *refs):
    n_text, n_image = counts
    place_ref = refs[0]
    text_refs = refs[1 : 1 + n_text]
    image_refs = refs[1 + n_text : 1 + n_text + n_image]
    (s_hbm, t_hbm, text_hbm, image_hbm, row_ref, col_ref) = refs[
        1 + n_text + n_image : 7 + n_text + n_image
    ]
    (
        s_ref,
        t_ref,
        text_out,
        image_out,
        text_frozen,
        image_frozen,
        s_high,
        s_sum,
        t_high,
        t_sum,
        sems,
        out_sems,
    ) = refs[7 + n_text + n_image :]
    copies = []
    k = 0
    for group, out, frozen in (
        (text_refs, text_out, text_frozen),
        (image_refs, image_out, image_frozen),
    ):
        for ref in group:
            for b in range(ref.shape[0] // BLOCK):
                at = pl.multiple_of(place_ref[k] * BLOCK, BLOCK)
                for half, target in ((0, out), (1, frozen)):
                    copies.append(
                        pltpu.make_async_copy(
                            ref.at[pl.ds(b * BLOCK, BLOCK), pl.ds(half * WIDTH, WIDTH)],
                            target.at[pl.ds(at, BLOCK), :],
                            sems.at[2 * k + half],
                        )
                    )
                k += 1
    for half in (0, 1):
        for copy in copies[half::2]:
            copy.start()
    outward = [
        pltpu.make_async_copy(text_out, text_hbm, out_sems.at[2]),
        pltpu.make_async_copy(image_out, image_hbm, out_sems.at[3]),
        pltpu.make_async_copy(s_ref, s_hbm, out_sems.at[0]),
        pltpu.make_async_copy(t_ref, t_hbm, out_sems.at[1]),
    ]

    for which, left, right, out in (
        (0, image_out, text_out, s_ref),
        (1, image_frozen, text_frozen, t_ref),
    ):
        for copy in copies[which::2]:
            copy.wait()

        @pl.loop(0, SIDE // CHUNK)
        def _(j):
            cols = pl.ds(pl.multiple_of(j * CHUNK, CHUNK), CHUNK)
            tile = (SCALE * LOG2E) * lax.dot_general(
                left[...],
                right[cols, :],
                (((1,), (1,)), ((), ())),
                preferred_element_type=jnp.float32,
            )
            out[:, cols] = tile
            tile = tile.reshape(SIDE // 8, 8, CHUNK)
            high = jnp.max(tile, axis=0)
            total = jnp.sum(jnp.exp2(tile - high), axis=0)
            top = jnp.max(high, axis=0, keepdims=True)
            total = jnp.sum(total * jnp.exp2(high - top), axis=0, keepdims=True)
            lse = top + jnp.log2(total)
            for n in range(GROUP):
                col_ref[n, which : which + 1, cols] = lse

        for copy in outward[:3] if which == 0 else outward[3:]:
            copy.start()

    @pl.loop(0, SIDE // 64)
    def _(i):
        for g in range(8):
            rows = pl.ds(pl.multiple_of(i * 64 + g * 8, 8), 8)
            for ref, high_ref, sum_ref in ((s_ref, s_high, s_sum), (t_ref, t_high, t_sum)):
                tiles = [ref[rows, pl.ds(k * 128, 128)] for k in range(SIDE // 128)]
                high = functools.reduce(jnp.maximum, tiles)
                high_ref[rows, :] = high
                sum_ref[rows, :] = functools.reduce(jnp.add, [jnp.exp2(v - high) for v in tiles])

    @pl.loop(0, SIDE // 128)
    def _(i):
        rows = pl.ds(pl.multiple_of(i * 128, 128), 128)
        for which, high_ref, sum_ref in ((0, s_high, s_sum), (1, t_high, t_sum)):
            high = jnp.transpose(high_ref[rows, :])
            total = jnp.transpose(sum_ref[rows, :])
            top = jnp.max(high, axis=0, keepdims=True)
            total = jnp.sum(total * jnp.exp2(high - top), axis=0, keepdims=True)
            lse = top + jnp.log2(total)
            for n in range(GROUP):
                row_ref[n, which : which + 1, rows] = lse

    for slab, ref in ((text_out, row_ref), (image_out, col_ref)):
        largest = jnp.max(jnp.abs(slab[...]), axis=0, keepdims=True).astype(jnp.float32)
        largest = jnp.full((2, 128), jnp.max(largest), jnp.float32)
        for n in range(GROUP):
            ref[n, :, SIDE : SIDE + 128] = largest
    for copy in outward:
        copy.wait()


def logits_and_statistics(places_in, text, images):
    f32 = jnp.float32
    anywhere = pl.BlockSpec(memory_space=pl.ANY)
    vmem = pl.BlockSpec(memory_space=pltpu.VMEM)
    smem = pl.BlockSpec(memory_space=pltpu.SMEM)
    hbm = pl.BlockSpec(memory_space=pltpu.HBM)

    def kernel(*refs):
        logits_kernel((len(text), len(images)), *refs)

    square = pltpu.HBM((SIDE, SIDE), f32)
    half = jax.ShapeDtypeStruct((SIDE, WIDTH), jnp.bfloat16)
    small = jax.ShapeDtypeStruct((GROUP, 2, SIDE + 128), f32)
    return pl.pallas_call(
        kernel,
        out_shape=(square, square, half, half, small, small),
        in_specs=[smem] + [anywhere] * (len(text) + len(images)),
        out_specs=(hbm,) * 4 + (vmem,) * 2,
        scratch_shapes=[
            pltpu.VMEM((SIDE, SIDE), f32),
            pltpu.VMEM((SIDE, SIDE), f32),
            pltpu.VMEM((SIDE, WIDTH), jnp.bfloat16),
            pltpu.VMEM((SIDE, WIDTH), jnp.bfloat16),
            pltpu.VMEM((SIDE, WIDTH), jnp.bfloat16),
            pltpu.VMEM((SIDE, WIDTH), jnp.bfloat16),
            pltpu.VMEM((SIDE, 128), f32),
            pltpu.VMEM((SIDE, 128), f32),
            pltpu.VMEM((SIDE, 128), f32),
            pltpu.VMEM((SIDE, 128), f32),
            pltpu.SemaphoreType.DMA((64,)),
            pltpu.SemaphoreType.DMA((4,)),
        ],
        compiler_params=pltpu.CompilerParams(vmem_limit_bytes=LOGITS_VMEM),
        cost_estimate=pl.CostEstimate(
            flops=4 * SIDE * SIDE * WIDTH, bytes_accessed=20 << 20, transcendentals=4 * SIDE * SIDE
        ),
    )(places_in, *text, *images)


def gradient_kernel(
    s_ref,
    t_ref,
    row_ref,
    col_ref,
    row_id_ref,
    col_id_ref,
    out_ref,
    turned_ref,
    factor_ref,
    part_ref,
    lse_ref,
    total_ref,
):
    step = pl.program_id(0)
    size = 16

    def joined(ref, which):
        values = ref[:, which, :SIDE]
        top = jnp.max(values, axis=0, keepdims=True)
        return top + jnp.log2(jnp.sum(jnp.exp2(values - top), axis=0, keepdims=True))

    @pl.when(step == 0)
    def _():
        s_row_all, t_row_all = joined(row_ref, 0), joined(row_ref, 1)
        s_col_all, t_col_all = joined(col_ref, 0), joined(col_ref, 1)
        shared = (s_row_all - 0.5 * t_row_all) + (s_col_all - 0.5 * t_col_all)
        lse_ref[0:1, :] = s_row_all
        lse_ref[1:2, :] = t_row_all + 1.0
        lse_ref[2:3, :] = s_col_all
        lse_ref[3:4, :] = t_col_all + 1.0
        lse_ref[4:5, :] = shared
        for k, ref in ((0, row_ref), (1, col_ref)):
            scale = 2.0 / jnp.maximum(jnp.max(ref[:, 0, SIDE : SIDE + 128]), 1e-30)
            scale = jnp.full((1, SIDE), scale, jnp.float32)
            factor_ref[k : k + 1, :] = scale
            factor_ref[k + 2 : k + 3, :] = SCALE / scale
        factor_ref[4:8, :] = jnp.zeros((4, SIDE), jnp.float32)
        total_ref[...] = jnp.zeros((size, 128), jnp.float32)

    def strip(i, total):
        base = pl.multiple_of(i * STRIP, STRIP)
        at = pl.multiple_of(step * ROWS + base, STRIP)
        turned = jnp.transpose(lse_ref[:, pl.ds(at, STRIP)])
        for g in range(STRIP // size):
            rows = pl.ds(pl.multiple_of(base + g * size, size), size)
            s_row = jnp.broadcast_to(turned[g * size : (g + 1) * size, 0:1], (size, 128))
            t_row = jnp.broadcast_to(turned[g * size : (g + 1) * size, 1:2], (size, 128))
            row_id = jnp.broadcast_to(row_id_ref[rows, :], (size, 128))
            for k in range(SIDE // 128):
                lanes = pl.ds(k * 128, 128)
                s = s_ref[rows, lanes]
                t = t_ref[rows, lanes]
                weights = jnp.exp2(t - t_row) + jnp.exp2(t - lse_ref[3:4, lanes])
                value = (jnp.exp2(s - s_row) + jnp.exp2(s - lse_ref[2:3, lanes])) - weights
                same = row_id == col_id_ref[:, lanes]
                out_ref[rows, lanes] = jnp.where(same, value - 1.0, value).astype(jnp.bfloat16)
                total = total + (weights * (t - s) - jnp.where(same, s, 0.0))
        for k in range(SIDE // 128):
            tile = out_ref[pl.ds(base, STRIP), pl.ds(k * 128, 128)].astype(jnp.float32)
            turned_ref[pl.ds(k * 128, 128), pl.ds(base, STRIP)] = jnp.transpose(tile).astype(
                jnp.bfloat16
            )
        return total

    total_ref[...] = lax.fori_loop(0, ROWS // STRIP, strip, total_ref[...])

    @pl.when(step == pl.num_programs(0) - 1)
    def _():
        part = jnp.sum(total_ref[...]) + jnp.sum(lse_ref[4:5, :]) * (1.0 / GROUP)
        part_ref[...] = jnp.full(part_ref.shape, LN2 * part, jnp.float32)


def gradient_of_logits(s, t, row, col, row_id, col_id):
    f32 = jnp.float32
    by_rows = pl.BlockSpec((ROWS, SIDE), lambda i: (i, 0))

    def whole(shape):
        return pl.BlockSpec(shape, lambda i: (0,) * len(shape))

    return pl.pallas_call(
        gradient_kernel,
        grid=(SIDE // ROWS,),
        out_shape=(
            jax.ShapeDtypeStruct((SIDE, SIDE), jnp.bfloat16),
            jax.ShapeDtypeStruct((SIDE, SIDE), jnp.bfloat16),
            jax.ShapeDtypeStruct((8, SIDE), f32),
            jax.ShapeDtypeStruct((GROUP, 8, 128), f32),
        ),
        in_specs=[
            by_rows,
            by_rows,
            whole(row.shape),
            whole(col.shape),
            pl.BlockSpec((ROWS, 1), lambda i: (i, 0)),
            whole(col_id.shape),
        ],
        out_specs=(by_rows, pl.BlockSpec((SIDE, ROWS), lambda i: (0, i)), whole((8, SIDE)), whole((GROUP, 8, 128))),
        scratch_shapes=[pltpu.VMEM((8, SIDE), f32), pltpu.VMEM((16, 128), f32)],
        compiler_params=pltpu.CompilerParams(vmem_limit_bytes=GRADIENT_VMEM),
        cost_estimate=pl.CostEstimate(
            flops=16 * SIDE * SIDE, bytes_accessed=10 << 20, transcendentals=4 * SIDE * SIDE
        ),
    )(
        *(pltpu.with_memory_space_constraint(v, pltpu.HBM) for v in (s, t)),
        row,
        col,
        row_id,
        col_id,
    )


def exchanged(copies, axis):
    return lax.all_to_all(copies, axis, split_axis=0, concat_axis=0, tiled=True)


def body(image_student, text_student, image_teacher, text_teacher):
    y, zl, x, zh, c = (lax.axis_index(n) for n in NAMES)
    z = zh * 2 + zl
    text_pieces, image_pieces = gathered(
        *joined_halves(text_student, text_teacher, image_student, image_teacher)
    )

    sign = 1 - 2 * c
    at = []
    for _, offsets in text_pieces:
        for du, dv in offsets:
            dx = jnp.where(c == 0, du, dv)
            dy = jnp.where(c == 0, dv, du)
            at.append(((y + dy) % 4) * 4 + (x + dx) % 4)
    for _, offsets in image_pieces:
        for swapped, step in offsets:
            at.append((c ^ swapped) * 8 + (z + sign * step) % 8)
    where = jnp.stack(at).astype(jnp.int32)

    numbers = jnp.arange(SIDE, dtype=jnp.int32)
    slot, inner = numbers // BLOCK, numbers % BLOCK
    text_y, text_x = slot // 4, slot % 4
    col_id = (((text_x * 8 + zh * 2 + c) * 8) + text_y * 2 + zl) * BLOCK + inner
    image_c, image_z = slot // 8, slot % 8
    row_id = ((y * 2 + image_z % 2) * 32 + x * 8 + (image_z // 2) * 2 + image_c) * BLOCK + inner
    row_id, col_id = row_id[:, None], col_id[None, :]

    s, t, text_slab, image_slab, row_part, col_part = logits_and_statistics(
        where, [p for p, _ in text_pieces], [p for p, _ in image_pieces]
    )
    col_all = exchanged(col_part, TEXT_GROUP)
    row_all = exchanged(row_part, IMAGE_GROUP)
    gradient, turned, factors, part = gradient_of_logits(s, t, row_all, col_all, row_id, col_id)
    text_scale, image_scale = factors[0:1], factors[1:2]
    image_factor, text_factor = factors[2:3], factors[3:4]

    tie = lax.optimization_barrier
    steps = [lambda p, k=k: flipped(p, k) for k in (4, 2, 1)] + [other_core]
    half = SIDE // 2
    theirs = lax.dynamic_slice_in_dim(gradient, (1 - c) * half, half)
    mine = lax.dynamic_slice_in_dim(gradient, c * half, half)
    image_theirs = jnp.dot(theirs, text_slab, preferred_element_type=jnp.float32)
    image_theirs, part = tie(((image_theirs * text_scale).astype(jnp.float16), part))
    arrived = moved(image_theirs, other_core)
    value = jnp.sum(exchanged(part, TEXT_GROUP), axis=0)
    image_mine = (
        jnp.dot(mine, text_slab, preferred_element_type=jnp.float32) * text_scale
    ) + arrived.astype(jnp.float32)
    blocks = image_mine.astype(jnp.float16).reshape(8, BLOCK, WIDTH)

    def block(step):
        return lax.dynamic_index_in_dim(blocks, (z + sign * step) % 8, 0, keepdims=False).astype(
            jnp.float32
        )

    def narrow(v):
        return v.astype(jnp.float16)

    start, turned = tie((narrow(block(4)), turned))
    down = moved(start, along_z(-1)).astype(jnp.float32)
    text_part = (
        jnp.dot(turned, image_slab, preferred_element_type=jnp.float32) * image_scale
    ).astype(jnp.float16)
    down, text_part = tie((down, text_part))
    text_blocks = lax.all_to_all(text_part.reshape(16, BLOCK, WIDTH), TEXT_GROUP, 0, 0, tiled=True)
    first, second = tie((narrow(block(-3) + down), narrow(block(3))))
    down = moved(first, along_z(-1)).astype(jnp.float32)
    up = moved(second, along_z(1)).astype(jnp.float32)
    value = value + moved(value, steps[0])
    first, second = tie((narrow(block(-2) + down), narrow(block(2) + up)))
    down = moved(first, along_z(-1)).astype(jnp.float32)
    up = moved(second, along_z(1)).astype(jnp.float32)
    first, second, value = tie((narrow(block(-1) + down), narrow(block(1) + up), value))
    down = moved(first, along_z(-1)).astype(jnp.float32)
    up = moved(second, along_z(1)).astype(jnp.float32)
    for to in steps[1:]:
        value = value + moved(value, to)
    loss = value[0, 0] / (256 * BLOCK)
    image_grad = (block(0) + down + up) * image_factor
    text_grad = jnp.sum(text_blocks.astype(jnp.float32) * text_factor, axis=0)
    return (loss, image_grad, text_grad)


def flipped(p, bit):
    y, zl, x, zh, c = p
    z = (zh * 2 + zl) ^ bit
    return (y, z % 2, x, z // 2, c)


def solution(mesh):
    finer = Mesh(mesh.devices.reshape(SIZES), NAMES)
    placed = (P(ROW_COL, None), P(COL_ROW, None), P(ROW_COL, None), P(COL_ROW, None))
    return jax.shard_map(
        body,
        mesh=finer,
        in_specs=placed,
        out_specs=(P(), P(ROW_COL, None), P(COL_ROW, None)),
        check_vma=False,
    )
```

```python
import functools
import itertools
import math

import jax
import jax.numpy as jnp
from jax import lax
from jax.experimental import pallas as pl
from jax.experimental.pallas import tpu as pltpu
from jax.sharding import Mesh
from jax.sharding import PartitionSpec as P

NAMES = ("y", "zl", "x", "zh", "c")
SIZES = (4, 2, 4, 4, 2)
ROW_COL = ("y", "zl", "x", "zh", "c")
COL_ROW = ("x", "zh", "c", "y", "zl")
TEXT_GROUP = ("y", "x")
IMAGE_GROUP = ("zl", "zh", "c")

LOG2E = math.log2(math.e)
LN2 = math.log(2.0)
SCALE = 100.0
BLOCK = 64
WIDTH = 1024
SIDE = 1024
STRIP = 128
CHUNK = 256
GROUP = 16
LOGITS_VMEM = 58 * 1024 * 1024
GRADIENT_VMEM = 20 * 1024 * 1024
ROWS = 256


def places():
    return list(itertools.product(*(range(n) for n in SIZES)))


def index_of(place):
    at = 0
    for value, size in zip(place, SIZES):
        at = at * size + value % size
    return at


def shifted(place, axis, by):
    y, zl, x, zh, c = place
    if axis == "z":
        z = (zh * 2 + zl + by) % 8
        return (y, z % 2, x, z // 2, c)
    if axis == "x":
        return (y, zl, (x + by) % 4, zh, c)
    if axis == "y":
        return ((y + by) % 4, zl, x, zh, c)
    return (y, zl, x, zh, (c + by) % 2)


def moved(value, to):
    pairs = [(index_of(p), index_of(to(p))) for p in places()]
    return lax.ppermute(value, NAMES, pairs)


def along_u(by):
    return lambda p: shifted(p, "x" if p[4] == 0 else "y", by)


def along_v(by):
    return lambda p: shifted(p, "y" if p[4] == 0 else "x", by)


def along_z(by):
    return lambda p: shifted(p, "z", by if p[4] == 0 else -by)


def other_core(p):
    return shifted(p, "c", 1)


def joined_halves(*halves):
    def kernel(*refs):
        for k in range(4):
            refs[4 + k // 2][:, k % 2 * WIDTH : (k % 2 + 1) * WIDTH] = refs[k][...]

    vmem = pl.BlockSpec(memory_space=pltpu.VMEM)
    pair = jax.ShapeDtypeStruct((BLOCK, 2 * WIDTH), jnp.bfloat16)
    return pl.pallas_call(
        kernel,
        out_shape=(pair, pair),
        in_specs=[vmem] * 4,
        out_specs=(vmem,) * 2,
        cost_estimate=pl.CostEstimate(flops=0, bytes_accessed=1 << 20, transcendentals=0),
    )(*halves)


def gathered(text, image):
    tie = lax.optimization_barrier
    back, ahead = moved(text, along_u(1)), moved(text, along_u(-1))
    far = moved(text, along_u(2))
    mine = [image, moved(image, along_z(1))]
    theirs = [moved(image, other_core)]
    back, ahead, far, mine[1], theirs[0] = tie((back, ahead, far, mine[1], theirs[0]))

    line = jnp.concatenate([text, back, ahead, far], axis=0)
    line, mine[1], theirs[0] = tie((line, mine[1], theirs[0]))
    line_back, line_ahead = moved(line, along_v(1)), moved(line, along_v(-1))
    mine.append(moved(mine[1], along_z(1)))
    theirs.append(moved(theirs[0], along_z(1)))
    mine[2], theirs[1] = tie((mine[2], theirs[1]))
    mine.append(moved(mine[2], along_z(1)))
    theirs.append(moved(theirs[1], along_z(1)))
    line_back, line_ahead, mine[3], theirs[2] = tie((line_back, line_ahead, mine[3], theirs[2]))

    first_far = moved(line_back[:128], along_v(1))
    second_far = moved(line_ahead[128:], along_v(-1))
    mine.append(moved(mine[3], along_z(1)))
    theirs.append(moved(theirs[2], along_z(1)))
    early = jnp.concatenate([mine[1], mine[2], mine[3], theirs[1], theirs[2]], axis=0)
    early_other = moved(early, other_core)
    mine[4], theirs[3] = tie((mine[4], theirs[3]))
    late = jnp.concatenate([mine[4], theirs[3]], axis=0)
    late_other = moved(late, other_core)
    us = (0, -1, 1, 2)
    return [
        (line, [(du, 0) for du in us]),
        (line_back, [(du, -1) for du in us]),
        (line_ahead, [(du, 1) for du in us]),
        (first_far, ((0, 2), (-1, 2))),
        (second_far, ((1, 2), (2, 2))),
    ], [
        (image, ((0, 0),)),
        (theirs[0], ((1, 0),)),
        (early, ((0, -1), (0, -2), (0, -3), (1, -1), (1, -2))),
        (early_other, ((1, 1), (1, 2), (1, 3), (0, 1), (0, 2))),
        (late, ((0, 4), (1, -3))),
        (late_other, ((1, 4), (0, 3))),
    ]


def logits_kernel(counts, *refs):
    n_text, n_image = counts
    place_ref = refs[0]
    text_refs = refs[1 : 1 + n_text]
    image_refs = refs[1 + n_text : 1 + n_text + n_image]
    (s_hbm, t_hbm, text_hbm, image_hbm, row_ref, col_ref) = refs[
        1 + n_text + n_image : 7 + n_text + n_image
    ]
    (
        s_ref,
        t_ref,
        text_out,
        image_out,
        text_frozen,
        image_frozen,
        s_high,
        s_sum,
        t_high,
        t_sum,
        sems,
        out_sems,
    ) = refs[7 + n_text + n_image :]
    copies = []
    k = 0
    for group, out, frozen in (
        (text_refs, text_out, text_frozen),
        (image_refs, image_out, image_frozen),
    ):
        for ref in group:
            for b in range(ref.shape[0] // BLOCK):
                at = pl.multiple_of(place_ref[k] * BLOCK, BLOCK)
                for half, target in ((0, out), (1, frozen)):
                    copies.append(
                        pltpu.make_async_copy(
                            ref.at[pl.ds(b * BLOCK, BLOCK), pl.ds(half * WIDTH, WIDTH)],
                            target.at[pl.ds(at, BLOCK), :],
                            sems.at[2 * k + half],
                        )
                    )
                k += 1
    for half in (0, 1):
        for copy in copies[half::2]:
            copy.start()
    outward = [
        pltpu.make_async_copy(text_out, text_hbm, out_sems.at[2]),
        pltpu.make_async_copy(image_out, image_hbm, out_sems.at[3]),
        pltpu.make_async_copy(s_ref, s_hbm, out_sems.at[0]),
        pltpu.make_async_copy(t_ref, t_hbm, out_sems.at[1]),
    ]

    for which, left, right, out in (
        (0, image_out, text_out, s_ref),
        (1, image_frozen, text_frozen, t_ref),
    ):
        for copy in copies[which::2]:
            copy.wait()

        @pl.loop(0, SIDE // CHUNK)
        def _(j):
            cols = pl.ds(pl.multiple_of(j * CHUNK, CHUNK), CHUNK)
            tile = (SCALE * LOG2E) * lax.dot_general(
                left[...],
                right[cols, :],
                (((1,), (1,)), ((), ())),
                preferred_element_type=jnp.float32,
            )
            out[:, cols] = tile
            tile = tile.reshape(SIDE // 8, 8, CHUNK)
            high = jnp.max(tile, axis=0)
            total = jnp.sum(jnp.exp2(tile - high), axis=0)
            top = jnp.max(high, axis=0, keepdims=True)
            total = jnp.sum(total * jnp.exp2(high - top), axis=0, keepdims=True)
            lse = top + jnp.log2(total)
            for n in range(GROUP):
                col_ref[n, which : which + 1, cols] = lse

        for copy in outward[:3] if which == 0 else outward[3:]:
            copy.start()

    @pl.loop(0, SIDE // 64)
    def _(i):
        for g in range(8):
            rows = pl.ds(pl.multiple_of(i * 64 + g * 8, 8), 8)
            for ref, high_ref, sum_ref in ((s_ref, s_high, s_sum), (t_ref, t_high, t_sum)):
                tiles = [ref[rows, pl.ds(k * 128, 128)] for k in range(SIDE // 128)]
                high = functools.reduce(jnp.maximum, tiles)
                high_ref[rows, :] = high
                sum_ref[rows, :] = functools.reduce(jnp.add, [jnp.exp2(v - high) for v in tiles])

    @pl.loop(0, SIDE // 128)
    def _(i):
        rows = pl.ds(pl.multiple_of(i * 128, 128), 128)
        for which, high_ref, sum_ref in ((0, s_high, s_sum), (1, t_high, t_sum)):
            high = jnp.transpose(high_ref[rows, :])
            total = jnp.transpose(sum_ref[rows, :])
            top = jnp.max(high, axis=0, keepdims=True)
            total = jnp.sum(total * jnp.exp2(high - top), axis=0, keepdims=True)
            lse = top + jnp.log2(total)
            for n in range(GROUP):
                row_ref[n, which : which + 1, rows] = lse

    for slab, ref in ((text_out, row_ref), (image_out, col_ref)):
        largest = jnp.max(jnp.abs(slab[...]), axis=0, keepdims=True).astype(jnp.float32)
        largest = jnp.full((2, 128), jnp.max(largest), jnp.float32)
        for n in range(GROUP):
            ref[n, :, SIDE : SIDE + 128] = largest
    for copy in outward:
        copy.wait()


def logits_and_statistics(places_in, text, images):
    f32 = jnp.float32
    anywhere = pl.BlockSpec(memory_space=pl.ANY)
    vmem = pl.BlockSpec(memory_space=pltpu.VMEM)
    smem = pl.BlockSpec(memory_space=pltpu.SMEM)
    hbm = pl.BlockSpec(memory_space=pltpu.HBM)

    def kernel(*refs):
        logits_kernel((len(text), len(images)), *refs)

    square = pltpu.HBM((SIDE, SIDE), f32)
    half = jax.ShapeDtypeStruct((SIDE, WIDTH), jnp.bfloat16)
    small = jax.ShapeDtypeStruct((GROUP, 2, SIDE + 128), f32)
    return pl.pallas_call(
        kernel,
        out_shape=(square, square, half, half, small, small),
        in_specs=[smem] + [anywhere] * (len(text) + len(images)),
        out_specs=(hbm,) * 4 + (vmem,) * 2,
        scratch_shapes=[
            pltpu.VMEM((SIDE, SIDE), f32),
            pltpu.VMEM((SIDE, SIDE), f32),
            pltpu.VMEM((SIDE, WIDTH), jnp.bfloat16),
            pltpu.VMEM((SIDE, WIDTH), jnp.bfloat16),
            pltpu.VMEM((SIDE, WIDTH), jnp.bfloat16),
            pltpu.VMEM((SIDE, WIDTH), jnp.bfloat16),
            pltpu.VMEM((SIDE, 128), f32),
            pltpu.VMEM((SIDE, 128), f32),
            pltpu.VMEM((SIDE, 128), f32),
            pltpu.VMEM((SIDE, 128), f32),
            pltpu.SemaphoreType.DMA((64,)),
            pltpu.SemaphoreType.DMA((4,)),
        ],
        compiler_params=pltpu.CompilerParams(vmem_limit_bytes=LOGITS_VMEM),
        cost_estimate=pl.CostEstimate(
            flops=4 * SIDE * SIDE * WIDTH, bytes_accessed=20 << 20, transcendentals=4 * SIDE * SIDE
        ),
    )(places_in, *text, *images)


def gradient_kernel(
    s_ref,
    t_ref,
    row_ref,
    col_ref,
    row_id_ref,
    col_id_ref,
    out_ref,
    turned_ref,
    factor_ref,
    part_ref,
    lse_ref,
    total_ref,
):
    step = pl.program_id(0)
    size = 16

    def joined(ref, which):
        values = ref[:, which, :SIDE]
        top = jnp.max(values, axis=0, keepdims=True)
        return top + jnp.log2(jnp.sum(jnp.exp2(values - top), axis=0, keepdims=True))

    @pl.when(step == 0)
    def _():
        s_row_all, t_row_all = joined(row_ref, 0), joined(row_ref, 1)
        s_col_all, t_col_all = joined(col_ref, 0), joined(col_ref, 1)
        shared = (s_row_all - 0.5 * t_row_all) + (s_col_all - 0.5 * t_col_all)
        lse_ref[0:1, :] = s_row_all
        lse_ref[1:2, :] = t_row_all + 1.0
        lse_ref[2:3, :] = s_col_all
        lse_ref[3:4, :] = t_col_all + 1.0
        lse_ref[4:5, :] = shared
        for k, ref in ((0, row_ref), (1, col_ref)):
            scale = 2.0 / jnp.maximum(jnp.max(ref[:, 0, SIDE : SIDE + 128]), 1e-30)
            scale = jnp.full((1, SIDE), scale, jnp.float32)
            factor_ref[k : k + 1, :] = scale
            factor_ref[k + 2 : k + 3, :] = SCALE / scale
        factor_ref[4:8, :] = jnp.zeros((4, SIDE), jnp.float32)
        total_ref[...] = jnp.zeros((size, 128), jnp.float32)

    def strip(i, total):
        base = pl.multiple_of(i * STRIP, STRIP)
        at = pl.multiple_of(step * ROWS + base, STRIP)
        turned = jnp.transpose(lse_ref[:, pl.ds(at, STRIP)])
        for g in range(STRIP // size):
            rows = pl.ds(pl.multiple_of(base + g * size, size), size)
            s_row = jnp.broadcast_to(turned[g * size : (g + 1) * size, 0:1], (size, 128))
            t_row = jnp.broadcast_to(turned[g * size : (g + 1) * size, 1:2], (size, 128))
            row_id = jnp.broadcast_to(row_id_ref[rows, :], (size, 128))
            for k in range(SIDE // 128):
                lanes = pl.ds(k * 128, 128)
                s = s_ref[rows, lanes]
                t = t_ref[rows, lanes]
                weights = jnp.exp2(t - t_row) + jnp.exp2(t - lse_ref[3:4, lanes])
                value = (jnp.exp2(s - s_row) + jnp.exp2(s - lse_ref[2:3, lanes])) - weights
                same = row_id == col_id_ref[:, lanes]
                out_ref[rows, lanes] = jnp.where(same, value - 1.0, value).astype(jnp.bfloat16)
                total = total + (weights * (t - s) - jnp.where(same, s, 0.0))
        for k in range(SIDE // 128):
            tile = out_ref[pl.ds(base, STRIP), pl.ds(k * 128, 128)].astype(jnp.float32)
            turned_ref[pl.ds(k * 128, 128), pl.ds(base, STRIP)] = jnp.transpose(tile).astype(
                jnp.bfloat16
            )
        return total

    total_ref[...] = lax.fori_loop(0, ROWS // STRIP, strip, total_ref[...])

    @pl.when(step == pl.num_programs(0) - 1)
    def _():
        part = jnp.sum(total_ref[...]) + jnp.sum(lse_ref[4:5, :]) * (1.0 / GROUP)
        part_ref[...] = jnp.full(part_ref.shape, LN2 * part, jnp.float32)


def gradient_of_logits(s, t, row, col, row_id, col_id):
    f32 = jnp.float32
    by_rows = pl.BlockSpec((ROWS, SIDE), lambda i: (i, 0))

    def whole(shape):
        return pl.BlockSpec(shape, lambda i: (0,) * len(shape))

    return pl.pallas_call(
        gradient_kernel,
        grid=(SIDE // ROWS,),
        out_shape=(
            jax.ShapeDtypeStruct((SIDE, SIDE), jnp.bfloat16),
            jax.ShapeDtypeStruct((SIDE, SIDE), jnp.bfloat16),
            jax.ShapeDtypeStruct((8, SIDE), f32),
            jax.ShapeDtypeStruct((GROUP, 8, 128), f32),
        ),
        in_specs=[
            by_rows,
            by_rows,
            whole(row.shape),
            whole(col.shape),
            pl.BlockSpec((ROWS, 1), lambda i: (i, 0)),
            whole(col_id.shape),
        ],
        out_specs=(by_rows, pl.BlockSpec((SIDE, ROWS), lambda i: (0, i)), whole((8, SIDE)), whole((GROUP, 8, 128))),
        scratch_shapes=[pltpu.VMEM((8, SIDE), f32), pltpu.VMEM((16, 128), f32)],
        compiler_params=pltpu.CompilerParams(vmem_limit_bytes=GRADIENT_VMEM),
        cost_estimate=pl.CostEstimate(
            flops=16 * SIDE * SIDE, bytes_accessed=10 << 20, transcendentals=4 * SIDE * SIDE
        ),
    )(
        *(pltpu.with_memory_space_constraint(v, pltpu.HBM) for v in (s, t)),
        row,
        col,
        row_id,
        col_id,
    )


def exchanged(copies, axis):
    return lax.all_to_all(copies, axis, split_axis=0, concat_axis=0, tiled=True)


def body(image_student, text_student, image_teacher, text_teacher):
    y, zl, x, zh, c = (lax.axis_index(n) for n in NAMES)
    z = zh * 2 + zl
    text_pieces, image_pieces = gathered(
        *joined_halves(text_student, text_teacher, image_student, image_teacher)
    )

    sign = 1 - 2 * c
    at = []
    for _, offsets in text_pieces:
        for du, dv in offsets:
            dx = jnp.where(c == 0, du, dv)
            dy = jnp.where(c == 0, dv, du)
            at.append(((y + dy) % 4) * 4 + (x + dx) % 4)
    for _, offsets in image_pieces:
        for swapped, step in offsets:
            at.append((c ^ swapped) * 8 + (z + sign * step) % 8)
    where = jnp.stack(at).astype(jnp.int32)

    numbers = jnp.arange(SIDE, dtype=jnp.int32)
    slot, inner = numbers // BLOCK, numbers % BLOCK
    text_y, text_x = slot // 4, slot % 4
    col_id = (((text_x * 8 + zh * 2 + c) * 8) + text_y * 2 + zl) * BLOCK + inner
    image_c, image_z = slot // 8, slot % 8
    row_id = ((y * 2 + image_z % 2) * 32 + x * 8 + (image_z // 2) * 2 + image_c) * BLOCK + inner
    row_id, col_id = row_id[:, None], col_id[None, :]

    s, t, text_slab, image_slab, row_part, col_part = logits_and_statistics(
        where, [p for p, _ in text_pieces], [p for p, _ in image_pieces]
    )
    col_all = exchanged(col_part, TEXT_GROUP)
    row_all = exchanged(row_part, IMAGE_GROUP)
    gradient, turned, factors, part = gradient_of_logits(s, t, row_all, col_all, row_id, col_id)
    text_scale, image_scale = factors[0:1], factors[1:2]
    image_factor, text_factor = factors[2:3], factors[3:4]

    tie = lax.optimization_barrier
    steps = [lambda p, k=k: flipped(p, k) for k in (4, 2, 1)] + [other_core]
    half = SIDE // 2
    theirs = lax.dynamic_slice_in_dim(gradient, (1 - c) * half, half)
    mine = lax.dynamic_slice_in_dim(gradient, c * half, half)
    image_theirs = jnp.dot(theirs, text_slab, preferred_element_type=jnp.float32)
    image_theirs, part = tie(((image_theirs * text_scale).astype(jnp.float16), part))
    arrived = moved(image_theirs, other_core)
    value = jnp.sum(exchanged(part, TEXT_GROUP), axis=0)
    image_mine = (
        jnp.dot(mine, text_slab, preferred_element_type=jnp.float32) * text_scale
    ) + arrived.astype(jnp.float32)
    blocks = image_mine.astype(jnp.float16).reshape(8, BLOCK, WIDTH)

    def block(step):
        return lax.dynamic_index_in_dim(blocks, (z + sign * step) % 8, 0, keepdims=False).astype(
            jnp.float32
        )

    def narrow(v):
        return v.astype(jnp.float16)

    start, turned = tie((narrow(block(4)), turned))
    down = moved(start, along_z(-1)).astype(jnp.float32)
    text_part = (
        jnp.dot(turned, image_slab, preferred_element_type=jnp.float32) * image_scale
    ).astype(jnp.float16)
    down, text_part = tie((down, text_part))
    text_blocks = lax.all_to_all(text_part.reshape(16, BLOCK, WIDTH), TEXT_GROUP, 0, 0, tiled=True)
    first, second = tie((narrow(block(-3) + down), narrow(block(3))))
    down = moved(first, along_z(-1)).astype(jnp.float32)
    up = moved(second, along_z(1)).astype(jnp.float32)
    value = value + moved(value, steps[0])
    first, second, value = tie((narrow(block(-2) + down), narrow(block(2) + up), value))
    down = moved(first, along_z(-1)).astype(jnp.float32)
    up = moved(second, along_z(1)).astype(jnp.float32)
    value = value + moved(value, steps[1])
    first, second, value = tie((narrow(block(-1) + down), narrow(block(1) + up), value))
    down = moved(first, along_z(-1)).astype(jnp.float32)
    up = moved(second, along_z(1)).astype(jnp.float32)
    for to in steps[2:]:
        value = value + moved(value, to)
    loss = value[0, 0] / (256 * BLOCK)
    image_grad = (block(0) + down + up) * image_factor
    text_grad = jnp.sum(text_blocks.astype(jnp.float32) * text_factor, axis=0)
    return (loss, image_grad, text_grad)


def flipped(p, bit):
    y, zl, x, zh, c = p
    z = (zh * 2 + zl) ^ bit
    return (y, z % 2, x, z // 2, c)


def solution(mesh):
    finer = Mesh(mesh.devices.reshape(SIZES), NAMES)
    placed = (P(ROW_COL, None), P(COL_ROW, None), P(ROW_COL, None), P(COL_ROW, None))
    return jax.shard_map(
        body,
        mesh=finer,
        in_specs=placed,
        out_specs=(P(), P(ROW_COL, None), P(COL_ROW, None)),
        check_vma=False,
    )
```
